32 devices in a mesh: sx: 4 (over z), sy: 4 (over x, core), gz: 2 (over y).
Axes of the slice: x: 2, y: 2, z: 4, core: 2. Of those that a mesh axis runs over, the one named last changes fastest.
Arguments:
- observed: float32 [512, 64, 512], P('gz', 'sx', 'sy'), may hold values from 0.25 to 2
- zone_of_slice: int32 [512], P('gz'), may hold values from 0 to 7
- lateral_x: float32 [8, 7], replicated, may hold values from 0.05 to 1
- lateral_y: float32 [8, 7], replicated, may hold values from 0.05 to 1
- depth_psf: float32 [17], replicated, may hold values from 0.05 to 1
- stitch_width: int32 [4, 4, 2], replicated, may hold values from 1 to 8
Outputs:
- estimate: float32 [512, 64, 512], P('gz', 'sx', 'sy')
The draws below stay inside these ranges and needn't reach their ends.
All inputs are finite; a program needn't handle non-finite values.
Results may differ from the reference program's by a relative error of at most 0.0001.
Values sent between devices are 32-bit elements; how exact they have to be, the bound alone decides.
No kernel may reach another device: no remote copies, remote signals or barrier semaphores. Data moves between devices by JAX's collectives and lax.ppermute only.
A program may use at most 64 MiB of HBM per device.

```python
import math
import jax
import jax.numpy as jnp
from jax import lax

NZ = 512
CX = 16
CY = 128
ZONES = 8
ITERS = 2
TAPS = 7
DEPTH_TAPS = 17
NX = 64
NY = 512
STACKS_X = 4
STACKS_Y = 4


def set_ends(values, key, least, top_value):
    spot = [jax.random.randint(jax.random.fold_in(key, axis), (), 0, length) for axis, length in enumerate(values.shape)]
    longest = values.shape.index(max(values.shape))
    beside = spot[:longest] + [(spot[longest] + 1) % values.shape[longest]] + spot[longest + 1:]
    return values.at[tuple(spot)].set(least).at[tuple(beside)].set(top_value)


def block_scale(rng, dims, split, least, high):
    factor_of, own = 1.0, jax.random.fold_in(rng, 6)
    for axis_at, shards_of in split:
        draws = jnp.exp(jax.random.uniform(jax.random.fold_in(own, axis_at), (shards_of,), jnp.float32, least / len(split), high / len(split)))
        factor_of = factor_of * jnp.repeat(draws, dims[axis_at] // shards_of).reshape([-1 if axis == axis_at else 1 for axis in range(len(dims))])
    return factor_of


def setup_inputs(seed: int = 0) -> dict:
    key_list = jax.random.split(jax.random.key(seed), 7)
    return {
        "observed": jnp.clip(0.25 + 1.75 * jax.random.uniform(key_list[0], (NZ, NX, NY), jnp.float32) ** block_scale(key_list[0], (NZ, NX, NY), ((0, 2), (1, 4), (2, 4)), -0.2, 0.2), 0.25, 2.0),
        "zone_of_slice": set_ends(jax.random.randint(key_list[1], (NZ,), 0, ZONES), jax.random.fold_in(key_list[1], 1), 0, ZONES - 1).astype(jnp.int32),
        "lateral_x": jnp.clip(jnp.exp(jax.random.uniform(key_list[2], (ZONES, TAPS), jnp.float32, math.log(0.05), math.log(1.0))), 0.05, 1.0),
        "lateral_y": jnp.clip(jnp.exp(jax.random.uniform(key_list[3], (ZONES, TAPS), jnp.float32, math.log(0.05), math.log(1.0))), 0.05, 1.0),
        "depth_psf": jnp.clip(jnp.exp(jax.random.uniform(key_list[4], (DEPTH_TAPS,), jnp.float32, math.log(0.05), math.log(1.0))), 0.05, 1.0),
        "stitch_width": set_ends(jax.random.randint(key_list[5], (STACKS_X, STACKS_Y, 2), 1, CX // 2 + 1), jax.random.fold_in(key_list[5], 1), 1, (CX // 2 + 1) - 1).astype(jnp.int32),
    }


def slice_taps(zone_of_slice, kernels):
    ids = jnp.arange(kernels.shape[0], dtype=jnp.int32)
    onehot = (zone_of_slice[:, None] == ids[None, :]).astype(jnp.float32)
    return jnp.sum(onehot[:, :, None] * kernels[None, :, :], axis=1)


def lateral_core(padded, taps_x, taps_y, width_x, width_y):
    count = taps_x.shape[1]
    along = taps_x[:, 0, None, None] * padded[:, 0:width_x, :]
    for a in range(1, count):
        along = along + taps_x[:, a, None, None] * padded[:, a:a + width_x, :]
    result = taps_y[:, 0, None, None] * along[:, :, 0:width_y]
    for b in range(1, count):
        result = result + taps_y[:, b, None, None] * along[:, :, b:b + width_y]
    return result


def lateral_full(volume, taps_x, taps_y, flip):
    if flip:
        taps_x = taps_x[:, ::-1]
        taps_y = taps_y[:, ::-1]
    reach = (taps_x.shape[1] - 1) // 2
    padded = jnp.pad(volume, ((0, 0), (reach, reach), (reach, reach)))
    return lateral_core(padded, taps_x, taps_y, volume.shape[1], volume.shape[2])


def depth_tables(depth_psf, length):
    kernel = depth_psf / jnp.sum(depth_psf)
    reach = (depth_psf.shape[0] - 1) // 2
    freq = jnp.arange(length, dtype=jnp.int32)
    offs = jnp.arange(depth_psf.shape[0], dtype=jnp.int32) - reach
    phase = jnp.mod(freq[:, None] * offs[None, :], length).astype(jnp.float32) * (2.0 * math.pi / length)
    gain_c = jnp.sum(kernel[None, :] * jnp.cos(phase), axis=1)
    gain_s = jnp.sum(kernel[None, :] * jnp.sin(phase), axis=1)
    pos = jnp.arange(length, dtype=jnp.int32)
    angle = jnp.mod(freq[:, None] * pos[None, :], length).astype(jnp.float32) * (2.0 * math.pi / length)
    table = jnp.concatenate([jnp.cos(angle), jnp.sin(angle)], axis=0)
    return table, gain_c, gain_s


def depth_columns(columns, table, gain_c, gain_s, sign):
    length = table.shape[1]
    coef = jnp.dot(table, columns, precision=lax.Precision.HIGHEST, preferred_element_type=jnp.float32)
    cpart = coef[:length]
    spart = coef[length:]
    upper = cpart * gain_c[:, None] - sign * spart * gain_s[:, None]
    lower = sign * cpart * gain_s[:, None] + spart * gain_c[:, None]
    stacked = jnp.concatenate([upper, lower], axis=0)
    back = lax.dot_general(table, stacked, (((0,), (0,)), ((), ())), precision=lax.Precision.HIGHEST, preferred_element_type=jnp.float32)
    return back / length


def depth_full(volume, table, gain_c, gain_s, sign):
    shape = volume.shape
    flat = volume.reshape(shape[0], -1)
    return depth_columns(flat, table, gain_c, gain_s, sign).reshape(shape)


def reference(observed, zone_of_slice, lateral_x, lateral_y, depth_psf, stitch_width):
    taps_x = slice_taps(zone_of_slice, lateral_x)
    taps_y = slice_taps(zone_of_slice, lateral_y)
    table, gain_c, gain_s = depth_tables(depth_psf, NZ)
    xpos = jnp.arange(NX, dtype=jnp.int32)
    ypos = jnp.arange(NY, dtype=jnp.int32)
    stack_x = xpos // CX
    stack_y = ypos // CY
    band_x = stitch_width[stack_x[:, None], stack_y[None, :], 0]
    band_y = stitch_width[stack_x[:, None], stack_y[None, :], 1]
    weight = jnp.where((xpos % CX)[:, None] < band_x, 0.5, 1.0) * jnp.where((ypos % CY)[None, :] < band_y, 0.5, 1.0)
    weight = weight.astype(jnp.float32)
    weight_vol = jnp.broadcast_to(weight[None, :, :], observed.shape)
    data = weight_vol * observed
    norm = lateral_full(weight_vol, taps_x, taps_y, True)
    estimate = observed
    for step in range(ITERS):
        blurred = depth_full(lateral_full(estimate, taps_x, taps_y, False), table, gain_c, gain_s, 1.0)
        ratio = data / blurred
        update = lateral_full(depth_full(ratio, table, gain_c, gain_s, -1.0), taps_x, taps_y, True)
        estimate = estimate * update / norm
    return estimate
```

```python
import functools

import jax
import jax.numpy as jnp
from jax import lax
from jax.experimental import pallas as pl
from jax.experimental.pallas import tpu as pltpu
from jax.sharding import PartitionSpec as P

ITERS = 2
LANES = 128
TINY = 1e-30
VMEM = pl.BlockSpec(memory_space=pltpu.VMEM)


def ceil_to(value, unit):
    return -(-value // unit) * unit


def line(axis):
    count = lax.axis_size(axis)
    up = [(i, i + 1) for i in range(count - 1)]
    return up, [(j, i) for i, j in up]


def x_conv(src, dst, taps, reverse, t, width, blocks):
    count = taps.shape[1]
    k = [taps[t, count - 1 - a if reverse else a] for a in range(count)]

    def step(j, carry):
        rows = pl.ds(pl.multiple_of(8 * j, 8), 8)
        v = [src[t, x, rows, :] for x in range(width + count - 1)]
        for x in range(width):
            acc = k[0] * v[x]
            for a in range(1, count):
                acc = acc + k[a] * v[x + a]
            dst[t, x, rows, :] = acc
        return carry

    lax.fori_loop(0, blocks, step, 0)


def y_conv(src, taps, reverse, t, width, blocks, emit):
    count = taps.shape[1]
    k = [taps[t, count - 1 - b if reverse else b] for b in range(count)]

    def step(x, carry):
        for j in range(blocks):
            acc = k[0] * src[t, x, 8 * j : 8 * j + 8, :]
            for b in range(1, count):
                acc = acc + k[b] * src[t, x, 8 * j + b : 8 * j + b + 8, :]
            emit(t, x, j, acc)
        return carry

    lax.fori_loop(0, width, step, 0)


def windows_of(tiles):
    return [(0, tiles)] if tiles <= 2 else [(w, 2) for w in range(tiles - 1)]


def depth_rows(parts, hi_ref, lo_ref):
    tiles = len(parts)
    split = []
    for part in parts:
        hi = part.astype(jnp.bfloat16)
        split.append((hi, (part - hi.astype(jnp.float32)).astype(jnp.bfloat16)))
    out = [None] * tiles
    for index, (first, span) in enumerate(windows_of(tiles)):
        his = jnp.concatenate([split[first + s][0] for s in range(span)], axis=1)
        los = jnp.concatenate([split[first + s][1] for s in range(span)], axis=1)
        dot = functools.partial(jnp.dot, preferred_element_type=jnp.float32)
        res = dot(his, hi_ref[index]) + (dot(los, hi_ref[index]) + dot(his, lo_ref[index]))
        for s in range(span):
            piece = res[:, s * LANES : (s + 1) * LANES]
            out[first + s] = piece if out[first + s] is None else out[first + s] + piece
    return out


def norm_kernel(w_ref, tx_ref, ty_ref, out_ref, mid_ref):
    tiles = tx_ref.shape[0]
    width = out_ref.shape[1]
    blocks = out_ref.shape[2] // 8
    count = tx_ref.shape[1]
    for t in range(tiles):
        k = [tx_ref[t, count - 1 - a] for a in range(count)]

        def step(j, carry, k=k):
            rows = pl.ds(pl.multiple_of(8 * j, 8), 8)
            v = [w_ref[x, rows, :] for x in range(width + count - 1)]
            for x in range(width):
                acc = k[0] * v[x]
                for a in range(1, count):
                    acc = acc + k[a] * v[x + a]
                mid_ref[0, x, rows, :] = acc
            return carry

        lax.fori_loop(0, mid_ref.shape[2] // 8, step, 0)
        ky = [ty_ref[t, count - 1 - b] for b in range(count)]

        def ystep(x, carry, ky=ky, t=t):
            for j in range(blocks):
                acc = ky[0] * mid_ref[0, x, 8 * j : 8 * j + 8, :]
                for b in range(1, count):
                    acc = acc + ky[b] * mid_ref[0, x, 8 * j + b : 8 * j + b + 8, :]
                out_ref[t, x, 8 * j : 8 * j + 8, :] = 1.0 / jnp.maximum(acc, TINY)
            return carry

        lax.fori_loop(0, width, ystep, 0)


def iterate_kernel(dy, need, est_ref, obs_ref, w_ref, inv_ref, tx_ref, ty_ref, fh_ref, fl_ref, bh_ref, bl_ref, out_ref, mid_ref, blur_ref):
    tiles = est_ref.shape[0]
    reach = (tx_ref.shape[1] - 1) // 2
    wide = blur_ref.shape[1]
    rows = blur_ref.shape[2]
    width = out_ref.shape[1]
    blocks = out_ref.shape[2] // 8

    def put(t, x, j, acc):
        blur_ref[t, x, 8 * j : 8 * j + 8, :] = acc

    for t in range(tiles):
        x_conv(est_ref, mid_ref, tx_ref, False, t, wide, -(-need // 8))
        y_conv(mid_ref, ty_ref, False, t, wide, rows // 8, put)

    def depth(i, carry):
        spot = pl.ds(2 * i, 2)
        size = 2 * rows
        parts = [blur_ref[t, spot].reshape(size, LANES) for t in range(tiles)]
        blurred = depth_rows(parts, fh_ref, fl_ref)
        weight = w_ref[spot, dy : dy + rows, :].reshape(size, LANES)
        ratio = []
        for t in range(tiles):
            seen = obs_ref[t, pl.ds(2 * i + reach, 2), dy + reach : dy + reach + rows, :].reshape(size, LANES)
            ratio.append(weight * seen / jnp.maximum(blurred[t], TINY))
        spread = depth_rows(ratio, bh_ref, bl_ref)
        for t in range(tiles):
            blur_ref[t, spot] = spread[t].reshape(2, rows, LANES)
        return carry

    lax.fori_loop(0, wide // 2, depth, 0)

    def finish(t, x, j, acc):
        old = est_ref[t, x + 2 * reach, 8 * j + 2 * reach : 8 * j + 2 * reach + 8, :]
        out_ref[t, x, 8 * j : 8 * j + 8, :] = old * acc * inv_ref[t, x, 8 * j + dy : 8 * j + dy + 8, :]

    for t in range(tiles):
        x_conv(blur_ref, mid_ref, tx_ref, True, t, width, rows // 8)
        y_conv(mid_ref, ty_ref, True, t, width, blocks, finish)


def body(observed, zone_of_slice, lateral_x, lateral_y, depth_psf, stitch_width):
    nz, cx, cy = observed.shape
    taps = lateral_x.shape[1]
    reach = (taps - 1) // 2
    zreach = (depth_psf.shape[0] - 1) // 2
    hz = 2 * zreach * ITERS
    hy = 2 * reach * ITERS
    hx = 2 * reach
    slabs = lax.axis_size("gz")
    tiles = ceil_to(nz + 2 * hz, LANES) // LANES
    f32 = jnp.float32

    zones = zone_of_slice.astype(f32)

    def with_zones(part, ids):
        flat = jnp.pad(ids, (0, cx * cy - ids.shape[0]))
        return jnp.concatenate([part, flat.reshape(1, cx, cy)], axis=0)

    if slabs == 2:
        both = jnp.concatenate([observed[nz - hz :], observed[:hz]], axis=0)
        got = lax.ppermute(with_zones(both, jnp.concatenate([zones[nz - hz :], zones[:hz]])), "gz", [(0, 1), (1, 0)])
        before, after = got[:hz], got[hz : 2 * hz]
        got_ids = got[2 * hz].reshape(-1)
        ids_before, ids_after = got_ids[:hz], got_ids[hz : 2 * hz]
    else:
        up = [(i, (i + 1) % slabs) for i in range(slabs)]
        first = lax.ppermute(with_zones(observed[nz - hz :], zones[nz - hz :]), "gz", up)
        second = lax.ppermute(with_zones(observed[:hz], zones[:hz]), "gz", [(j, i) for i, j in up])
        before, after = first[:hz], second[:hz]
        ids_before, ids_after = first[hz].reshape(-1)[:hz], second[hz].reshape(-1)[:hz]
    pad = tiles * LANES - nz - 2 * hz
    volume = jnp.concatenate([before, observed, after, jnp.zeros((pad, cx, cy), f32)], axis=0)
    ids = jnp.concatenate([ids_before, zones, ids_after, jnp.full((pad,), -1.0, f32)])
    volume = volume.reshape(tiles, LANES, cx, cy).transpose(0, 2, 3, 1)

    match = (ids[None, :] == jnp.arange(lateral_x.shape[0], dtype=f32)[:, None]).astype(f32)

    def lanes_of(kernels):
        table = jnp.sum(match[:, None, :] * kernels[:, :, None], axis=0)
        table = table.reshape(taps, tiles, 1, LANES).transpose(1, 0, 2, 3)
        return jnp.broadcast_to(table, (tiles, taps, 8, LANES))

    tx, ty = lanes_of(lateral_x), lanes_of(lateral_y)

    kernel = depth_psf / jnp.sum(depth_psf)
    wins = windows_of(tiles)
    size = wins[0][1] * LANES
    off = jnp.arange(size)[None, :] - jnp.arange(size)[:, None]
    band = jnp.zeros((size, size), f32)
    flip = jnp.zeros((size, size), f32)
    for j in range(kernel.shape[0]):
        band = band + jnp.where(off == j - zreach, kernel[j], 0.0)
        flip = flip + jnp.where(off == zreach - j, kernel[j], 0.0)

    def halves(matrix):
        cols = jnp.arange(size)
        parts = []
        for index in range(len(wins)):
            low = 0 if index == 0 else LANES // 2
            high = size if index == len(wins) - 1 else LANES + LANES // 2
            parts.append(jnp.where((cols >= low) & (cols < high), matrix, 0.0))
        full = jnp.stack(parts)
        top = lax.reduce_precision(full, 8, 7)
        return top.astype(jnp.bfloat16), (full - top).astype(jnp.bfloat16)

    fh, fl = halves(band)
    bh, bl = halves(flip)

    sx, sy = lax.axis_index("sx"), lax.axis_index("sy")
    stacks_x, stacks_y = stitch_width.shape[:2]
    rows1 = ceil_to(cy + 2 * hy - 2 * reach, 8)
    gx = sx * cx - reach + jnp.arange(cx + 2 * reach)
    gy = sy * cy - (hy - reach) + jnp.arange(rows1)
    near = lax.dynamic_slice(jnp.pad(stitch_width, ((1, 1), (1, 1), (0, 0))), (sx, sy, jnp.int32(0)), (3, 3, 2))
    of_x = gx // cx - sx + 1
    of_y = gy // cy - sy + 1
    bands = jnp.zeros((2, gx.shape[0], rows1), jnp.int32)
    for a in range(3):
        for b in range(3):
            hit = (of_x[:, None] == a) & (of_y[None, :] == b)
            bands = jnp.where(hit[None], near[a, b][:, None, None], bands)
    inside = ((gx >= 0) & (gx < stacks_x * cx))[:, None] & ((gy >= 0) & (gy < stacks_y * cy))[None, :]
    weight = jnp.where((gx % cx)[:, None] < bands[0], 0.5, 1.0) * jnp.where((gy % cy)[None, :] < bands[1], 0.5, 1.0)
    weight = jnp.where(inside, weight, 0.0).astype(f32)
    weight = jnp.broadcast_to(weight[:, :, None], (cx + 2 * reach, rows1, LANES))

    rows_est1 = ceil_to(cy + 2 * hy - 4 * reach, 8)
    rows_mid = ceil_to(rows1 + 2 * reach, 8)
    inv = pl.pallas_call(
        norm_kernel,
        out_shape=jax.ShapeDtypeStruct((tiles, cx, rows_est1, LANES), f32),
        in_specs=[VMEM] * 3,
        out_specs=VMEM,
        scratch_shapes=[pltpu.VMEM((1, cx, rows1, LANES), f32)],
        name="norm",
    )(weight, tx, ty)

    up, down = line("sy")
    low = lax.ppermute(volume[:, :, cy - hy :].reshape(tiles, cx * hy, LANES), "sy", up)
    high = lax.ppermute(volume[:, :, :hy].reshape(tiles, cx * hy, LANES), "sy", down)
    volume = [low.reshape(tiles, cx, hy, LANES), volume, high.reshape(tiles, cx, hy, LANES)]
    spare = ceil_to(rows1 + reach, 8) - cy - 2 * hy
    volume = jnp.concatenate(volume + [jnp.zeros((tiles, cx, spare, LANES), f32)], axis=2)

    def x_halo(value):
        up, down = line("sx")
        low = lax.ppermute(value[:, cx - hx :], "sx", up)
        high = lax.ppermute(value[:, :hx], "sx", down)
        return jnp.concatenate([low, value, high], axis=1)

    estimate = x_halo(volume)
    seen = estimate
    for step in range(ITERS):
        dy = 2 * reach * step
        if step:
            estimate = x_halo(estimate)
        need = cy + 2 * (hy - dy)
        rows_blur = ceil_to(need - 2 * reach, 8)
        rows_out = ceil_to(need - 4 * reach, 8)
        wide = cx + 2 * reach
        estimate = pl.pallas_call(
            functools.partial(iterate_kernel, dy, need),
            out_shape=jax.ShapeDtypeStruct((tiles, cx, rows_out, LANES), f32),
            in_specs=[VMEM] * 10,
            out_specs=VMEM,
            scratch_shapes=[
                pltpu.VMEM((tiles, wide, rows_mid, LANES), f32),
                pltpu.VMEM((tiles, wide, rows_blur, LANES), f32),
            ],
            name="iterate",
        )(estimate, seen, weight, inv, tx, ty, fh, fl, bh, bl)
    result = estimate.transpose(0, 3, 1, 2).reshape(tiles * LANES, cx, cy)
    return result[hz : hz + nz]


def solution(mesh):
    in_specs = (P("gz", "sx", "sy"), P("gz"), P(), P(), P(), P())
    out_specs = P("gz", "sx", "sy")
    return jax.shard_map(body, mesh=mesh, in_specs=in_specs, out_specs=out_specs, check_vma=False)
```

```python
import functools

import jax
import jax.numpy as jnp
from jax import lax
from jax.experimental import pallas as pl
from jax.experimental.pallas import tpu as pltpu
from jax.sharding import PartitionSpec as P

ITERS = 2
LANES = 128
TINY = 1e-30
VMEM = pl.BlockSpec(memory_space=pltpu.VMEM)


def ceil_to(value, unit):
    return -(-value // unit) * unit


def line(axis):
    count = lax.axis_size(axis)
    up = [(i, i + 1) for i in range(count - 1)]
    return up, [(j, i) for i, j in up]


def lane_is_low():
    return lax.broadcasted_iota(jnp.int32, (8, LANES), 1) < LANES // 2


def halo_row(ref, tiles, packed, hx, t, p, rows):
    if not packed or t < tiles - 1:
        return ref[hx * t + p, rows, :]
    half = hx // 2
    value = ref[hx * t + p % half, rows, :]
    if p >= half:
        value = pltpu.roll(value, LANES // 2, 1)
    return jnp.where(lane_is_low(), value, 0.0)


def pack_rows(src, pay, packed, hx, x0, blocks, src_block, pay_block):
    tiles = src.shape[0]

    def step(j, carry):
        here = pl.ds(pl.multiple_of(8 * (j + src_block), 8), 8)
        there = pl.ds(pl.multiple_of(8 * (j + pay_block), 8), 8)
        for t in range(tiles - 1 if packed else tiles):
            for p in range(hx):
                pay[hx * t + p, there, :] = src[t, x0 + p, here, :]
        if packed:
            half = hx // 2
            for p in range(half):
                other = pltpu.roll(src[tiles - 1, x0 + p + half, here, :], LANES // 2, 1)
                pay[hx * (tiles - 1) + p, there, :] = jnp.where(lane_is_low(), src[tiles - 1, x0 + p, here, :], other)
        return carry

    lax.fori_loop(0, blocks, step, 0)


def conv_rows(k, v, width):
    out = []
    for x in range(width):
        acc = k[0] * v[x]
        for a in range(1, len(k)):
            acc = acc + k[a] * v[x + a]
        out.append(acc)
    return out


def y_conv(src, taps, reverse, t, width, blocks, emit):
    count = taps.shape[1]
    k = [taps[t, count - 1 - b if reverse else b] for b in range(count)]

    def step(x, carry):
        for j in range(blocks):
            acc = k[0] * src[t, x, 8 * j : 8 * j + 8, :]
            for b in range(1, count):
                acc = acc + k[b] * src[t, x, 8 * j + b : 8 * j + b + 8, :]
            emit(t, x, j, acc)
        return carry

    lax.fori_loop(0, width, step, 0)


def windows_of(tiles):
    return [(0, tiles)] if tiles <= 2 else [(w, 2) for w in range(tiles - 1)]


def depth_rows(parts, hi_ref, lo_ref):
    tiles = len(parts)
    split = []
    for part in parts:
        hi = part.astype(jnp.bfloat16)
        split.append((hi, (part - hi.astype(jnp.float32)).astype(jnp.bfloat16)))
    out = [None] * tiles
    for index, (first, span) in enumerate(windows_of(tiles)):
        his = jnp.concatenate([split[first + s][0] for s in range(span)], axis=1)
        los = jnp.concatenate([split[first + s][1] for s in range(span)], axis=1)
        dot = functools.partial(jnp.dot, preferred_element_type=jnp.float32)
        res = dot(his, hi_ref[index]) + (dot(los, hi_ref[index]) + dot(his, lo_ref[index]))
        for s in range(span):
            piece = res[:, s * LANES : (s + 1) * LANES]
            out[first + s] = piece if out[first + s] is None else out[first + s] + piece
    return out


def norm_kernel(w_ref, tx_ref, ty_ref, out_ref, mid_ref):
    tiles, count = tx_ref.shape[:2]
    reach = (count - 1) // 2
    width = out_ref.shape[1]
    for t in range(tiles):
        k = [tx_ref[t, count - 1 - a] for a in range(count)]

        def step(j, carry, k=k):
            rows = pl.ds(pl.multiple_of(8 * j, 8), 8)
            v = [w_ref[x, rows, :] for x in range(width + count - 1)]
            for x, acc in enumerate(conv_rows(k, v, width)):
                mid_ref[0, x, rows, :] = acc
            return carry

        lax.fori_loop(0, mid_ref.shape[2] // 8, step, 0)
        ky = [ty_ref[t, count - 1 - b] for b in range(count)]

        def ystep(x, carry, ky=ky, t=t):
            for j in range(out_ref.shape[2] // 8):
                at = 8 * j + reach
                acc = ky[0] * mid_ref[0, x, at : at + 8, :]
                for b in range(1, count):
                    acc = acc + ky[b] * mid_ref[0, x, at + b : at + b + 8, :]
                out_ref[t, x, 8 * j : 8 * j + 8, :] = 1.0 / jnp.maximum(acc, TINY)
            return carry

        lax.fori_loop(0, width, ystep, 0)


def assemble_kernel(packed, hx, cut, vol_ref, low_ref, high_ref, ext_ref, *pays):
    tiles, cx, cy = vol_ref.shape[:3]
    hy = low_ref.shape[1] // cx
    end = cy + 2 * hy
    for t in range(tiles):
        for x in range(cx):
            ext_ref[t, x, 0:hy, :] = low_ref[t, hy * x : hy * x + hy, :]
            ext_ref[t, x, hy : hy + cy, :] = vol_ref[t, x]
            ext_ref[t, x, hy + cy : end, :] = high_ref[t, hy * x : hy * x + hy, :]
            ext_ref[t, x, end:, :] = jnp.zeros((ext_ref.shape[2] - end, LANES), jnp.float32)
    for n, (pay_up, pay_down) in enumerate((pays[:2], pays[2:])):
        first, last = (0, cut) if n == 0 else (cut, end)
        blocks = -(-(last - first) // 8)
        pack_rows(ext_ref, pay_up, packed, hx, cx - hx, blocks, first // 8, 0)
        pack_rows(ext_ref, pay_down, packed, hx, 0, blocks, first // 8, 0)


def iterate_kernel(plan, *refs):
    refs = list(refs)
    take = refs.pop
    est_ref = take(0)
    halos = [(take(0), take(0), first, last) for first, last in plan["halos"]]
    w_ref = take(0) if plan["make_data"] else None
    data_in = None if plan["make_data"] else take(0)
    tail_ref = take(0) if plan["tail"] else None
    inv_ref, tx_ref, ty_ref, fh_ref, fl_ref, bh_ref, bl_ref = [take(0) for _ in range(7)]
    out_ref = take(0)
    data_ref = take(0) if plan["make_data"] else data_in
    pays = [take(0), take(0)] if plan["pay"] else None
    mid_ref, blur_ref = refs
    packed, hx, low, high = plan["packed"], plan["hx"], plan["low"], plan["high"]
    est_base, data_base, data_off, inv_off = plan["est_base"], plan["data_base"], plan["data_off"], plan["inv_off"]
    tiles, cx = est_ref.shape[:2]
    count = tx_ref.shape[1]
    reach = (count - 1) // 2
    wide = cx + 2 * reach
    rows = blur_ref.shape[2]
    last_block = -(-(high + 4 * reach) // 8)
    data_first = data_base // 8 if plan["make_data"] else low // 8
    half = (hx - 2 * reach) // 2

    for t in range(tiles):
        k = [tx_ref[t, a] for a in range(count)]
        for lo_ref, hi_ref, first, last in halos:

            def gather(j, t=t, lo_ref=lo_ref, hi_ref=hi_ref, first=first):
                here = pl.ds(pl.multiple_of(8 * j - est_base, 8), 8)
                there = pl.ds(pl.multiple_of(8 * j - first, 8), 8)
                v = [halo_row(lo_ref, tiles, packed, hx, t, p, there) for p in range(hx)]
                v += [est_ref[t, x, here, :] for x in range(cx)]
                return v + [halo_row(hi_ref, tiles, packed, hx, t, p, there) for p in range(hx)]

            def keep(j, v, t=t):
                here = pl.ds(pl.multiple_of(8 * j, 8), 8)
                there = pl.ds(pl.multiple_of(8 * j - data_base, 8), 8)
                for x in range(wide):
                    data_ref[t, x, there, :] = w_ref[x, here, :] * v[x + reach]

            def only_data(j, carry, gather=gather, keep=keep):
                keep(j, gather(j))
                return carry

            def step(j, carry, gather=gather, keep=keep, k=k, t=t):
                v = gather(j)
                if plan["make_data"]:
                    keep(j, v)
                mid = pl.ds(pl.multiple_of(8 * j - low, 8), 8)
                for x, acc in enumerate(conv_rows(k, v, wide)):
                    mid_ref[t, x, mid, :] = acc
                return carry

            a, b = max(first // 8, data_first), min(last // 8, low // 8)
            if plan["make_data"] and a < b:
                lax.fori_loop(a, b, only_data, 0)
            a, b = max(first // 8, low // 8), min(-(-last // 8), last_block)
            if a < b:
                lax.fori_loop(a, b, step, 0)

        def put(t, x, j, acc):
            blur_ref[t, x, 8 * j : 8 * j + 8, :] = acc

        y_conv(mid_ref, ty_ref, False, t, wide, rows // 8, put)

    spot0 = low + data_off + reach - data_base

    def depth(i, carry):
        spot = pl.ds(2 * i, 2)
        size = 2 * rows
        parts = [blur_ref[t, spot].reshape(size, LANES) for t in range(tiles)]
        blurred = depth_rows(parts, fh_ref, fl_ref)
        ratio = []
        for t in range(tiles):
            seen = data_ref[t, spot, spot0 : spot0 + rows, :].reshape(size, LANES)
            ratio.append(seen / jnp.maximum(blurred[t], TINY))
        spread = depth_rows(ratio, bh_ref, bl_ref)
        for t in range(tiles):
            blur_ref[t, spot] = spread[t].reshape(2, rows, LANES)
        return carry

    lax.fori_loop(0, wide // 2, depth, 0)

    out_skip = plan["tail"]
    blocks = -(-(high - low) // 8)
    for t in range(tiles):
        k = [tx_ref[t, count - 1 - a] for a in range(count)]

        def back(j, carry, k=k, t=t):
            here = pl.ds(pl.multiple_of(8 * j, 8), 8)
            v = [blur_ref[t, x, here, :] for x in range(wide)]
            for x, acc in enumerate(conv_rows(k, v, cx)):
                mid_ref[t, x, here, :] = acc
            return carry

        lax.fori_loop(0, rows // 8, back, 0)

        def finish(t, x, j, acc):
            at = 8 * j + low + 2 * reach - est_base
            to = 8 * j + out_skip
            scale = 8 * j + low + inv_off
            out_ref[t, x, to : to + 8, :] = est_ref[t, x, at : at + 8, :] * acc * inv_ref[t, x, scale : scale + 8, :]

        y_conv(mid_ref, ty_ref, True, t, cx, blocks, finish)

    if out_skip:
        have = tail_ref.shape[2]
        for t in range(tiles):

            def copy(x, carry, t=t):
                out_ref[t, x, 0:out_skip, :] = tail_ref[t, x, have - out_skip : have, :]
                return carry

            lax.fori_loop(0, cx, copy, 0)
    if pays:
        pack_rows(out_ref, pays[0], packed, hx, cx - hx, blocks, out_skip // 8, 0)
        pack_rows(out_ref, pays[1], packed, hx, 0, blocks, out_skip // 8, 0)


def body(observed, zone_of_slice, lateral_x, lateral_y, depth_psf, stitch_width):
    nz, cx, cy = observed.shape
    taps = lateral_x.shape[1]
    reach = (taps - 1) // 2
    zreach = (depth_psf.shape[0] - 1) // 2
    hz = 2 * zreach * ITERS
    hy = 2 * reach * ITERS
    hx = 2 * reach
    slabs = lax.axis_size("gz")
    tiles = ceil_to(nz + 2 * hz, LANES) // LANES
    f32 = jnp.float32

    zones = zone_of_slice.astype(f32)

    def with_zones(part, ids):
        flat = jnp.pad(ids, (0, cx * cy - ids.shape[0]))
        return jnp.concatenate([part, flat.reshape(1, cx, cy)], axis=0)

    if slabs == 2:
        both = jnp.concatenate([observed[nz - hz :], observed[:hz]], axis=0)
        got = lax.ppermute(with_zones(both, jnp.concatenate([zones[nz - hz :], zones[:hz]])), "gz", [(0, 1), (1, 0)])
        before, after = got[:hz], got[hz : 2 * hz]
        got_ids = got[2 * hz].reshape(-1)
        ids_before, ids_after = got_ids[:hz], got_ids[hz : 2 * hz]
    else:
        up = [(i, (i + 1) % slabs) for i in range(slabs)]
        first = lax.ppermute(with_zones(observed[nz - hz :], zones[nz - hz :]), "gz", up)
        second = lax.ppermute(with_zones(observed[:hz], zones[:hz]), "gz", [(j, i) for i, j in up])
        before, after = first[:hz], second[:hz]
        ids_before, ids_after = first[hz].reshape(-1)[:hz], second[hz].reshape(-1)[:hz]
    pad = tiles * LANES - nz - 2 * hz
    volume = jnp.concatenate([before, observed, after, jnp.zeros((pad, cx, cy), f32)], axis=0)
    ids = jnp.concatenate([ids_before, zones, ids_after, jnp.full((pad,), -1.0, f32)])
    volume = volume.reshape(tiles, LANES, cx, cy).transpose(0, 2, 3, 1)

    match = (ids[None, :] == jnp.arange(lateral_x.shape[0], dtype=f32)[:, None]).astype(f32)

    def lanes_of(kernels):
        table = jnp.sum(match[:, None, :] * kernels[:, :, None], axis=0)
        table = table.reshape(taps, tiles, 1, LANES).transpose(1, 0, 2, 3)
        return jnp.broadcast_to(table, (tiles, taps, 8, LANES))

    tx, ty = lanes_of(lateral_x), lanes_of(lateral_y)

    kernel = depth_psf / jnp.sum(depth_psf)
    wins = windows_of(tiles)
    size = wins[0][1] * LANES
    off = jnp.arange(size)[None, :] - jnp.arange(size)[:, None]
    band = jnp.zeros((size, size), f32)
    flip = jnp.zeros((size, size), f32)
    for j in range(kernel.shape[0]):
        band = band + jnp.where(off == j - zreach, kernel[j], 0.0)
        flip = flip + jnp.where(off == zreach - j, kernel[j], 0.0)

    def halves(matrix):
        cols = jnp.arange(size)
        parts = []
        for index in range(len(wins)):
            low = 0 if index == 0 else LANES // 2
            high = size if index == len(wins) - 1 else LANES + LANES // 2
            parts.append(jnp.where((cols >= low) & (cols < high), matrix, 0.0))
        full = jnp.stack(parts)
        top = lax.reduce_precision(full, 8, 7)
        return top.astype(jnp.bfloat16), (full - top).astype(jnp.bfloat16)

    fh, fl = halves(band)
    bh, bl = halves(flip)

    sx, sy = lax.axis_index("sx"), lax.axis_index("sy")
    stacks_x, stacks_y = stitch_width.shape[:2]
    full = ceil_to(cy + 2 * hy + reach, 8)
    gx = sx * cx - reach + jnp.arange(cx + 2 * reach)
    gy = sy * cy - hy + jnp.arange(full)
    near = lax.dynamic_slice(jnp.pad(stitch_width, ((1, 1), (1, 1), (0, 0))), (sx, sy, jnp.int32(0)), (3, 3, 2))
    of_x = gx // cx - sx + 1
    of_y = gy // cy - sy + 1
    bands = jnp.zeros((2, gx.shape[0], full), jnp.int32)
    for a in range(3):
        for b in range(3):
            hit = (of_x[:, None] == a) & (of_y[None, :] == b)
            bands = jnp.where(hit[None], near[a, b][:, None, None], bands)
    inside = ((gx >= 0) & (gx < stacks_x * cx))[:, None] & ((gy >= 0) & (gy < stacks_y * cy))[None, :]
    weight = jnp.where((gx % cx)[:, None] < bands[0], 0.5, 1.0) * jnp.where((gy % cy)[None, :] < bands[1], 0.5, 1.0)
    weight = jnp.where(inside, weight, 0.0).astype(f32)
    weight = jnp.broadcast_to(weight[:, :, None], (cx + 2 * reach, full, LANES))

    up, down = line("sy")
    low = lax.ppermute(volume[:, :, cy - hy :].reshape(tiles, cx * hy, LANES), "sy", up)
    high = lax.ppermute(volume[:, :, :hy].reshape(tiles, cx * hy, LANES), "sy", down)

    wide = cx + 2 * reach
    packed = nz + 2 * hz - (tiles - 1) * LANES <= LANES // 2
    planes = hx * (tiles - 1) + hx // 2 if packed else hx * tiles
    end0, end1, end2 = cy + 2 * hy, cy + 2 * hy - 4 * reach, cy
    mid1 = ceil_to(end1 // 2, 8) + 8
    mid2 = mid1 - ceil_to(4 * reach, 8)
    cut = ceil_to(mid1 + 4 * reach, 8)
    up, down = line("sx")

    def shape(*dims):
        return jax.ShapeDtypeStruct(dims, f32)

    def pay_shapes(rows):
        return [shape(planes, ceil_to(rows, 8), LANES)] * 2

    def swap(pays):
        return lax.ppermute(pays[0], "sx", up), lax.ppermute(pays[1], "sx", down)

    def call(kernel, out_shape, args, scratch, name, limit, flops):
        moved = sum(a.size * 4 for a in args) + sum(o.size * 4 for o in out_shape)
        return pl.pallas_call(
            kernel,
            out_shape=out_shape,
            in_specs=[VMEM] * len(args),
            out_specs=[VMEM] * len(out_shape),
            scratch_shapes=[pltpu.VMEM(dims, f32) for dims in scratch],
            compiler_params=pltpu.CompilerParams(vmem_limit_bytes=limit << 20),
            cost_estimate=pl.CostEstimate(flops=flops, bytes_accessed=moved, transcendentals=0),
            name=name,
        )(*args)

    ext, *pays = call(
        functools.partial(assemble_kernel, packed, hx, cut),
        [shape(tiles, cx, full, LANES)] + pay_shapes(cut) + pay_shapes(end0 - cut),
        (volume, low, high), [], "assemble", 8, 1,
    )
    halo_a = swap(pays[:2])
    halo_b = swap(pays[2:])
    (inv,) = call(
        norm_kernel, [shape(tiles, cx, ceil_to(end1, 8), LANES)], (weight, tx, ty),
        [(1, cx, full, LANES)], "norm", 8, 1,
    )
    tables = (inv, tx, ty, fh, fl, bh, bl)

    def iterate(name, est, halos, extra, plan, outs):
        rows = ceil_to(plan["high"] - plan["low"] + 2 * reach, 8)
        args = (est,) + tuple(h for _, pair in halos for h in pair) + extra + tables
        plan = dict(plan, hx=hx, packed=packed, halos=[rng for rng, _ in halos])
        scratch = [(tiles, wide, rows + 16, LANES), (tiles, wide, rows, LANES)]
        return call(functools.partial(iterate_kernel, plan), outs, args, scratch, name, 16, 1)

    data_at = mid2 + 8
    est_a, data_a, *pays = iterate(
        "first_a", ext, [((0, cut), halo_a)], (weight,),
        dict(low=0, high=mid1, est_base=0, data_base=0, data_off=0, inv_off=0, make_data=True, tail=0, pay=True),
        [shape(tiles, cx, mid1, LANES), shape(tiles, wide, cut, LANES)] + pay_shapes(mid1),
    )
    halo_c = swap(pays)
    tail = mid1 - mid2
    est_b, data_b, *pays = iterate(
        "first_b", ext, [((0, cut), halo_a), ((cut, end0), halo_b)], (weight, est_a),
        dict(low=mid1, high=end1, est_base=0, data_base=data_at, data_off=0, inv_off=0, make_data=True, tail=tail, pay=True),
        [shape(tiles, cx, ceil_to(end1, 8) - mid2, LANES), shape(tiles, wide, full - data_at, LANES)] + pay_shapes(end1 - mid1),
    )
    halo_d = swap(pays)
    shift = 2 * reach
    (out_a,) = iterate(
        "second_a", est_a, [((0, mid1), halo_c)], (data_a,),
        dict(low=0, high=mid2, est_base=0, data_base=0, data_off=shift, inv_off=shift, make_data=False, tail=0, pay=False),
        [shape(tiles, cx, mid2, LANES)],
    )
    (out_b,) = iterate(
        "second_b", est_b, [((0, mid1), halo_c), ((mid1, end1), halo_d)], (data_b,),
        dict(low=mid2, high=end2, est_base=mid2, data_base=data_at, data_off=shift, inv_off=shift, make_data=False, tail=0, pay=False),
        [shape(tiles, cx, end2 - mid2, LANES)],
    )
    estimate = jnp.concatenate([out_a, out_b], axis=2)
    result = estimate.transpose(0, 3, 1, 2).reshape(tiles * LANES, cx, cy)
    return result[hz : hz + nz]


def solution(mesh):
    in_specs = (P("gz", "sx", "sy"), P("gz"), P(), P(), P(), P())
    out_specs = P("gz", "sx", "sy")
    return jax.shard_map(body, mesh=mesh, in_specs=in_specs, out_specs=out_specs, check_vma=False)
```

```python
import functools

import jax
import jax.numpy as jnp
from jax import lax
from jax.experimental import pallas as pl
from jax.experimental.pallas import tpu as pltpu
from jax.sharding import PartitionSpec as P

ITERS = 2
LANES = 128
TINY = 1e-30
VMEM = pl.BlockSpec(memory_space=pltpu.VMEM)


def ceil_to(value, unit):
    return -(-value // unit) * unit


def line(axis):
    count = lax.axis_size(axis)
    up = [(i, i + 1) for i in range(count - 1)]
    return up, [(j, i) for i, j in up]


def lane_is_low():
    return lax.broadcasted_iota(jnp.int32, (8, LANES), 1) < LANES // 2


def halo_row(ref, tiles, packed, hx, t, p, rows):
    if not packed or t < tiles - 1:
        return ref[hx * t + p, rows, :]
    half = hx // 2
    value = ref[hx * t + p % half, rows, :]
    if p >= half:
        value = pltpu.roll(value, LANES // 2, 1)
    return jnp.where(lane_is_low(), value, 0.0)


def pack_rows(src, pay, packed, hx, x0, blocks, src_block, pay_block):
    tiles = src.shape[0]

    def step(j, carry):
        here = pl.ds(pl.multiple_of(8 * (j + src_block), 8), 8)
        there = pl.ds(pl.multiple_of(8 * (j + pay_block), 8), 8)
        for t in range(tiles - 1 if packed else tiles):
            for p in range(hx):
                pay[hx * t + p, there, :] = src[t, x0 + p, here, :]
        if packed:
            half = hx // 2
            for p in range(half):
                other = pltpu.roll(src[tiles - 1, x0 + p + half, here, :], LANES // 2, 1)
                pay[hx * (tiles - 1) + p, there, :] = jnp.where(lane_is_low(), src[tiles - 1, x0 + p, here, :], other)
        return carry

    lax.fori_loop(0, blocks, step, 0)


def conv_rows(k, v, width):
    out = []
    for x in range(width):
        acc = k[0] * v[x]
        for a in range(1, len(k)):
            acc = acc + k[a] * v[x + a]
        out.append(acc)
    return out


def y_conv(src, taps, reverse, t, width, blocks, emit):
    count = taps.shape[1]
    k = [taps[t, count - 1 - b if reverse else b] for b in range(count)]

    def step(x, carry):
        for j in range(blocks):
            acc = k[0] * src[t, x, 8 * j : 8 * j + 8, :]
            for b in range(1, count):
                acc = acc + k[b] * src[t, x, 8 * j + b : 8 * j + b + 8, :]
            emit(t, x, j, acc)
        return carry

    lax.fori_loop(0, width, step, 0)


def windows_of(tiles):
    return [(0, tiles)] if tiles <= 2 else [(w, 2) for w in range(tiles - 1)]


def depth_rows(parts, hi_ref, lo_ref):
    tiles = len(parts)
    split = []
    for part in parts:
        hi = part.astype(jnp.bfloat16)
        split.append((hi, (part - hi.astype(jnp.float32)).astype(jnp.bfloat16)))
    out = [None] * tiles
    for index, (first, span) in enumerate(windows_of(tiles)):
        his = jnp.concatenate([split[first + s][0] for s in range(span)], axis=1)
        los = jnp.concatenate([split[first + s][1] for s in range(span)], axis=1)
        dot = functools.partial(jnp.dot, preferred_element_type=jnp.float32)
        res = dot(his, hi_ref[index]) + (dot(los, hi_ref[index]) + dot(his, lo_ref[index]))
        for s in range(span):
            piece = res[:, s * LANES : (s + 1) * LANES]
            out[first + s] = piece if out[first + s] is None else out[first + s] + piece
    return out


def norm_kernel(w_ref, tx_ref, ty_ref, out_ref, mid_ref):
    tiles, count = tx_ref.shape[:2]
    reach = (count - 1) // 2
    width = out_ref.shape[1]
    for t in range(tiles):
        k = [tx_ref[t, count - 1 - a] for a in range(count)]

        def step(j, carry, k=k):
            rows = pl.ds(pl.multiple_of(8 * j, 8), 8)
            v = [w_ref[x, rows, :] for x in range(width + count - 1)]
            for x, acc in enumerate(conv_rows(k, v, width)):
                mid_ref[0, x, rows, :] = acc
            return carry

        lax.fori_loop(0, mid_ref.shape[2] // 8, step, 0)
        ky = [ty_ref[t, count - 1 - b] for b in range(count)]

        def ystep(x, carry, ky=ky, t=t):
            for j in range(out_ref.shape[2] // 8):
                at = 8 * j + reach
                acc = ky[0] * mid_ref[0, x, at : at + 8, :]
                for b in range(1, count):
                    acc = acc + ky[b] * mid_ref[0, x, at + b : at + b + 8, :]
                out_ref[t, x, 8 * j : 8 * j + 8, :] = 1.0 / jnp.maximum(acc, TINY)
            return carry

        lax.fori_loop(0, width, ystep, 0)


def band_kernel(psf_ref, fh_ref, fl_ref, bh_ref, bl_ref):
    windows, size = fh_ref.shape[:2]
    taps = psf_ref.shape[0]
    total = psf_ref[0]
    for j in range(1, taps):
        total = total + psf_ref[j]
    step = LANES // 2
    for r in range(0, size, step):
        shape = (step, size)
        cols = lax.broadcasted_iota(jnp.int32, shape, 1)
        off = cols - lax.broadcasted_iota(jnp.int32, shape, 0) - r + (taps - 1) // 2
        band, flip = jnp.zeros(shape, jnp.float32), jnp.zeros(shape, jnp.float32)
        for j in range(taps):
            band = jnp.where(off == j, psf_ref[j], band)
            flip = jnp.where(off == taps - 1 - j, psf_ref[j], flip)
        for matrix, hi_ref, lo_ref in ((band, fh_ref, fl_ref), (flip, bh_ref, bl_ref)):
            matrix = matrix / jnp.full(shape, total, jnp.float32)
            for w in range(windows):
                first = 0 if w == 0 else LANES // 2
                last = size if w == windows - 1 else LANES + LANES // 2
                part = jnp.where((cols >= first) & (cols < last), matrix, 0.0)
                hi = part.astype(jnp.bfloat16)
                hi_ref[w, r : r + step, :] = hi
                lo_ref[w, r : r + step, :] = (part - hi.astype(jnp.float32)).astype(jnp.bfloat16)


def edges_kernel(hy, after, vol_ref, low_ref, high_ref, *diags):
    tiles, cx, cy = vol_ref.shape[:3]
    for x in range(cx):
        to = slice(hy * x, hy * x + hy)
        for ref, rows, diag in ((low_ref, slice(cy - hy, cy), 0), (high_ref, slice(0, hy), 1)):
            for t in range(tiles):
                ref[t, to, :] = vol_ref[t, x, rows, :]
            if diags:
                lane = lax.broadcasted_iota(jnp.int32, (hy, LANES), 1)
                diags[diag][to, :] = jnp.where(lane < after, vol_ref[tiles - 1, x, rows, :], vol_ref[0, x, rows, :])


def assemble_kernel(packed, hx, cut, after, refs_in, *refs):
    vol_ref, low_ref, high_ref = refs[:3]
    halo_ref, low_z, high_z = refs[3:6] if refs_in == 6 else (None,) * 3
    ext_ref, *pays = refs[refs_in:]
    tiles, cx, cy = vol_ref.shape[:3]
    hy = low_ref.shape[1] // cx
    end = cy + 2 * hy

    def merge(t, value, halo, rows):
        if halo is None or 0 < t < tiles - 1:
            return value
        lane = lax.broadcasted_iota(jnp.int32, value.shape, 1)
        use = lane < after if t == 0 else (lane >= after) & (lane < 2 * after)
        return jnp.where(use, halo[rows], value)

    for t in range(tiles):
        for x in range(cx):
            edge = slice(hy * x, hy * x + hy)
            ext_ref[t, x, 0:hy, :] = merge(t, low_ref[t, edge, :], low_z, edge)
            ext_ref[t, x, hy : hy + cy, :] = merge(t, vol_ref[t, x], halo_ref, x)
            ext_ref[t, x, hy + cy : end, :] = merge(t, high_ref[t, edge, :], high_z, edge)
            ext_ref[t, x, end:, :] = jnp.zeros((ext_ref.shape[2] - end, LANES), jnp.float32)
    for n, (pay_up, pay_down) in enumerate((pays[:2], pays[2:])):
        first, last = (0, cut) if n == 0 else (cut, end)
        blocks = -(-(last - first) // 8)
        pack_rows(ext_ref, pay_up, packed, hx, cx - hx, blocks, first // 8, 0)
        pack_rows(ext_ref, pay_down, packed, hx, 0, blocks, first // 8, 0)


def iterate_kernel(plan, *refs):
    refs = list(refs)
    take = refs.pop
    est_ref = take(0)
    halos = [(take(0), take(0), first, last) for first, last in plan["halos"]]
    w_ref = take(0) if plan["make_data"] else None
    data_in = None if plan["make_data"] else take(0)
    tail_ref = take(0) if plan["tail"] else None
    inv_ref, tx_ref, ty_ref, fh_ref, fl_ref, bh_ref, bl_ref = [take(0) for _ in range(7)]
    out_ref = take(0)
    data_ref = take(0) if plan["make_data"] else data_in
    pays = [take(0), take(0)] if plan["pay"] else None
    mid_ref, blur_ref = refs
    packed, hx, low, high = plan["packed"], plan["hx"], plan["low"], plan["high"]
    est_base, data_base, data_off, inv_off = plan["est_base"], plan["data_base"], plan["data_off"], plan["inv_off"]
    tiles, cx = est_ref.shape[:2]
    count = tx_ref.shape[1]
    reach = (count - 1) // 2
    wide = cx + 2 * reach
    rows = blur_ref.shape[2]
    last_block = -(-(high + 4 * reach) // 8)
    data_first = data_base // 8 if plan["make_data"] else low // 8
    half = (hx - 2 * reach) // 2

    for t in range(tiles):
        k = [tx_ref[t, a] for a in range(count)]
        for lo_ref, hi_ref, first, last in halos:

            def gather(j, t=t, lo_ref=lo_ref, hi_ref=hi_ref, first=first):
                here = pl.ds(pl.multiple_of(8 * j - est_base, 8), 8)
                there = pl.ds(pl.multiple_of(8 * j - first, 8), 8)
                v = [halo_row(lo_ref, tiles, packed, hx, t, p, there) for p in range(hx)]
                v += [est_ref[t, x, here, :] for x in range(cx)]
                return v + [halo_row(hi_ref, tiles, packed, hx, t, p, there) for p in range(hx)]

            def keep(j, v, t=t):
                here = pl.ds(pl.multiple_of(8 * j, 8), 8)
                there = pl.ds(pl.multiple_of(8 * j - data_base, 8), 8)
                for x in range(wide):
                    data_ref[t, x, there, :] = w_ref[x, here, :] * v[x + reach]

            def only_data(j, carry, gather=gather, keep=keep):
                keep(j, gather(j))
                return carry

            def step(j, carry, gather=gather, keep=keep, k=k, t=t):
                v = gather(j)
                if plan["make_data"]:
                    keep(j, v)
                mid = pl.ds(pl.multiple_of(8 * j - low, 8), 8)
                for x, acc in enumerate(conv_rows(k, v, wide)):
                    mid_ref[t, x, mid, :] = acc
                return carry

            a, b = max(first // 8, data_first), min(last // 8, low // 8)
            if plan["make_data"] and a < b:
                lax.fori_loop(a, b, only_data, 0)
            a, b = max(first // 8, low // 8), min(-(-last // 8), last_block)
            if a < b:
                lax.fori_loop(a, b, step, 0)

        def put(t, x, j, acc):
            blur_ref[t, x, 8 * j : 8 * j + 8, :] = acc

        y_conv(mid_ref, ty_ref, False, t, wide, rows // 8, put)

    spot0 = low + data_off + reach - data_base

    def depth(i, carry):
        spot = pl.ds(2 * i, 2)
        size = 2 * rows
        parts = [blur_ref[t, spot].reshape(size, LANES) for t in range(tiles)]
        blurred = depth_rows(parts, fh_ref, fl_ref)
        ratio = []
        for t in range(tiles):
            seen = data_ref[t, spot, spot0 : spot0 + rows, :].reshape(size, LANES)
            ratio.append(seen / jnp.maximum(blurred[t], TINY))
        spread = depth_rows(ratio, bh_ref, bl_ref)
        for t in range(tiles):
            blur_ref[t, spot] = spread[t].reshape(2, rows, LANES)
        return carry

    lax.fori_loop(0, wide // 2, depth, 0)

    out_skip = plan["tail"]
    blocks = -(-(high - low) // 8)
    for t in range(tiles):
        k = [tx_ref[t, count - 1 - a] for a in range(count)]

        def back(j, carry, k=k, t=t):
            here = pl.ds(pl.multiple_of(8 * j, 8), 8)
            v = [blur_ref[t, x, here, :] for x in range(wide)]
            for x, acc in enumerate(conv_rows(k, v, cx)):
                mid_ref[t, x, here, :] = acc
            return carry

        lax.fori_loop(0, rows // 8, back, 0)

        def finish(t, x, j, acc):
            at = 8 * j + low + 2 * reach - est_base
            to = 8 * j + out_skip
            scale = 8 * j + low + inv_off
            out_ref[t, x, to : to + 8, :] = est_ref[t, x, at : at + 8, :] * acc * inv_ref[t, x, scale : scale + 8, :]

        y_conv(mid_ref, ty_ref, True, t, cx, blocks, finish)

    if out_skip:
        have = tail_ref.shape[2]
        for t in range(tiles):

            def copy(x, carry, t=t):
                out_ref[t, x, 0:out_skip, :] = tail_ref[t, x, have - out_skip : have, :]
                return carry

            lax.fori_loop(0, cx, copy, 0)
    if pays:
        pack_rows(out_ref, pays[0], packed, hx, cx - hx, blocks, out_skip // 8, 0)
        pack_rows(out_ref, pays[1], packed, hx, 0, blocks, out_skip // 8, 0)


def body(observed, zone_of_slice, lateral_x, lateral_y, depth_psf, stitch_width):
    nz, cx, cy = observed.shape
    taps = lateral_x.shape[1]
    reach = (taps - 1) // 2
    zreach = (depth_psf.shape[0] - 1) // 2
    hz = 2 * zreach * ITERS
    hy = 2 * reach * ITERS
    hx = 2 * reach
    slabs = lax.axis_size("gz")
    tiles = ceil_to(nz + 2 * hz, LANES) // LANES
    f32 = jnp.float32

    zones = zone_of_slice.astype(f32)

    def with_zones(part, ids):
        flat = jnp.pad(ids, (0, cx * cy - ids.shape[0]))
        return jnp.concatenate([part, flat.reshape(1, cx, cy)], axis=0)

    if slabs == 2:
        both = jnp.concatenate([observed[nz - hz :], observed[:hz]], axis=0)
        got = lax.ppermute(with_zones(both, jnp.concatenate([zones[nz - hz :], zones[:hz]])), "gz", [(0, 1), (1, 0)])
        before, after = got[:hz], got[hz : 2 * hz]
        got_ids = got[2 * hz].reshape(-1)
        ids_before, ids_after = got_ids[:hz], got_ids[hz : 2 * hz]
    else:
        up = [(i, (i + 1) % slabs) for i in range(slabs)]
        first = lax.ppermute(with_zones(observed[nz - hz :], zones[nz - hz :]), "gz", up)
        second = lax.ppermute(with_zones(observed[:hz], zones[:hz]), "gz", [(j, i) for i, j in up])
        before, after = first[:hz], second[:hz]
        ids_before, ids_after = first[hz].reshape(-1)[:hz], second[hz].reshape(-1)[:hz]
    pad = tiles * LANES - nz - 2 * hz
    ids = jnp.concatenate([ids_before, zones, ids_after, jnp.full((pad,), -1.0, f32)])
    direct = slabs == 2 and nz % LANES == 0 and 2 * hz <= LANES
    if direct:
        volume = jnp.pad(observed, ((hz, hz + pad), (0, 0), (0, 0)))
        halo = jnp.pad(got[: 2 * hz], ((0, LANES - 2 * hz), (0, 0), (0, 0))).transpose(1, 2, 0)
    else:
        volume = jnp.concatenate([before, observed, after, jnp.zeros((pad, cx, cy), f32)], axis=0)
    volume = volume.reshape(tiles, LANES, cx, cy).transpose(0, 2, 3, 1)

    match = (ids[None, :] == jnp.arange(lateral_x.shape[0], dtype=f32)[:, None]).astype(f32)

    def lanes_of(kernels):
        table = jnp.sum(match[:, None, :] * kernels[:, :, None], axis=0)
        table = table.reshape(taps, tiles, 1, LANES).transpose(1, 0, 2, 3)
        return jnp.broadcast_to(table, (tiles, taps, 8, LANES))

    tx, ty = lanes_of(lateral_x), lanes_of(lateral_y)

    sx, sy = lax.axis_index("sx"), lax.axis_index("sy")
    stacks_x, stacks_y = stitch_width.shape[:2]
    full = ceil_to(cy + 2 * hy + reach, 8)
    gx = sx * cx - reach + jnp.arange(cx + 2 * reach)
    gy = sy * cy - hy + jnp.arange(full)
    near = lax.dynamic_slice(jnp.pad(stitch_width, ((1, 1), (1, 1), (0, 0))), (sx, sy, jnp.int32(0)), (3, 3, 2))
    of_x = gx // cx - sx + 1
    of_y = gy // cy - sy + 1
    bands = jnp.zeros((2, gx.shape[0], full), jnp.int32)
    for a in range(3):
        for b in range(3):
            hit = (of_x[:, None] == a) & (of_y[None, :] == b)
            bands = jnp.where(hit[None], near[a, b][:, None, None], bands)
    inside = ((gx >= 0) & (gx < stacks_x * cx))[:, None] & ((gy >= 0) & (gy < stacks_y * cy))[None, :]
    weight = jnp.where((gx % cx)[:, None] < bands[0], 0.5, 1.0) * jnp.where((gy % cy)[None, :] < bands[1], 0.5, 1.0)
    weight = jnp.where(inside, weight, 0.0).astype(f32)
    weight = jnp.broadcast_to(weight[:, :, None], (cx + 2 * reach, full, LANES))

    wide = cx + 2 * reach
    packed = nz + 2 * hz - (tiles - 1) * LANES <= LANES // 2
    planes = hx * (tiles - 1) + hx // 2 if packed else hx * tiles
    end0, end1, end2 = cy + 2 * hy, cy + 2 * hy - 4 * reach, cy
    mid1 = ceil_to(end1 // 2, 8) + 8
    mid2 = mid1 - ceil_to(4 * reach, 8)
    cut = ceil_to(mid1 + 4 * reach, 8)
    up, down = line("sx")

    def shape(*dims):
        return jax.ShapeDtypeStruct(dims, f32)

    def pay_shapes(rows):
        return [shape(planes, ceil_to(rows, 8), LANES)] * 2

    def swap(pays):
        return lax.ppermute(pays[0], "sx", up), lax.ppermute(pays[1], "sx", down)

    def call(kernel, out_shape, args, scratch, name, limit, flops, specs=VMEM):
        moved = sum(a.size * 4 for a in args) + sum(o.size * 4 for o in out_shape)
        return pl.pallas_call(
            kernel,
            out_shape=out_shape,
            in_specs=[specs] * len(args),
            out_specs=[VMEM] * len(out_shape),
            scratch_shapes=[pltpu.VMEM(dims, f32) for dims in scratch],
            compiler_params=pltpu.CompilerParams(vmem_limit_bytes=limit << 20),
            cost_estimate=pl.CostEstimate(flops=flops, bytes_accessed=moved, transcendentals=0),
            name=name,
        )(*args)

    wins = windows_of(tiles)
    size = wins[0][1] * LANES
    fh, fl, bh, bl = call(
        band_kernel, [jax.ShapeDtypeStruct((len(wins), size, size), jnp.bfloat16)] * 4, (depth_psf,), [], "band", 8, 1,
        specs=pl.BlockSpec(memory_space=pltpu.SMEM),
    )

    stacks = lax.axis_size("sy")
    edge = shape(tiles, cx * hy, LANES)
    diag = [shape(cx * hy, LANES)] * 2 if direct else []
    low, high, *corner = call(functools.partial(edges_kernel, hy, hz), [edge, edge] + diag, (volume,), [], "edges", 8, 1)
    yup, ydown = line("sy")
    parts = [volume, lax.ppermute(low, "sy", yup), lax.ppermute(high, "sy", ydown)]
    if direct:
        cross = [(2 * i + g, 2 * i + 2 + (1 - g)) for i in range(stacks - 1) for g in range(2)]
        parts.append(halo)
        parts.append(lax.ppermute(corner[0], ("sy", "gz"), cross))
        parts.append(lax.ppermute(corner[1], ("sy", "gz"), [(j, i) for i, j in cross]))

    ext, *pays = call(
        functools.partial(assemble_kernel, packed, hx, cut, hz, len(parts)),
        [shape(tiles, cx, full, LANES)] + pay_shapes(cut) + pay_shapes(end0 - cut),
        tuple(parts), [], "assemble", 8, 1,
    )
    halo_a = swap(pays[:2])
    halo_b = swap(pays[2:])
    (inv,) = call(
        norm_kernel, [shape(tiles, cx, ceil_to(end1, 8), LANES)], (weight, tx, ty),
        [(1, cx, full, LANES)], "norm", 8, 1,
    )
    tables = (inv, tx, ty, fh, fl, bh, bl)

    def iterate(name, est, halos, extra, plan, outs):
        rows = ceil_to(plan["high"] - plan["low"] + 2 * reach, 8)
        args = (est,) + tuple(h for _, pair in halos for h in pair) + extra + tables
        plan = dict(plan, hx=hx, packed=packed, halos=[rng for rng, _ in halos])
        scratch = [(tiles, wide, rows + 16, LANES), (tiles, wide, rows, LANES)]
        return call(functools.partial(iterate_kernel, plan), outs, args, scratch, name, 16, 1)

    data_at = mid2 + 8
    est_a, data_a, *pays = iterate(
        "first_a", ext, [((0, cut), halo_a)], (weight,),
        dict(low=0, high=mid1, est_base=0, data_base=0, data_off=0, inv_off=0, make_data=True, tail=0, pay=True),
        [shape(tiles, cx, mid1, LANES), shape(tiles, wide, cut, LANES)] + pay_shapes(mid1),
    )
    halo_c = swap(pays)
    tail = mid1 - mid2
    est_b, data_b, *pays = iterate(
        "first_b", ext, [((0, cut), halo_a), ((cut, end0), halo_b)], (weight, est_a),
        dict(low=mid1, high=end1, est_base=0, data_base=data_at, data_off=0, inv_off=0, make_data=True, tail=tail, pay=True),
        [shape(tiles, cx, ceil_to(end1, 8) - mid2, LANES), shape(tiles, wide, full - data_at, LANES)] + pay_shapes(end1 - mid1),
    )
    halo_d = swap(pays)
    shift = 2 * reach
    (out_a,) = iterate(
        "second_a", est_a, [((0, mid1), halo_c)], (data_a,),
        dict(low=0, high=mid2, est_base=0, data_base=0, data_off=shift, inv_off=shift, make_data=False, tail=0, pay=False),
        [shape(tiles, cx, mid2, LANES)],
    )
    (out_b,) = iterate(
        "second_b", est_b, [((0, mid1), halo_c), ((mid1, end1), halo_d)], (data_b,),
        dict(low=mid2, high=end2, est_base=mid2, data_base=data_at, data_off=shift, inv_off=shift, make_data=False, tail=0, pay=False),
        [shape(tiles, cx, end2 - mid2, LANES)],
    )
    estimate = jnp.concatenate([out_a, out_b], axis=2)
    result = estimate.transpose(0, 3, 1, 2).reshape(tiles * LANES, cx, cy)
    return result[hz : hz + nz]


def solution(mesh):
    in_specs = (P("gz", "sx", "sy"), P("gz"), P(), P(), P(), P())
    out_specs = P("gz", "sx", "sy")
    return jax.shard_map(body, mesh=mesh, in_specs=in_specs, out_specs=out_specs, check_vma=False)
```

```python
import functools

import jax
import jax.numpy as jnp
from jax import lax
from jax.experimental import pallas as pl
from jax.experimental.pallas import tpu as pltpu
from jax.sharding import PartitionSpec as P

ITERS = 2
LANES = 128
TINY = 1e-30
VMEM = pl.BlockSpec(memory_space=pltpu.VMEM)


def ceil_to(value, unit):
    return -(-value // unit) * unit


def line(axis):
    count = lax.axis_size(axis)
    up = [(i, i + 1) for i in range(count - 1)]
    return up, [(j, i) for i, j in up]


def lane_is_low():
    return lax.broadcasted_iota(jnp.int32, (8, LANES), 1) < LANES // 2


def halo_row(ref, tiles, packed, hx, t, p, rows):
    if not packed or t < tiles - 1:
        return ref[hx * t + p, rows, :]
    half = hx // 2
    value = ref[hx * t + p % half, rows, :]
    if p >= half:
        value = pltpu.roll(value, LANES // 2, 1)
    return jnp.where(lane_is_low(), value, 0.0)


def pack_rows(src, pay, packed, hx, x0, blocks, src_block, pay_block):
    tiles = src.shape[0]

    def step(j, carry):
        here = pl.ds(pl.multiple_of(8 * (j + src_block), 8), 8)
        there = pl.ds(pl.multiple_of(8 * (j + pay_block), 8), 8)
        for t in range(tiles - 1 if packed else tiles):
            for p in range(hx):
                pay[hx * t + p, there, :] = src[t, x0 + p, here, :]
        if packed:
            half = hx // 2
            for p in range(half):
                other = pltpu.roll(src[tiles - 1, x0 + p + half, here, :], LANES // 2, 1)
                pay[hx * (tiles - 1) + p, there, :] = jnp.where(lane_is_low(), src[tiles - 1, x0 + p, here, :], other)
        return carry

    lax.fori_loop(0, blocks, step, 0)


def conv_rows(k, v, width):
    out = []
    for x in range(width):
        acc = k[0] * v[x]
        for a in range(1, len(k)):
            acc = acc + k[a] * v[x + a]
        out.append(acc)
    return out


def y_conv(src, taps, reverse, t, width, blocks, emit):
    count = taps.shape[1]
    k = [taps[t, count - 1 - b if reverse else b] for b in range(count)]

    def step(x, carry):
        for j in range(blocks):
            acc = k[0] * src[t, x, 8 * j : 8 * j + 8, :]
            for b in range(1, count):
                acc = acc + k[b] * src[t, x, 8 * j + b : 8 * j + b + 8, :]
            emit(t, x, j, acc)
        return carry

    lax.fori_loop(0, width, step, 0)


def windows_of(tiles):
    return [(0, tiles)] if tiles <= 2 else [(w, 2) for w in range(tiles - 1)]


def depth_rows(parts, hi_ref, lo_ref, shifted=False):
    split = []
    for part in parts:
        hi = part.astype(jnp.bfloat16)
        split.append((hi, (part - hi.astype(jnp.float32)).astype(jnp.bfloat16)))
    dot = functools.partial(jnp.dot, preferred_element_type=jnp.float32)
    out = {}
    for index, (first, span) in enumerate(windows_of(len(parts))):
        his = jnp.concatenate([split[first + s][0] for s in range(span)], axis=1)
        los = jnp.concatenate([split[first + s][1] for s in range(span)], axis=1)
        res = dot(his, hi_ref[index]) + (dot(los, hi_ref[index]) + dot(his, lo_ref[index]))
        for s in range(res.shape[1] // LANES):
            to = s if shifted else first + s
            piece = res[:, s * LANES : (s + 1) * LANES]
            out[to] = out[to] + piece if to in out else piece
    return [out[t] for t in range(len(out))]


def x_loop(taps, reverse, first, last, rows_in, rows_out):
    tiles, count = taps.shape[:2]

    def step(j, carry):
        for t in range(tiles):
            k = [taps[t, count - 1 - a if reverse else a] for a in range(count)]
            for n, v in enumerate(rows_in(t, j)):
                rows_out(t, j, n, conv_rows(k, v, len(v) - count + 1))
        return carry

    if first < last:
        lax.fori_loop(first, last, step, 0)


def y_pair(mid_ref, taps, t, i, blocks):
    count = taps.shape[1]
    k = [taps[t, b] for b in range(count)]
    out = []
    for x in (2 * i, 2 * i + 1):
        for j in range(blocks):
            acc = k[0] * mid_ref[t, x, 8 * j : 8 * j + 8, :]
            for b in range(1, count):
                acc = acc + k[b] * mid_ref[t, x, 8 * j + b : 8 * j + b + 8, :]
            out.append(acc)
    return jnp.concatenate(out, axis=0)


def correct(mid_ref, ty_ref, mats, shifted, pairs, rows, data_of, spread_ref, at=lambda i: 2 * i):
    fh_ref, fl_ref, bh_ref, bl_ref = mats
    tiles = mid_ref.shape[0]

    def depth(i, carry):
        blurred = depth_rows([y_pair(mid_ref, ty_ref, t, i, rows // 8) for t in range(tiles)], fh_ref, fl_ref)
        ratio = [data_of(t, i) / jnp.maximum(blurred[t], TINY) for t in range(tiles)]
        for t, value in enumerate(depth_rows(ratio, bh_ref, bl_ref, shifted)):
            spread_ref[t, pl.ds(2 * i, 2), 0:rows, :] = value.reshape(2, rows, LANES)
        return carry

    lax.fori_loop(0, pairs, depth, 0)


def inner_kernel(plan, est_ref, obs_ref, w_ref, tx_ref, ty_ref, fh_ref, fl_ref, bh_ref, bl_ref, spread_ref, mid_ref):
    tiles, cx = est_ref.shape[:2]
    reach = (tx_ref.shape[1] - 1) // 2
    rows = spread_ref.shape[2]
    first = plan["data_off"] + reach
    count = cx - 2 * reach

    def rows_in(t, j):
        here = pl.ds(pl.multiple_of(8 * j, 8), 8)
        return [[est_ref[t, x, here, :] for x in range(cx)]]

    def rows_out(t, j, n, values):
        here = pl.ds(pl.multiple_of(8 * j, 8), 8)
        for x, value in enumerate(values):
            mid_ref[t, x, here, :] = value

    x_loop(tx_ref, False, 0, -(-plan["need"] // 8), rows_in, rows_out)

    def data_of(t, i):
        seen = obs_ref[t, pl.ds(2 * i + reach, 2), first : first + rows, :]
        return (seen * w_ref[pl.ds(2 * i + 2 * reach, 2), first : first + rows, :]).reshape(2 * rows, LANES)

    correct(mid_ref, ty_ref, (fh_ref, fl_ref, bh_ref, bl_ref), plan["shifted"], count // 2, rows, data_of, spread_ref)


def norm_kernel(w_ref, tx_ref, ty_ref, out_ref, mid_ref):
    tiles, count = tx_ref.shape[:2]
    reach = (count - 1) // 2
    width = out_ref.shape[1]
    for t in range(tiles):
        k = [tx_ref[t, count - 1 - a] for a in range(count)]

        def step(j, carry, k=k):
            rows = pl.ds(pl.multiple_of(8 * j, 8), 8)
            v = [w_ref[x, rows, :] for x in range(width + count - 1)]
            for x, acc in enumerate(conv_rows(k, v, width)):
                mid_ref[0, x, rows, :] = acc
            return carry

        lax.fori_loop(0, mid_ref.shape[2] // 8, step, 0)
        ky = [ty_ref[t, count - 1 - b] for b in range(count)]

        def ystep(x, carry, ky=ky, t=t):
            for j in range(out_ref.shape[2] // 8):
                at = 8 * j + reach
                acc = ky[0] * mid_ref[0, x, at : at + 8, :]
                for b in range(1, count):
                    acc = acc + ky[b] * mid_ref[0, x, at + b : at + b + 8, :]
                out_ref[t, x, 8 * j : 8 * j + 8, :] = 1.0 / jnp.maximum(acc, TINY)
            return carry

        lax.fori_loop(0, width, ystep, 0)


def band_kernel(lane0, psf_ref, fh_ref, fl_ref, bh_ref, bl_ref, sh_ref, sl_ref):
    windows, size = fh_ref.shape[:2]
    taps = psf_ref.shape[0]
    total = psf_ref[0]
    for j in range(1, taps):
        total = total + psf_ref[j]
    step = LANES // 2
    for r in range(0, size, step):
        shape = (step, size)
        cols = lax.broadcasted_iota(jnp.int32, shape, 1)
        off = cols - lax.broadcasted_iota(jnp.int32, shape, 0) - r + (taps - 1) // 2
        band, flip = jnp.zeros(shape, jnp.float32), jnp.zeros(shape, jnp.float32)
        for j in range(taps):
            band = jnp.where(off == j, psf_ref[j], band)
            flip = jnp.where(off == taps - 1 - j, psf_ref[j], flip)
        for matrix, hi_ref, lo_ref in ((band, fh_ref, fl_ref), (flip, bh_ref, bl_ref)):
            matrix = matrix / jnp.full(shape, total, jnp.float32)
            for w in range(windows):
                first = 0 if w == 0 else LANES // 2
                last = size if w == windows - 1 else LANES + LANES // 2
                part = jnp.where((cols >= first) & (cols < last), matrix, 0.0)
                hi = part.astype(jnp.bfloat16)
                hi_ref[w, r : r + step, :] = hi
                lo_ref[w, r : r + step, :] = (part - hi.astype(jnp.float32)).astype(jnp.bfloat16)
        shape = (step, sh_ref.shape[2])
        for w in range(windows):
            ext = lax.broadcasted_iota(jnp.int32, shape, 0) + r + w * LANES
            off = ext - lax.broadcasted_iota(jnp.int32, shape, 1) - lane0 + (taps - 1) // 2
            part = jnp.zeros(shape, jnp.float32)
            first = 0 if w == 0 else LANES // 2
            last = size if w == windows - 1 else LANES + LANES // 2
            if first <= r < last:
                for j in range(taps):
                    part = jnp.where(off == j, psf_ref[j], part)
                part = part / jnp.full(shape, total, jnp.float32)
            hi = part.astype(jnp.bfloat16)
            sh_ref[w, r : r + step, :] = hi
            sl_ref[w, r : r + step, :] = (part - hi.astype(jnp.float32)).astype(jnp.bfloat16)


def edges_kernel(hy, after, vol_ref, low_ref, high_ref, *diags):
    tiles, cx, cy = vol_ref.shape[:3]
    for x in range(cx):
        to = slice(hy * x, hy * x + hy)
        for ref, rows, diag in ((low_ref, slice(cy - hy, cy), 0), (high_ref, slice(0, hy), 1)):
            for t in range(tiles):
                ref[t, to, :] = vol_ref[t, x, rows, :]
            if diags:
                lane = lax.broadcasted_iota(jnp.int32, (hy, LANES), 1)
                diags[diag][to, :] = jnp.where(lane < after, vol_ref[tiles - 1, x, rows, :], vol_ref[0, x, rows, :])


def assemble_kernel(packed, hx, cut, after, refs_in, *refs):
    vol_ref, low_ref, high_ref = refs[:3]
    halo_ref, low_z, high_z = refs[3:6] if refs_in == 6 else (None,) * 3
    ext_ref, *pays = refs[refs_in:]
    tiles, cx, cy = vol_ref.shape[:3]
    hy = low_ref.shape[1] // cx
    end = cy + 2 * hy

    def merge(t, value, halo, rows):
        if halo is None or 0 < t < tiles - 1:
            return value
        lane = lax.broadcasted_iota(jnp.int32, value.shape, 1)
        use = lane < after if t == 0 else (lane >= after) & (lane < 2 * after)
        return jnp.where(use, halo[rows], value)

    for t in range(tiles):
        for x in range(cx):
            edge = slice(hy * x, hy * x + hy)
            ext_ref[t, x, 0:hy, :] = merge(t, low_ref[t, edge, :], low_z, edge)
            ext_ref[t, x, hy : hy + cy, :] = merge(t, vol_ref[t, x], halo_ref, x)
            ext_ref[t, x, hy + cy : end, :] = merge(t, high_ref[t, edge, :], high_z, edge)
            ext_ref[t, x, end:, :] = jnp.zeros((ext_ref.shape[2] - end, LANES), jnp.float32)
    for n, (pay_up, pay_down) in enumerate((pays[:2], pays[2:])):
        first, last = (0, cut) if n == 0 else (cut, end)
        blocks = -(-(last - first) // 8)
        pack_rows(ext_ref, pay_up, packed, hx, cx - hx, blocks, first // 8, 0)
        pack_rows(ext_ref, pay_down, packed, hx, 0, blocks, first // 8, 0)


def outer_kernel(plan, *refs):
    refs = list(refs)
    take = refs.pop
    est_ref = take(0)
    halos = [(take(0), take(0), first, last) for first, last in plan["halos"]]
    make = plan["make_data"]
    w_ref = take(0) if make else None
    data_in = None if make else take(0)
    prior_ref = take(0) if plan["prior"] else None
    inner_ref, inv_ref, tx_ref, ty_ref, bx_ref, by_ref = [take(0) for _ in range(6)]
    mats = [take(0) for _ in range(4)]
    out_ref = take(0)
    data_ref = take(0) if make else data_in
    pays = [take(0), take(0)] if plan["pay"] else None
    mid_ref, edge_ref = refs
    packed, hx, low, high = plan["packed"], plan["hx"], plan["low"], plan["high"]
    data_base, off, lane0 = plan["data_base"], plan["data_off"], plan["lane0"]
    tiles, cx = est_ref.shape[:2]
    outs = out_ref.shape[0]
    count = tx_ref.shape[1]
    reach = (count - 1) // 2
    rows = edge_ref.shape[2]
    last_block = -(-(high + 4 * reach) // 8)
    data_first = data_base // 8 if make else low // 8

    for lo_ref, hi_ref, first, last in halos:

        def rows_in(t, j, lo_ref=lo_ref, hi_ref=hi_ref, first=first):
            here = pl.ds(pl.multiple_of(8 * j, 8), 8)
            there = pl.ds(pl.multiple_of(8 * j - first, 8), 8)
            one = [halo_row(lo_ref, tiles, packed, hx, t, p, there) for p in range(hx)]
            one += [est_ref[t, x, here, :] for x in range(hx)]
            two = [est_ref[t, x, here, :] for x in range(cx - hx, cx)]
            two += [halo_row(hi_ref, tiles, packed, hx, t, p, there) for p in range(hx)]
            return [one, two]

        def keep(t, j, pair):
            here = pl.ds(pl.multiple_of(8 * j, 8), 8)
            there = pl.ds(pl.multiple_of(8 * j - data_base, 8), 8)
            for n, v in enumerate(pair):
                for x in range(hx):
                    data_ref[t, hx * n + x, there, :] = w_ref[x + cx * n, here, :] * v[x + reach]

        def rows_in_keep(t, j, rows_in=rows_in, keep=keep):
            pair = rows_in(t, j)
            if make:
                keep(t, j, pair)
            return pair

        def rows_out(t, j, n, values):
            mid = pl.ds(pl.multiple_of(8 * j - low, 8), 8)
            for x, value in enumerate(values):
                mid_ref[t, hx * n + x, mid, :] = value

        def only_data(j, carry, rows_in=rows_in, keep=keep):
            for t in range(tiles):
                keep(t, j, rows_in(t, j))
            return carry

        a, b = max(first // 8, data_first), min(last // 8, low // 8)
        if make and a < b:
            lax.fori_loop(a, b, only_data, 0)
        x_loop(tx_ref, False, max(first // 8, low // 8), min(-(-last // 8), last_block), rows_in_keep, rows_out)

    spot0 = low + off + reach - data_base

    def data_of(t, i):
        return data_ref[t, pl.ds(2 * i, 2), spot0 : spot0 + rows, :].reshape(2 * rows, LANES)

    correct(mid_ref, ty_ref, mats, plan["shifted"], hx, rows, data_of, edge_ref)

    blocks = -(-(high - low) // 8)

    def back_in(t, j):
        here = pl.ds(pl.multiple_of(8 * j, 8), 8)
        there = pl.ds(pl.multiple_of(8 * j + low, 8), 8)
        v = [edge_ref[t, x, here, :] for x in range(hx)]
        v += [inner_ref[t, x, there, :] for x in range(cx - 2 * reach)]
        return [v + [edge_ref[t, x, here, :] for x in range(hx, 2 * hx)]]

    def back_out(t, j, n, values):
        here = pl.ds(pl.multiple_of(8 * j, 8), 8)
        for x, value in enumerate(values):
            mid_ref[t, x, here, :] = value

    x_loop(bx_ref, True, 0, rows // 8, back_in, back_out)
    base = low if prior_ref is not None else 0

    def finish(t, x, j, acc):
        at = 8 * j + low + 2 * reach
        scale = 8 * j + low + off
        old = est_ref[t, x, at : at + 8, :] * inv_ref[t, x, scale : scale + 8, :]
        if lane0:
            if t + 1 < tiles:
                more = est_ref[t + 1, x, at : at + 8, :] * inv_ref[t + 1, x, scale : scale + 8, :]
                lane = lax.broadcasted_iota(jnp.int32, (8, LANES), 1)
                old = jnp.where(lane >= lane0, old, more)
            old = pltpu.roll(old, LANES - lane0, 1)
        to = 8 * j + base
        out_ref[t, x, to : to + 8, :] = old * acc

    for t in range(outs):
        y_conv(mid_ref, by_ref, True, t, cx, blocks, finish)

    if prior_ref is not None:
        for t in range(outs):

            def copy(x, carry, t=t):
                out_ref[t, x, 0:low, :] = prior_ref[t, x, 0:low, :]
                return carry

            lax.fori_loop(0, cx, copy, 0)
    if pays:
        pack_rows(out_ref, pays[0], packed, hx, cx - hx, blocks, base // 8, 0)
        pack_rows(out_ref, pays[1], packed, hx, 0, blocks, base // 8, 0)


def body(observed, zone_of_slice, lateral_x, lateral_y, depth_psf, stitch_width):
    nz, cx, cy = observed.shape
    taps = lateral_x.shape[1]
    reach = (taps - 1) // 2
    zreach = (depth_psf.shape[0] - 1) // 2
    hz = 2 * zreach * ITERS
    hy = 2 * reach * ITERS
    hx = 2 * reach
    slabs = lax.axis_size("gz")
    tiles = ceil_to(nz + 2 * hz, LANES) // LANES
    f32 = jnp.float32

    zones = zone_of_slice.astype(f32)

    def with_zones(part, ids):
        flat = jnp.pad(ids, (0, cx * cy - ids.shape[0]))
        return jnp.concatenate([part, flat.reshape(1, cx, cy)], axis=0)

    if slabs == 2:
        both = jnp.concatenate([observed[nz - hz :], observed[:hz]], axis=0)
        got = lax.ppermute(with_zones(both, jnp.concatenate([zones[nz - hz :], zones[:hz]])), "gz", [(0, 1), (1, 0)])
        before, after = got[:hz], got[hz : 2 * hz]
        got_ids = got[2 * hz].reshape(-1)
        ids_before, ids_after = got_ids[:hz], got_ids[hz : 2 * hz]
    else:
        up = [(i, (i + 1) % slabs) for i in range(slabs)]
        first = lax.ppermute(with_zones(observed[nz - hz :], zones[nz - hz :]), "gz", up)
        second = lax.ppermute(with_zones(observed[:hz], zones[:hz]), "gz", [(j, i) for i, j in up])
        before, after = first[:hz], second[:hz]
        ids_before, ids_after = first[hz].reshape(-1)[:hz], second[hz].reshape(-1)[:hz]
    pad = tiles * LANES - nz - 2 * hz
    ids = jnp.concatenate([ids_before, zones, ids_after, jnp.full((pad,), -1.0, f32)])
    direct = slabs == 2 and nz % LANES == 0 and 2 * hz <= LANES
    if direct:
        volume = jnp.pad(observed, ((hz, hz + pad), (0, 0), (0, 0)))
        halo = jnp.pad(got[: 2 * hz], ((0, LANES - 2 * hz), (0, 0), (0, 0))).transpose(1, 2, 0)
    else:
        volume = jnp.concatenate([before, observed, after, jnp.zeros((pad, cx, cy), f32)], axis=0)
    volume = volume.reshape(tiles, LANES, cx, cy).transpose(0, 2, 3, 1)

    def lanes_of(kernels, names):
        match = (names[None, :] == jnp.arange(lateral_x.shape[0], dtype=f32)[:, None]).astype(f32)
        table = jnp.sum(match[:, None, :] * kernels[:, :, None], axis=0)
        table = table.reshape(taps, -1, 1, LANES).transpose(1, 0, 2, 3)
        return jnp.broadcast_to(table, (table.shape[0], taps, 8, LANES))

    tx, ty = lanes_of(lateral_x, ids), lanes_of(lateral_y, ids)
    own = ceil_to(nz, LANES) // LANES
    own_ids = jnp.concatenate([zones, jnp.full((own * LANES - nz,), -1.0, f32)])
    tx_own, ty_own = lanes_of(lateral_x, own_ids), lanes_of(lateral_y, own_ids)

    sx, sy = lax.axis_index("sx"), lax.axis_index("sy")
    stacks_x, stacks_y = stitch_width.shape[:2]
    full = ceil_to(cy + 2 * hy + reach, 8)
    gx = sx * cx - reach + jnp.arange(cx + 2 * reach)
    gy = sy * cy - hy + jnp.arange(full)
    near = lax.dynamic_slice(jnp.pad(stitch_width, ((1, 1), (1, 1), (0, 0))), (sx, sy, jnp.int32(0)), (3, 3, 2))
    of_x = gx // cx - sx + 1
    of_y = gy // cy - sy + 1
    bands = jnp.zeros((2, gx.shape[0], full), jnp.int32)
    for a in range(3):
        for b in range(3):
            hit = (of_x[:, None] == a) & (of_y[None, :] == b)
            bands = jnp.where(hit[None], near[a, b][:, None, None], bands)
    inside = ((gx >= 0) & (gx < stacks_x * cx))[:, None] & ((gy >= 0) & (gy < stacks_y * cy))[None, :]
    weight = jnp.where((gx % cx)[:, None] < bands[0], 0.5, 1.0) * jnp.where((gy % cy)[None, :] < bands[1], 0.5, 1.0)
    weight = jnp.where(inside, weight, 0.0).astype(f32)
    weight = jnp.broadcast_to(weight[:, :, None], (cx + 2 * reach, full, LANES))

    wide = cx + 2 * reach
    packed = nz + 2 * hz - (tiles - 1) * LANES <= LANES // 2
    planes = hx * (tiles - 1) + hx // 2 if packed else hx * tiles
    end0, end1, end2 = cy + 2 * hy, cy + 2 * hy - 4 * reach, cy
    mid1 = ceil_to(end1 // 2, 8) + 8
    mid2 = mid1 - ceil_to(4 * reach, 8)
    cut = ceil_to(mid1 + 4 * reach, 8)
    up, down = line("sx")

    def shape(*dims):
        return jax.ShapeDtypeStruct(dims, f32)

    def pay_shapes(rows):
        return [shape(planes, ceil_to(rows, 8), LANES)] * 2

    def swap(pays):
        return lax.ppermute(pays[0], "sx", up), lax.ppermute(pays[1], "sx", down)

    def call(kernel, out_shape, args, scratch, name, limit, flops, specs=VMEM):
        moved = sum(a.size * 4 for a in args) + sum(o.size * 4 for o in out_shape)
        return pl.pallas_call(
            kernel,
            out_shape=out_shape,
            in_specs=[specs] * len(args),
            out_specs=[VMEM] * len(out_shape),
            scratch_shapes=[pltpu.VMEM(dims, f32) for dims in scratch],
            compiler_params=pltpu.CompilerParams(vmem_limit_bytes=limit << 20),
            cost_estimate=pl.CostEstimate(flops=flops, bytes_accessed=moved, transcendentals=0),
            name=name,
        )(*args)

    wins = windows_of(tiles)
    size = wins[0][1] * LANES
    fh, fl, bh, bl, sh, sl = call(
        functools.partial(band_kernel, hz),
        [jax.ShapeDtypeStruct((len(wins), size, size), jnp.bfloat16)] * 4
        + [jax.ShapeDtypeStruct((len(wins), size, own * LANES), jnp.bfloat16)] * 2,
        (depth_psf,), [], "band", 8, 1,
        specs=pl.BlockSpec(memory_space=pltpu.SMEM),
    )

    stacks = lax.axis_size("sy")
    edge = shape(tiles, cx * hy, LANES)
    diag = [shape(cx * hy, LANES)] * 2 if direct else []
    low, high, *corner = call(functools.partial(edges_kernel, hy, hz), [edge, edge] + diag, (volume,), [], "edges", 8, 1)
    yup, ydown = line("sy")
    parts = [volume, lax.ppermute(low, "sy", yup), lax.ppermute(high, "sy", ydown)]
    if direct:
        cross = [(2 * i + g, 2 * i + 2 + (1 - g)) for i in range(stacks - 1) for g in range(2)]
        parts.append(halo)
        parts.append(lax.ppermute(corner[0], ("sy", "gz"), cross))
        parts.append(lax.ppermute(corner[1], ("sy", "gz"), [(j, i) for i, j in cross]))

    ext, *pays = call(
        functools.partial(assemble_kernel, packed, hx, cut, hz, len(parts)),
        [shape(tiles, cx, full, LANES)] + pay_shapes(cut) + pay_shapes(end0 - cut),
        tuple(parts), [], "assemble", 8, 1,
    )
    halo_a = swap(pays[:2])
    halo_b = swap(pays[2:])
    (inv,) = call(
        norm_kernel, [shape(tiles, cx, ceil_to(end1, 8), LANES)], (weight, tx, ty),
        [(1, cx, full, LANES)], "norm", 8, 1,
    )
    shift = 2 * reach

    def inner(name, est, data_off, shifted, rows, need, back):
        plan = dict(data_off=data_off, shifted=shifted, need=need)
        args = (est, ext, weight, tx, ty, fh, fl) + back
        rows = ceil_to(rows, 8)
        return call(
            functools.partial(inner_kernel, plan),
            [shape(own if shifted else tiles, cx - shift, rows, LANES)], args,
            [(tiles, cx - shift, rows + 16, LANES)], name, 24, 1,
        )[0]

    def outer(name, est, halos, extra, inner_part, last, plan, outs):
        rows = ceil_to(plan["high"] - plan["low"] + 2 * reach, 8)
        back, lateral = ((sh, sl), (tx_own, ty_own)) if last else ((bh, bl), (tx, ty))
        args = (est,) + tuple(h for _, pair in halos for h in pair) + extra
        args += (inner_part, inv, tx, ty) + lateral + (fh, fl) + back
        plan = dict(
            plan, hx=hx, packed=packed, halos=[rng for rng, _ in halos], make_data=not last, pay=not last,
            shifted=last, data_off=shift if last else 0, lane0=hz if last else 0,
        )
        scratch = [(tiles, cx, rows + 16, LANES), (own if last else tiles, 2 * hx, rows, LANES)]
        return call(functools.partial(outer_kernel, plan), outs, args, scratch, name, 16, 1)

    data_at = mid2 + 8
    spread1 = inner("inner_1", ext, 0, False, end1 + shift, end0, (bh, bl))
    est_a, data_a, *pays = outer(
        "outer_1a", ext, [((0, cut), halo_a)], (weight,), spread1, False,
        dict(low=0, high=mid1, data_base=0, prior=False),
        [shape(tiles, cx, mid1, LANES), shape(tiles, 2 * hx, cut, LANES)] + pay_shapes(mid1),
    )
    halo_c = swap(pays)
    est, data_b, *pays = outer(
        "outer_1b", ext, [((0, cut), halo_a), ((cut, end0), halo_b)], (weight, est_a), spread1, False,
        dict(low=mid1, high=end1, data_base=data_at, prior=True),
        [shape(tiles, cx, ceil_to(end1, 8), LANES), shape(tiles, 2 * hx, full - data_at, LANES)] + pay_shapes(end1 - mid1),
    )
    halo_d = swap(pays)
    spread2 = inner("inner_2", est, shift, True, end2 + shift, end1, (sh, sl))
    (out_a,) = outer(
        "outer_2a", est, [((0, mid1), halo_c)], (data_a,), spread2, True,
        dict(low=0, high=mid2, data_base=0, prior=False), [shape(own, cx, mid2, LANES)],
    )
    (out_b,) = outer(
        "outer_2b", est, [((0, mid1), halo_c), ((mid1, end1), halo_d)], (data_b,), spread2, True,
        dict(low=mid2, high=end2, data_base=data_at, prior=False), [shape(own, cx, end2 - mid2, LANES)],
    )
    estimate = jnp.concatenate([out_a, out_b], axis=2)
    return estimate.transpose(0, 3, 1, 2).reshape(own * LANES, cx, cy)[:nz]


def solution(mesh):
    in_specs = (P("gz", "sx", "sy"), P("gz"), P(), P(), P(), P())
    out_specs = P("gz", "sx", "sy")
    return jax.shard_map(body, mesh=mesh, in_specs=in_specs, out_specs=out_specs, check_vma=False)
```

```python
import functools

import jax
import jax.numpy as jnp
from jax import lax
from jax.experimental import pallas as pl
from jax.experimental.pallas import tpu as pltpu
from jax.sharding import PartitionSpec as P

ITERS = 2
LANES = 128
TINY = 1e-30
VMEM = pl.BlockSpec(memory_space=pltpu.VMEM)


def ceil_to(value, unit):
    return -(-value // unit) * unit


def swaps(count):
    return [[(i, i + 1) for i in range(first, count - 1, 2)] for first in (0, 1)]


def both_ways(pairs):
    return pairs + [(j, i) for i, j in pairs]


def lane_is_low():
    return lax.broadcasted_iota(jnp.int32, (8, LANES), 1) < LANES // 2


def halo_row(ref, tiles, packed, hx, t, p, rows):
    if not packed or t < tiles - 1:
        return ref[hx * t + p, rows, :]
    half = hx // 2
    value = ref[hx * t + p % half, rows, :]
    if p >= half:
        value = pltpu.roll(value, LANES // 2, 1)
    return jnp.where(lane_is_low(), value, 0.0)


def pack_both(src, pays, odd, packed, hx, blocks, src_block):
    high = src.shape[1] - hx
    pack_rows(src, pays[0], packed, hx, jnp.where(odd == 1, 0, high), blocks, src_block, 0)
    pack_rows(src, pays[1], packed, hx, jnp.where(odd == 1, high, 0), blocks, src_block, 0)


def by_side(odd, first, second):
    return jnp.where(odd == 1, first, second), jnp.where(odd == 1, second, first)


def pack_rows(src, pay, packed, hx, x0, blocks, src_block, pay_block):
    tiles = src.shape[0]

    def step(j, carry):
        here = pl.ds(pl.multiple_of(8 * (j + src_block), 8), 8)
        there = pl.ds(pl.multiple_of(8 * (j + pay_block), 8), 8)
        for t in range(tiles - 1 if packed else tiles):
            for p in range(hx):
                pay[hx * t + p, there, :] = src[t, x0 + p, here, :]
        if packed:
            half = hx // 2
            for p in range(half):
                other = pltpu.roll(src[tiles - 1, x0 + p + half, here, :], LANES // 2, 1)
                pay[hx * (tiles - 1) + p, there, :] = jnp.where(lane_is_low(), src[tiles - 1, x0 + p, here, :], other)
        return carry

    lax.fori_loop(0, blocks, step, 0)


def conv_rows(k, v, width):
    out = []
    for x in range(width):
        acc = k[0] * v[x]
        for a in range(1, len(k)):
            acc = acc + k[a] * v[x + a]
        out.append(acc)
    return out


def y_conv(src, taps, reverse, t, width, blocks, emit):
    count = taps.shape[1]
    k = [taps[t, count - 1 - b if reverse else b] for b in range(count)]

    def step(x, carry):
        for j in range(blocks):
            acc = k[0] * src[t, x, 8 * j : 8 * j + 8, :]
            for b in range(1, count):
                acc = acc + k[b] * src[t, x, 8 * j + b : 8 * j + b + 8, :]
            emit(t, x, j, acc)
        return carry

    lax.fori_loop(0, width, step, 0)


def windows_of(tiles):
    return [(0, tiles)] if tiles <= 2 else [(w, 2) for w in range(tiles - 1)]


def depth_rows(parts, hi_ref, lo_ref, shifted=False):
    split = []
    for part in parts:
        hi = part.astype(jnp.bfloat16)
        split.append((hi, (part - hi.astype(jnp.float32)).astype(jnp.bfloat16)))
    dot = functools.partial(jnp.dot, preferred_element_type=jnp.float32)
    out = {}
    for index, (first, span) in enumerate(windows_of(len(parts))):
        his = jnp.concatenate([split[first + s][0] for s in range(span)], axis=1)
        los = jnp.concatenate([split[first + s][1] for s in range(span)], axis=1)
        res = dot(his, hi_ref[index]) + (dot(los, hi_ref[index]) + dot(his, lo_ref[index]))
        for s in range(res.shape[1] // LANES):
            to = s if shifted else first + s
            piece = res[:, s * LANES : (s + 1) * LANES]
            out[to] = out[to] + piece if to in out else piece
    return [out[t] for t in range(len(out))]


def x_loop(taps, reverse, first, last, rows_in, rows_out):
    tiles, count = taps.shape[:2]

    def step(j, carry):
        for t in range(tiles):
            k = [taps[t, count - 1 - a if reverse else a] for a in range(count)]
            for n, v in enumerate(rows_in(t, j)):
                rows_out(t, j, n, conv_rows(k, v, len(v) - count + 1))
        return carry

    if first < last:
        lax.fori_loop(first, last, step, 0)


def y_pair(mid_ref, taps, t, i, blocks):
    count = taps.shape[1]
    k = [taps[t, b] for b in range(count)]
    out = []
    for x in (2 * i, 2 * i + 1):
        for j in range(blocks):
            acc = k[0] * mid_ref[t, x, 8 * j : 8 * j + 8, :]
            for b in range(1, count):
                acc = acc + k[b] * mid_ref[t, x, 8 * j + b : 8 * j + b + 8, :]
            out.append(acc)
    return jnp.concatenate(out, axis=0)


def correct(mid_ref, ty_ref, mats, shifted, pairs, rows, data_of, spread_ref, at=lambda i: 2 * i):
    fh_ref, fl_ref, bh_ref, bl_ref = mats
    tiles = mid_ref.shape[0]

    def depth(i, carry):
        blurred = depth_rows([y_pair(mid_ref, ty_ref, t, i, rows // 8) for t in range(tiles)], fh_ref, fl_ref)
        ratio = [data_of(t, i) / jnp.maximum(blurred[t], TINY) for t in range(tiles)]
        for t, value in enumerate(depth_rows(ratio, bh_ref, bl_ref, shifted)):
            spread_ref[t, pl.ds(2 * i, 2), 0:rows, :] = value.reshape(2, rows, LANES)
        return carry

    lax.fori_loop(0, pairs, depth, 0)


def inner_kernel(plan, est_ref, obs_ref, w_ref, tx_ref, ty_ref, fh_ref, fl_ref, bh_ref, bl_ref, spread_ref, mid_ref):
    tiles, cx = est_ref.shape[:2]
    reach = (tx_ref.shape[1] - 1) // 2
    rows = spread_ref.shape[2]
    first = plan["data_off"] + reach
    count = cx - 2 * reach

    def rows_in(t, j):
        here = pl.ds(pl.multiple_of(8 * j, 8), 8)
        return [[est_ref[t, x, here, :] for x in range(cx)]]

    def rows_out(t, j, n, values):
        here = pl.ds(pl.multiple_of(8 * j, 8), 8)
        for x, value in enumerate(values):
            mid_ref[t, x, here, :] = value

    x_loop(tx_ref, False, 0, -(-plan["need"] // 8), rows_in, rows_out)

    def data_of(t, i):
        seen = obs_ref[t, pl.ds(2 * i + reach, 2), first : first + rows, :]
        return (seen * w_ref[pl.ds(2 * i + 2 * reach, 2), first : first + rows, :]).reshape(2 * rows, LANES)

    correct(mid_ref, ty_ref, (fh_ref, fl_ref, bh_ref, bl_ref), plan["shifted"], count // 2, rows, data_of, spread_ref)


def norm_kernel(plan, place_ref, bands_ref, _, tx_ref, ty_ref, w_ref, out_ref, mid_ref):
    cx, cy, hy, stacks_x, stacks_y = plan
    tiles, count = tx_ref.shape[:2]
    reach = (count - 1) // 2
    width = out_ref.shape[1]
    full = w_ref.shape[1]
    sx, sy = place_ref[0], place_ref[1]
    row = lax.broadcasted_iota(jnp.int32, (full, LANES), 0)
    for x in range(cx + 2 * reach):
        a = (x - reach) // cx
        px = (x - reach) % cx
        gx = sx + a
        value = jnp.zeros((full, LANES), jnp.float32)
        for b, first in ((-1, 0), (0, hy), (1, hy + cy)):
            gy = sy + b
            inside = (gx >= 0) & (gx < stacks_x) & (gy >= 0) & (gy < stacks_y)
            spot = 2 * (jnp.clip(gx, 0, stacks_x - 1) * stacks_y + jnp.clip(gy, 0, stacks_y - 1))
            along = jnp.where(inside, jnp.where(px < bands_ref[spot], 0.5, 1.0), 0.0)
            across = jnp.where(row - hy - b * cy < bands_ref[spot + 1], 0.5, 1.0)
            value = jnp.where(row >= first, across * along, value)
        w_ref[x] = value

    def rows_in(t, j):
        rows = pl.ds(pl.multiple_of(8 * j, 8), 8)
        return [[w_ref[x, rows, :] for x in range(width + count - 1)]]

    def rows_out(t, j, n, values):
        rows = pl.ds(pl.multiple_of(8 * j, 8), 8)
        for x, value in enumerate(values):
            mid_ref[t, x, rows, :] = value

    x_loop(tx_ref, True, 0, full // 8, rows_in, rows_out)
    for t in range(tiles):
        ky = [ty_ref[t, count - 1 - b] for b in range(count)]

        def ystep(x, carry, ky=ky, t=t):
            for j in range(out_ref.shape[2] // 8):
                at = 8 * j + reach
                acc = ky[0] * mid_ref[t, x, at : at + 8, :]
                for b in range(1, count):
                    acc = acc + ky[b] * mid_ref[t, x, at + b : at + b + 8, :]
                out_ref[t, x, 8 * j : 8 * j + 8, :] = 1.0 / jnp.maximum(acc, TINY)
            return carry

        lax.fori_loop(0, width, ystep, 0)


def band_kernel(lane0, psf_ref, _, fh_ref, fl_ref, bh_ref, bl_ref, sh_ref, sl_ref):
    windows, size = fh_ref.shape[:2]
    taps = psf_ref.shape[0]
    total = psf_ref[0]
    for j in range(1, taps):
        total = total + psf_ref[j]
    step = LANES // 2
    for r in range(0, size, step):
        shape = (step, size)
        cols = lax.broadcasted_iota(jnp.int32, shape, 1)
        off = cols - lax.broadcasted_iota(jnp.int32, shape, 0) - r + (taps - 1) // 2
        band, flip = jnp.zeros(shape, jnp.float32), jnp.zeros(shape, jnp.float32)
        for j in range(taps):
            band = jnp.where(off == j, psf_ref[j], band)
            flip = jnp.where(off == taps - 1 - j, psf_ref[j], flip)
        for matrix, hi_ref, lo_ref in ((band, fh_ref, fl_ref), (flip, bh_ref, bl_ref)):
            matrix = matrix / jnp.full(shape, total, jnp.float32)
            for w in range(windows):
                first = 0 if w == 0 else LANES // 2
                last = size if w == windows - 1 else LANES + LANES // 2
                part = jnp.where((cols >= first) & (cols < last), matrix, 0.0)
                hi = part.astype(jnp.bfloat16)
                hi_ref[w, r : r + step, :] = hi
                lo_ref[w, r : r + step, :] = (part - hi.astype(jnp.float32)).astype(jnp.bfloat16)
        shape = (step, sh_ref.shape[2])
        for w in range(windows):
            ext = lax.broadcasted_iota(jnp.int32, shape, 0) + r + w * LANES
            off = ext - lax.broadcasted_iota(jnp.int32, shape, 1) - lane0 + (taps - 1) // 2
            part = jnp.zeros(shape, jnp.float32)
            first = 0 if w == 0 else LANES // 2
            last = size if w == windows - 1 else LANES + LANES // 2
            if first <= r < last:
                for j in range(taps):
                    part = jnp.where(off == j, psf_ref[j], part)
                part = part / jnp.full(shape, total, jnp.float32)
            hi = part.astype(jnp.bfloat16)
            sh_ref[w, r : r + step, :] = hi
            sl_ref[w, r : r + step, :] = (part - hi.astype(jnp.float32)).astype(jnp.bfloat16)


def turned(shift, main, halo):
    if halo is None:
        return main
    lane = lax.broadcasted_iota(jnp.int32, main[0].shape, 1)
    moved = [pltpu.roll(m, shift, 1) for m in main]
    out = [jnp.where(lane < shift, halo, moved[0])]
    out += [jnp.where(lane < shift, moved[t - 1], moved[t]) for t in range(1, len(main))]
    tail = jnp.where(lane < shift, moved[-1], jnp.where(lane < 2 * shift, halo, 0.0))
    return out + [tail]


def edges_kernel(hy, shift, place_ref, vol_ref, *refs):
    tiles, cx, cy = vol_ref.shape[:3]
    odd = place_ref[1] % 2
    direct = len(refs) > 2
    if direct:
        zones_ref, first_ref, second_ref, first_z, second_z, depth_ref = refs
        lane = lax.broadcasted_iota(jnp.int32, (cy, LANES), 1)
        half = cx // 2

        def outmost(x):
            return pltpu.roll(jnp.where(lane < LANES // 2, vol_ref[0, x], vol_ref[tiles - 1, x]), shift, 1)

        for x in range(half):
            other = pltpu.roll(outmost(x + half), LANES // 2, 1)
            depth_ref[cy * x : cy * x + cy, :] = jnp.where(lane < LANES // 2, outmost(x), other)
        depth_ref[cy * half :, :] = zones_ref[...]
    else:
        first_ref, second_ref = refs
    lane = lax.broadcasted_iota(jnp.int32, (hy, LANES), 1)
    for x in range(cx):
        to = slice(hy * x, hy * x + hy)
        both = []
        for t in range(tiles):
            low, high = vol_ref[t, x, 0:hy, :], vol_ref[t, x, cy - hy : cy, :]
            both.append((jnp.where(odd == 1, low, high), jnp.where(odd == 1, high, low)))
            first_ref[t, to, :], second_ref[t, to, :] = both[-1]
        if direct:
            for n, ref in enumerate((first_z, second_z)):
                ref[to, :] = pltpu.roll(jnp.where(lane < LANES // 2, both[0][n], both[-1][n]), shift, 1)


def assemble_kernel(packed, hx, cut, shift, refs_in, place_ref, *refs):
    vol_ref, first_ref, second_ref = refs[:3]
    depth_ref, first_z, second_z = refs[3:6] if refs_in == 6 else (None,) * 3
    ext_ref, *pays = refs[refs_in:]
    main, cx, cy = vol_ref.shape[:3]
    hy = first_ref.shape[1] // cx
    end = cy + 2 * hy
    odd = place_ref[1] % 2
    half = cx // 2

    for x in range(cx):
        edge = slice(hy * x, hy * x + hy)
        low, high = zip(*[by_side(odd, first_ref[t, edge, :], second_ref[t, edge, :]) for t in range(main)])
        low_z = high_z = halo = None
        if depth_ref is not None:
            low_z, high_z = by_side(odd, first_z[edge, :], second_z[edge, :])
            halo = depth_ref[cy * (x % half) : cy * (x % half) + cy, :]
            halo = pltpu.roll(halo, LANES // 2, 1) if x >= half else halo
        low = turned(shift, low, low_z)
        mids = turned(shift, [vol_ref[t, x] for t in range(main)], halo)
        high = turned(shift, high, high_z)
        for t in range(ext_ref.shape[0]):
            ext_ref[t, x, 0:hy, :] = low[t]
            ext_ref[t, x, hy : hy + cy, :] = mids[t]
            ext_ref[t, x, hy + cy : end, :] = high[t]
            ext_ref[t, x, end:, :] = jnp.zeros((ext_ref.shape[2] - end, LANES), jnp.float32)
    odd_x = place_ref[0] % 2
    for n in range(2):
        start, stop = (0, cut) if n == 0 else (cut, end)
        pack_both(ext_ref, pays[2 * n : 2 * n + 2], odd_x, packed, hx, -(-(stop - start) // 8), start // 8)


def outer_kernel(plan, place_ref, *refs):
    refs = list(refs)
    odd = place_ref[0] % 2
    take = refs.pop
    est_ref = take(0)
    halos = [(take(0), take(0), first, last) for first, last in plan["halos"]]
    make = plan["make_data"]
    w_ref = take(0) if make else None
    data_in = None if make else take(0)
    prior_ref = take(0) if plan["prior"] else None
    inner_ref, inv_ref, tx_ref, ty_ref, bx_ref, by_ref = [take(0) for _ in range(6)]
    mats = [take(0) for _ in range(4)]
    out_ref = take(0)
    data_ref = take(0) if make else data_in
    pays = [take(0), take(0)] if plan["pay"] else None
    mid_ref, edge_ref = refs
    packed, hx, low, high = plan["packed"], plan["hx"], plan["low"], plan["high"]
    data_base, off, lane0 = plan["data_base"], plan["data_off"], plan["lane0"]
    tiles, cx = est_ref.shape[:2]
    outs = out_ref.shape[0]
    count = tx_ref.shape[1]
    reach = (count - 1) // 2
    rows = edge_ref.shape[2]
    last_block = -(-(high + 4 * reach) // 8)
    data_first = data_base // 8 if make else low // 8

    for lo_ref, hi_ref, first, last in halos:

        def rows_in(t, j, lo_ref=lo_ref, hi_ref=hi_ref, first=first):
            here = pl.ds(pl.multiple_of(8 * j, 8), 8)
            there = pl.ds(pl.multiple_of(8 * j - first, 8), 8)
            lows, highs = [], []
            for p in range(hx):
                came = [halo_row(ref, tiles, packed, hx, t, p, there) for ref in (lo_ref, hi_ref)]
                low_row, high_row = by_side(odd, *came)
                lows.append(low_row)
                highs.append(high_row)
            one = lows + [est_ref[t, x, here, :] for x in range(hx)]
            return [one, [est_ref[t, x, here, :] for x in range(cx - hx, cx)] + highs]

        def keep(t, j, pair):
            here = pl.ds(pl.multiple_of(8 * j, 8), 8)
            there = pl.ds(pl.multiple_of(8 * j - data_base, 8), 8)
            for n, v in enumerate(pair):
                for x in range(hx):
                    data_ref[t, hx * n + x, there, :] = w_ref[x + cx * n, here, :] * v[x + reach]

        def rows_in_keep(t, j, rows_in=rows_in, keep=keep):
            pair = rows_in(t, j)
            if make:
                keep(t, j, pair)
            return pair

        def rows_out(t, j, n, values):
            mid = pl.ds(pl.multiple_of(8 * j - low, 8), 8)
            for x, value in enumerate(values):
                mid_ref[t, hx * n + x, mid, :] = value

        def only_data(j, carry, rows_in=rows_in, keep=keep):
            for t in range(tiles):
                keep(t, j, rows_in(t, j))
            return carry

        a, b = max(first // 8, data_first), min(last // 8, low // 8)
        if make and a < b:
            lax.fori_loop(a, b, only_data, 0)
        x_loop(tx_ref, False, max(first // 8, low // 8), min(-(-last // 8), last_block), rows_in_keep, rows_out)

    spot0 = low + off + reach - data_base

    def data_of(t, i):
        return data_ref[t, pl.ds(2 * i, 2), spot0 : spot0 + rows, :].reshape(2 * rows, LANES)

    correct(mid_ref, ty_ref, mats, plan["shifted"], hx, rows, data_of, edge_ref)

    blocks = -(-(high - low) // 8)

    def back_in(t, j):
        here = pl.ds(pl.multiple_of(8 * j, 8), 8)
        there = pl.ds(pl.multiple_of(8 * j + low, 8), 8)
        v = [edge_ref[t, x, here, :] for x in range(hx)]
        v += [inner_ref[t, x, there, :] for x in range(cx - 2 * reach)]
        return [v + [edge_ref[t, x, here, :] for x in range(hx, 2 * hx)]]

    def back_out(t, j, n, values):
        here = pl.ds(pl.multiple_of(8 * j, 8), 8)
        for x, value in enumerate(values):
            mid_ref[t, x, here, :] = value

    x_loop(bx_ref, True, 0, rows // 8, back_in, back_out)
    base = low if prior_ref is not None else 0

    def finish(t, x, j, acc):
        at = 8 * j + low + 2 * reach
        scale = 8 * j + low + off
        old = est_ref[t, x, at : at + 8, :] * inv_ref[t, x, scale : scale + 8, :]
        if lane0:
            if t + 1 < tiles:
                more = est_ref[t + 1, x, at : at + 8, :] * inv_ref[t + 1, x, scale : scale + 8, :]
                lane = lax.broadcasted_iota(jnp.int32, (8, LANES), 1)
                old = jnp.where(lane >= lane0, old, more)
            old = pltpu.roll(old, LANES - lane0, 1)
        to = 8 * j + base
        out_ref[t, x, to : to + 8, :] = old * acc

    for t in range(outs):
        y_conv(mid_ref, by_ref, True, t, cx, blocks, finish)

    if prior_ref is not None:
        for t in range(outs):

            def copy(x, carry, t=t):
                out_ref[t, x, 0:low, :] = prior_ref[t, x, 0:low, :]
                return carry

            lax.fori_loop(0, cx, copy, 0)
    if pays:
        pack_both(out_ref, pays, odd, packed, hx, blocks, base // 8)


def body(observed, zone_of_slice, lateral_x, lateral_y, depth_psf, stitch_width):
    nz, cx, cy = observed.shape
    taps = lateral_x.shape[1]
    reach = (taps - 1) // 2
    zreach = (depth_psf.shape[0] - 1) // 2
    hz = 2 * zreach * ITERS
    hy = 2 * reach * ITERS
    hx = 2 * reach
    slabs = lax.axis_size("gz")
    tiles = ceil_to(nz + 2 * hz, LANES) // LANES
    f32 = jnp.float32

    zones = zone_of_slice.astype(f32)
    pad = tiles * LANES - nz - 2 * hz
    direct = slabs == 2 and nz % LANES == 0 and 4 * hz == LANES and cx % 2 == 0
    sx, sy = lax.axis_index("sx"), lax.axis_index("sy")
    place = jnp.stack([sx, sy]).astype(jnp.int32)

    def shape(*dims):
        return jax.ShapeDtypeStruct(dims, f32)

    def call(kernel, out_shape, args, scratch, name, limit, flops, scalars=0, unread=()):
        moved = sum(a.size * 4 for a in args) + sum(o.size * 4 for o in out_shape)
        spaces = [pltpu.SMEM] * scalars + [pltpu.VMEM] * (len(args) - scalars)
        spaces = [pl.ANY if n in unread else space for n, space in enumerate(spaces)]
        return pl.pallas_call(
            kernel,
            out_shape=out_shape,
            in_specs=[pl.BlockSpec(memory_space=space) for space in spaces],
            out_specs=[VMEM] * len(out_shape),
            scratch_shapes=[pltpu.VMEM(dims, f32) for dims in scratch],
            compiler_params=pltpu.CompilerParams(vmem_limit_bytes=limit << 20),
            cost_estimate=pl.CostEstimate(flops=flops, bytes_accessed=moved, transcendentals=0),
            name=name,
        )(*args)

    rounds_y = swaps(lax.axis_size("sy"))
    if direct:
        volume = observed.reshape(-1, LANES, cx, cy).transpose(0, 2, 3, 1)
        zone_rows = jnp.pad(zones.reshape(-1, LANES), ((0, 8 - nz // LANES), (0, 0)))
        edge, edge_z = shape(volume.shape[0], cx * hy, LANES), shape(cx * hy, LANES)
        first, second, first_z, second_z, borders = call(
            functools.partial(edges_kernel, hy, hz), [edge, edge, edge_z, edge_z, shape(cx // 2 * cy + 8, LANES)],
            (place, volume, zone_rows), [], "edges", 8, 1, scalars=1,
        )
        borders = lax.ppermute(borders, "gz", [(0, 1), (1, 0)])
        parts = [volume, lax.ppermute(first, "sy", both_ways(rounds_y[0])), lax.ppermute(second, "sy", both_ways(rounds_y[1]))]
        parts.append(borders)
        for value, pairs in ((first_z, rounds_y[0]), (second_z, rounds_y[1])):
            cross = [(2 * i + g, 2 * j + 1 - g) for i, j in pairs for g in range(2)]
            parts.append(lax.ppermute(value, ("sy", "gz"), both_ways(cross)))
        got_ids = borders[cx // 2 * cy :].reshape(-1)[:nz]
        ids_before, ids_after = got_ids[nz - hz :], got_ids[:hz]
    else:

        def with_zones(part, ids):
            flat = jnp.pad(ids, (0, cx * cy - ids.shape[0]))
            return jnp.concatenate([part, flat.reshape(1, cx, cy)], axis=0)

        ring = [(i, (i + 1) % slabs) for i in range(slabs)]
        first = lax.ppermute(with_zones(observed[nz - hz :], zones[nz - hz :]), "gz", ring)
        second = lax.ppermute(with_zones(observed[:hz], zones[:hz]), "gz", [(j, i) for i, j in ring])
        before, after = first[:hz], second[:hz]
        ids_before, ids_after = first[hz].reshape(-1)[:hz], second[hz].reshape(-1)[:hz]
        volume = jnp.concatenate([before, observed, after, jnp.zeros((pad, cx, cy), f32)], axis=0)
        volume = volume.reshape(tiles, LANES, cx, cy).transpose(0, 2, 3, 1)
        edge = shape(tiles, cx * hy, LANES)
        first, second = call(
            functools.partial(edges_kernel, hy, hz), [edge, edge], (place, volume), [], "edges", 8, 1, scalars=1
        )
        parts = [volume, lax.ppermute(first, "sy", both_ways(rounds_y[0])), lax.ppermute(second, "sy", both_ways(rounds_y[1]))]
    ids = jnp.concatenate([ids_before, zones, ids_after, jnp.full((pad,), -1.0, f32)])

    def lanes_of(kernels, names):
        match = (names[None, :] == jnp.arange(lateral_x.shape[0], dtype=f32)[:, None]).astype(f32)
        table = jnp.sum(match[:, None, :] * kernels[:, :, None], axis=0)
        table = table.reshape(taps, -1, 1, LANES).transpose(1, 0, 2, 3)
        return jnp.broadcast_to(table, (table.shape[0], taps, 8, LANES))

    tx, ty = lanes_of(lateral_x, ids), lanes_of(lateral_y, ids)
    own = ceil_to(nz, LANES) // LANES
    own_ids = jnp.concatenate([zones, jnp.full((own * LANES - nz,), -1.0, f32)])
    tx_own, ty_own = lanes_of(lateral_x, own_ids), lanes_of(lateral_y, own_ids)

    wide = cx + 2 * reach
    packed = nz + 2 * hz - (tiles - 1) * LANES <= LANES // 2
    planes = hx * (tiles - 1) + hx // 2 if packed else hx * tiles
    end0, end1, end2 = cy + 2 * hy, cy + 2 * hy - 4 * reach, cy
    mid1 = ceil_to(end1 // 2, 8) + 8
    mid2 = mid1 - ceil_to(4 * reach, 8)
    cut = ceil_to(mid1 + 4 * reach, 8)
    rounds_x = [both_ways(pairs) for pairs in swaps(lax.axis_size("sx"))]
    full = ceil_to(cy + 2 * hy + reach, 8)

    def pay_shapes(rows):
        return [shape(planes, ceil_to(rows, 8), LANES)] * 2

    def swap(pays):
        return lax.ppermute(pays[0], "sx", rounds_x[0]), lax.ppermute(pays[1], "sx", rounds_x[1])

    ext, *pays = call(
        functools.partial(assemble_kernel, packed, hx, cut, hz, len(parts)),
        [shape(tiles, cx, full, LANES)] + pay_shapes(cut) + pay_shapes(end0 - cut),
        (place, *parts), [], "assemble", 8, 1, scalars=1,
    )
    halo_a = swap(pays[:2])
    halo_b = swap(pays[2:])

    wins = windows_of(tiles)
    size = wins[0][1] * LANES
    fh, fl, bh, bl, sh, sl = call(
        functools.partial(band_kernel, hz),
        [jax.ShapeDtypeStruct((len(wins), size, size), jnp.bfloat16)] * 4
        + [jax.ShapeDtypeStruct((len(wins), size, own * LANES), jnp.bfloat16)] * 2,
        (depth_psf, pays[-1]), [], "band", 8, 1, scalars=1, unread=(1,),
    )
    stacks_x, stacks_y = stitch_width.shape[:2]
    weight, inv = call(
        functools.partial(norm_kernel, (cx, cy, hy, stacks_x, stacks_y)),
        [shape(wide, full, LANES), shape(tiles, cx, ceil_to(end1, 8), LANES)],
        (place, stitch_width.reshape(-1), pays[-1], tx, ty), [(tiles, cx, full, LANES)], "norm", 10, 1, scalars=2, unread=(2,),
    )
    shift = 2 * reach

    def inner(name, est, data_off, shifted, rows, need, back):
        plan = dict(data_off=data_off, shifted=shifted, need=need)
        args = (est, ext, weight, tx, ty, fh, fl) + back
        rows = ceil_to(rows, 8)
        return call(
            functools.partial(inner_kernel, plan),
            [shape(own if shifted else tiles, cx - shift, rows, LANES)], args,
            [(tiles, cx - shift, rows + 16, LANES)], name, 24, 1,
        )[0]

    def outer(name, est, halos, extra, inner_part, last, plan, outs):
        rows = ceil_to(plan["high"] - plan["low"] + 2 * reach, 8)
        back, lateral = ((sh, sl), (tx_own, ty_own)) if last else ((bh, bl), (tx, ty))
        args = (place, est) + tuple(h for _, pair in halos for h in pair) + extra
        args += (inner_part, inv, tx, ty) + lateral + (fh, fl) + back
        plan = dict(
            plan, hx=hx, packed=packed, halos=[rng for rng, _ in halos], make_data=not last, pay=not last,
            shifted=last, data_off=shift if last else 0, lane0=hz if last else 0,
        )
        scratch = [(tiles, cx, rows + 16, LANES), (own if last else tiles, 2 * hx, rows, LANES)]
        return call(functools.partial(outer_kernel, plan), outs, args, scratch, name, 16, 1, scalars=1)

    data_at = mid2 + 8
    spread1 = inner("inner_1", ext, 0, False, end1 + shift, end0, (bh, bl))
    est_a, data_a, *pays = outer(
        "outer_1a", ext, [((0, cut), halo_a)], (weight,), spread1, False,
        dict(low=0, high=mid1, data_base=0, prior=False),
        [shape(tiles, cx, mid1, LANES), shape(tiles, 2 * hx, cut, LANES)] + pay_shapes(mid1),
    )
    halo_c = swap(pays)
    est, data_b, *pays = outer(
        "outer_1b", ext, [((0, cut), halo_a), ((cut, end0), halo_b)], (weight, est_a), spread1, False,
        dict(low=mid1, high=end1, data_base=data_at, prior=True),
        [shape(tiles, cx, ceil_to(end1, 8), LANES), shape(tiles, 2 * hx, full - data_at, LANES)] + pay_shapes(end1 - mid1),
    )
    halo_d = swap(pays)
    spread2 = inner("inner_2", est, shift, True, end2 + shift, end1, (sh, sl))
    (out_a,) = outer(
        "outer_2a", est, [((0, mid1), halo_c)], (data_a,), spread2, True,
        dict(low=0, high=mid2, data_base=0, prior=False), [shape(own, cx, mid2, LANES)],
    )
    (out_b,) = outer(
        "outer_2b", est, [((0, mid1), halo_c), ((mid1, end1), halo_d)], (data_b,), spread2, True,
        dict(low=mid2, high=end2, data_base=data_at, prior=False), [shape(own, cx, end2 - mid2, LANES)],
    )
    estimate = jnp.concatenate([out_a, out_b], axis=2)
    return estimate.transpose(0, 3, 1, 2).reshape(own * LANES, cx, cy)[:nz]


def solution(mesh):
    in_specs = (P("gz", "sx", "sy"), P("gz"), P(), P(), P(), P())
    out_specs = P("gz", "sx", "sy")
    return jax.shard_map(body, mesh=mesh, in_specs=in_specs, out_specs=out_specs, check_vma=False)
```

```python
import functools

import jax
import jax.numpy as jnp
from jax import lax
from jax.experimental import pallas as pl
from jax.experimental.pallas import tpu as pltpu
from jax.sharding import PartitionSpec as P


ITERS = 2
LANES = 128
TINY = 1e-30
VMEM = pl.BlockSpec(memory_space=pltpu.VMEM)


def ceil_to(value, unit):
    return -(-value // unit) * unit


def swaps(count):
    return [[(i, i + 1) for i in range(first, count - 1, 2)] for first in (0, 1)]


def both_ways(pairs):
    return pairs + [(j, i) for i, j in pairs]


def lane_is_low():
    return lax.broadcasted_iota(jnp.int32, (8, LANES), 1) < LANES // 2


def halo_row(ref, tiles, packed, hx, t, p, rows):
    if not packed or t < tiles - 1:
        return ref[hx * t + p, rows, :]
    half = hx // 2
    value = ref[hx * t + p % half, rows, :]
    if p >= half:
        value = pltpu.roll(value, LANES // 2, 1)
    return jnp.where(lane_is_low(), value, 0.0)


def pack_both(src, pays, odd, packed, hx, blocks, src_block):
    high = src.shape[1] - hx
    pack_rows(src, pays[0], packed, hx, jnp.where(odd == 1, 0, high), blocks, src_block, 0)
    pack_rows(src, pays[1], packed, hx, jnp.where(odd == 1, high, 0), blocks, src_block, 0)


def by_side(odd, first, second):
    return jnp.where(odd == 1, first, second), jnp.where(odd == 1, second, first)


def pack_rows(src, pay, packed, hx, x0, blocks, src_block, pay_block):
    tiles = src.shape[0]

    def step(j, carry):
        here = pl.ds(pl.multiple_of(8 * (j + src_block), 8), 8)
        there = pl.ds(pl.multiple_of(8 * (j + pay_block), 8), 8)
        for t in range(tiles - 1 if packed else tiles):
            for p in range(hx):
                pay[hx * t + p, there, :] = src[t, x0 + p, here, :]
        if packed:
            half = hx // 2
            for p in range(half):
                other = pltpu.roll(src[tiles - 1, x0 + p + half, here, :], LANES // 2, 1)
                pay[hx * (tiles - 1) + p, there, :] = jnp.where(lane_is_low(), src[tiles - 1, x0 + p, here, :], other)
        return carry

    lax.fori_loop(0, blocks, step, 0)


def conv_rows(k, v, width):
    out = []
    for x in range(width):
        acc = k[0] * v[x]
        for a in range(1, len(k)):
            acc = acc + k[a] * v[x + a]
        out.append(acc)
    return out


def y_conv(src, taps, reverse, t, width, blocks, emit):
    count = taps.shape[1]
    k = [taps[t, count - 1 - b if reverse else b] for b in range(count)]

    def step(x, carry):
        for j in range(blocks):
            acc = k[0] * src[t, x, 8 * j : 8 * j + 8, :]
            for b in range(1, count):
                acc = acc + k[b] * src[t, x, 8 * j + b : 8 * j + b + 8, :]
            emit(t, x, j, acc)
        return carry

    lax.fori_loop(0, width, step, 0)


def windows_of(tiles):
    return [(0, tiles)] if tiles <= 2 else [(w, 2) for w in range(tiles - 1)]


def depth_rows(parts, hi_ref, lo_ref, shifted=False):
    split = []
    for part in parts:
        hi = part.astype(jnp.bfloat16)
        split.append((hi, (part - hi.astype(jnp.float32)).astype(jnp.bfloat16)))
    dot = functools.partial(jnp.dot, preferred_element_type=jnp.float32)
    out = {}
    for index, (first, span) in enumerate(windows_of(len(parts))):
        his = jnp.concatenate([split[first + s][0] for s in range(span)], axis=1)
        los = jnp.concatenate([split[first + s][1] for s in range(span)], axis=1)
        res = dot(his, hi_ref[index]) + (dot(los, hi_ref[index]) + dot(his, lo_ref[index]))
        for s in range(res.shape[1] // LANES):
            to = s if shifted else first + s
            piece = res[:, s * LANES : (s + 1) * LANES]
            out[to] = out[to] + piece if to in out else piece
    return [out[t] for t in range(len(out))]


def x_loop(taps, reverse, first, last, rows_in, rows_out):
    tiles, count = taps.shape[:2]

    def step(j, carry):
        for t in range(tiles):
            k = [taps[t, count - 1 - a if reverse else a] for a in range(count)]
            for n, v in enumerate(rows_in(t, j)):
                rows_out(t, j, n, conv_rows(k, v, len(v) - count + 1))
        return carry

    if first < last:
        lax.fori_loop(first, last, step, 0)


def y_group(mid_ref, taps, t, first, group, blocks):
    count = taps.shape[1]
    k = [taps[t, b] for b in range(count)]
    out = []
    for x in [first + n for n in range(group)]:
        for j in range(blocks):
            acc = k[0] * mid_ref[t, x, 8 * j : 8 * j + 8, :]
            for b in range(1, count):
                acc = acc + k[b] * mid_ref[t, x, 8 * j + b : 8 * j + b + 8, :]
            out.append(acc)
    return jnp.concatenate(out, axis=0)


def correct(mid_ref, ty_ref, mats, shifted, group, count, rows, data_of, spread_ref):
    fh_ref, fl_ref, bh_ref, bl_ref = mats
    tiles = mid_ref.shape[0]
    group = next(n for n in range(group, 0, -1) if count % n == 0 and n * rows % 16 == 0)

    def depth(i, carry):
        first = group * i
        blurred = [y_group(mid_ref, ty_ref, t, first, group, rows // 8) for t in range(tiles)]
        blurred = depth_rows(blurred, fh_ref, fl_ref)
        ratio = [data_of(t, first, group) / jnp.maximum(blurred[t], TINY) for t in range(tiles)]
        for t, value in enumerate(depth_rows(ratio, bh_ref, bl_ref, shifted)):
            spread_ref[t, pl.ds(first, group), 0:rows, :] = value.reshape(group, rows, LANES)
        return carry

    lax.fori_loop(0, count // group, depth, 0)


def inner_kernel(plan, est_ref, obs_ref, w_ref, tx_ref, ty_ref, fh_ref, fl_ref, bh_ref, bl_ref, spread_ref, mid_ref):
    _, cx = est_ref.shape[:2]
    reach = (tx_ref.shape[1] - 1) // 2
    rows = spread_ref.shape[2]
    first = plan["data_off"] + reach
    count = cx - 2 * reach

    def rows_in(t, j):
        here = pl.ds(pl.multiple_of(8 * j, 8), 8)
        return [[est_ref[t, x, here, :] for x in range(cx)]]

    def rows_out(t, j, n, values):
        here = pl.ds(pl.multiple_of(8 * j, 8), 8)
        for x, value in enumerate(values):
            mid_ref[t, x, here, :] = value

    x_loop(tx_ref, False, 0, -(-plan["need"] // 8), rows_in, rows_out)

    def data_of(t, x, group):
        seen = obs_ref[t, pl.ds(x + reach, group), first : first + rows, :]
        return (seen * w_ref[pl.ds(x + 2 * reach, group), first : first + rows, :]).reshape(group * rows, LANES)

    mats = (fh_ref, fl_ref, bh_ref, bl_ref)
    correct(mid_ref, ty_ref, mats, plan["shifted"], 2, count, rows, data_of, spread_ref)


def norm_kernel(plan, place_ref, bands_ref, _, tx_ref, ty_ref, w_ref, out_ref, mid_ref):
    cx, cy, hy, stacks_x, stacks_y = plan
    tiles, count = tx_ref.shape[:2]
    reach = (count - 1) // 2
    width = out_ref.shape[1]
    full = w_ref.shape[1]
    sx, sy = place_ref[0], place_ref[1]
    row = lax.broadcasted_iota(jnp.int32, (full, LANES), 0)
    for x in range(cx + 2 * reach):
        a = (x - reach) // cx
        px = (x - reach) % cx
        gx = sx + a
        value = jnp.zeros((full, LANES), jnp.float32)
        for b, first in ((-1, 0), (0, hy), (1, hy + cy)):
            gy = sy + b
            inside = (gx >= 0) & (gx < stacks_x) & (gy >= 0) & (gy < stacks_y)
            spot = 2 * (jnp.clip(gx, 0, stacks_x - 1) * stacks_y + jnp.clip(gy, 0, stacks_y - 1))
            along = jnp.where(inside, jnp.where(px < bands_ref[spot], 0.5, 1.0), 0.0)
            across = jnp.where(row - hy - b * cy < bands_ref[spot + 1], 0.5, 1.0)
            value = jnp.where(row >= first, across * along, value)
        w_ref[x] = value

    def rows_in(t, j):
        rows = pl.ds(pl.multiple_of(8 * j, 8), 8)
        return [[w_ref[x, rows, :] for x in range(width + count - 1)]]

    def rows_out(t, j, n, values):
        rows = pl.ds(pl.multiple_of(8 * j, 8), 8)
        for x, value in enumerate(values):
            mid_ref[t, x, rows, :] = value

    x_loop(tx_ref, True, 0, full // 8, rows_in, rows_out)
    for t in range(tiles):
        ky = [ty_ref[t, count - 1 - b] for b in range(count)]

        def ystep(x, carry, ky=ky, t=t):
            for j in range(out_ref.shape[2] // 8):
                at = 8 * j + reach
                acc = ky[0] * mid_ref[t, x, at : at + 8, :]
                for b in range(1, count):
                    acc = acc + ky[b] * mid_ref[t, x, at + b : at + b + 8, :]
                out_ref[t, x, 8 * j : 8 * j + 8, :] = 1.0 / jnp.maximum(acc, TINY)
            return carry

        lax.fori_loop(0, width, ystep, 0)


def band_kernel(lane0, psf_ref, _, fh_ref, fl_ref, bh_ref, bl_ref, sh_ref, sl_ref):
    windows, size = fh_ref.shape[:2]
    taps = psf_ref.shape[0]
    total = psf_ref[0]
    for j in range(1, taps):
        total = total + psf_ref[j]
    step = LANES // 2
    for r in range(0, size, step):
        shape = (step, size)
        cols = lax.broadcasted_iota(jnp.int32, shape, 1)
        off = cols - lax.broadcasted_iota(jnp.int32, shape, 0) - r + (taps - 1) // 2
        band, flip = jnp.zeros(shape, jnp.float32), jnp.zeros(shape, jnp.float32)
        for j in range(taps):
            band = jnp.where(off == j, psf_ref[j], band)
            flip = jnp.where(off == taps - 1 - j, psf_ref[j], flip)
        for matrix, hi_ref, lo_ref in ((band, fh_ref, fl_ref), (flip, bh_ref, bl_ref)):
            matrix = matrix / jnp.full(shape, total, jnp.float32)
            for w in range(windows):
                first = 0 if w == 0 else LANES // 2
                last = size if w == windows - 1 else LANES + LANES // 2
                part = jnp.where((cols >= first) & (cols < last), matrix, 0.0)
                hi = part.astype(jnp.bfloat16)
                hi_ref[w, r : r + step, :] = hi
                lo_ref[w, r : r + step, :] = (part - hi.astype(jnp.float32)).astype(jnp.bfloat16)
        shape = (step, sh_ref.shape[2])
        for w in range(windows):
            ext = lax.broadcasted_iota(jnp.int32, shape, 0) + r + w * LANES
            off = ext - lax.broadcasted_iota(jnp.int32, shape, 1) - lane0 + (taps - 1) // 2
            part = jnp.zeros(shape, jnp.float32)
            first = 0 if w == 0 else LANES // 2
            last = size if w == windows - 1 else LANES + LANES // 2
            if first <= r < last:
                for j in range(taps):
                    part = jnp.where(off == j, psf_ref[j], part)
                part = part / jnp.full(shape, total, jnp.float32)
            hi = part.astype(jnp.bfloat16)
            sh_ref[w, r : r + step, :] = hi
            sl_ref[w, r : r + step, :] = (part - hi.astype(jnp.float32)).astype(jnp.bfloat16)


def turned(shift, main, halo):
    if halo is None:
        return main
    lane = lax.broadcasted_iota(jnp.int32, main[0].shape, 1)
    moved = [pltpu.roll(m, shift, 1) for m in main]
    out = [jnp.where(lane < shift, halo, moved[0])]
    out += [jnp.where(lane < shift, moved[t - 1], moved[t]) for t in range(1, len(main))]
    tail = jnp.where(lane < shift, moved[-1], jnp.where(lane < 2 * shift, halo, 0.0))
    return out + [tail]


def edges_kernel(hy, shift, place_ref, vol_ref, *refs):
    tiles, cx, cy = vol_ref.shape[:3]
    odd = place_ref[1] % 2
    direct = len(refs) > 2
    if direct:
        zones_ref, first_ref, second_ref, first_z, second_z, depth_ref = refs
        lane = lax.broadcasted_iota(jnp.int32, (cy, LANES), 1)
        half = cx // 2

        def outmost(x):
            return pltpu.roll(jnp.where(lane < LANES // 2, vol_ref[0, x], vol_ref[tiles - 1, x]), shift, 1)

        for x in range(half):
            other = pltpu.roll(outmost(x + half), LANES // 2, 1)
            depth_ref[cy * x : cy * x + cy, :] = jnp.where(lane < LANES // 2, outmost(x), other)
        depth_ref[cy * half :, :] = zones_ref[...]
    else:
        first_ref, second_ref = refs
    lane = lax.broadcasted_iota(jnp.int32, (hy, LANES), 1)
    for x in range(cx):
        to = slice(hy * x, hy * x + hy)
        both = []
        for t in range(tiles):
            low, high = vol_ref[t, x, 0:hy, :], vol_ref[t, x, cy - hy : cy, :]
            both.append((jnp.where(odd == 1, low, high), jnp.where(odd == 1, high, low)))
            first_ref[t, to, :], second_ref[t, to, :] = both[-1]
        if direct:
            for n, ref in enumerate((first_z, second_z)):
                ref[to, :] = pltpu.roll(jnp.where(lane < LANES // 2, both[0][n], both[-1][n]), shift, 1)


def assemble_kernel(packed, hx, cut, shift, refs_in, place_ref, *refs):
    vol_ref, first_ref, second_ref = refs[:3]
    depth_ref, first_z, second_z = refs[3:6] if refs_in == 6 else (None,) * 3
    ext_ref, *pays = refs[refs_in:]
    main, cx, cy = vol_ref.shape[:3]
    hy = first_ref.shape[1] // cx
    end = cy + 2 * hy
    odd = place_ref[1] % 2
    half = cx // 2

    for x in range(cx):
        edge = slice(hy * x, hy * x + hy)
        low, high = zip(*[by_side(odd, first_ref[t, edge, :], second_ref[t, edge, :]) for t in range(main)])
        low_z = high_z = halo = None
        if depth_ref is not None:
            low_z, high_z = by_side(odd, first_z[edge, :], second_z[edge, :])
            halo = depth_ref[cy * (x % half) : cy * (x % half) + cy, :]
            halo = pltpu.roll(halo, LANES // 2, 1) if x >= half else halo
        low = turned(shift, low, low_z)
        mids = turned(shift, [vol_ref[t, x] for t in range(main)], halo)
        high = turned(shift, high, high_z)
        for t in range(ext_ref.shape[0]):
            ext_ref[t, x, 0:hy, :] = low[t]
            ext_ref[t, x, hy : hy + cy, :] = mids[t]
            ext_ref[t, x, hy + cy : end, :] = high[t]
            ext_ref[t, x, end:, :] = jnp.zeros((ext_ref.shape[2] - end, LANES), jnp.float32)
    odd_x = place_ref[0] % 2
    for n in range(2):
        start, stop = (0, cut) if n == 0 else (cut, end)
        pack_both(ext_ref, pays[2 * n : 2 * n + 2], odd_x, packed, hx, -(-(stop - start) // 8), start // 8)


def outer_kernel(plan, place_ref, *refs):
    refs = list(refs)
    odd = place_ref[0] % 2
    take = refs.pop
    est_ref = take(0)
    halos = [(take(0), take(0), first, last) for first, last in plan["halos"]]
    make = plan["make_data"]
    w_ref = take(0) if make else None
    data_in = None if make else take(0)
    prior_ref = take(0) if plan["prior"] else None
    inner_ref, inv_ref, tx_ref, ty_ref, bx_ref, by_ref = [take(0) for _ in range(6)]
    mats = [take(0) for _ in range(4)]
    out_ref = take(0)
    data_ref = take(0) if make else data_in
    pays = [take(0), take(0)] if plan["pay"] else None
    mid_ref, edge_ref = refs
    packed, hx, low, high = plan["packed"], plan["hx"], plan["low"], plan["high"]
    data_base, off, lane0 = plan["data_base"], plan["data_off"], plan["lane0"]
    tiles, cx = est_ref.shape[:2]
    outs = out_ref.shape[0]
    count = tx_ref.shape[1]
    reach = (count - 1) // 2
    rows = edge_ref.shape[2]
    last_block = -(-(high + 4 * reach) // 8)
    data_first = data_base // 8 if make else low // 8

    for lo_ref, hi_ref, first, last in halos:

        def rows_in(t, j, lo_ref=lo_ref, hi_ref=hi_ref, first=first):
            here = pl.ds(pl.multiple_of(8 * j, 8), 8)
            there = pl.ds(pl.multiple_of(8 * j - first, 8), 8)
            lows, highs = [], []
            for p in range(hx):
                came = [halo_row(ref, tiles, packed, hx, t, p, there) for ref in (lo_ref, hi_ref)]
                low_row, high_row = by_side(odd, *came)
                lows.append(low_row)
                highs.append(high_row)
            one = lows + [est_ref[t, x, here, :] for x in range(hx)]
            return [one, [est_ref[t, x, here, :] for x in range(cx - hx, cx)] + highs]

        def keep(t, j, pair):
            here = pl.ds(pl.multiple_of(8 * j, 8), 8)
            there = pl.ds(pl.multiple_of(8 * j - data_base, 8), 8)
            for n, v in enumerate(pair):
                for x in range(hx):
                    data_ref[t, hx * n + x, there, :] = w_ref[x + cx * n, here, :] * v[x + reach]

        def rows_in_keep(t, j, rows_in=rows_in, keep=keep):
            pair = rows_in(t, j)
            if make:
                keep(t, j, pair)
            return pair

        def rows_out(t, j, n, values):
            mid = pl.ds(pl.multiple_of(8 * j - low, 8), 8)
            for x, value in enumerate(values):
                mid_ref[t, hx * n + x, mid, :] = value

        def only_data(j, carry, rows_in=rows_in, keep=keep):
            for t in range(tiles):
                keep(t, j, rows_in(t, j))
            return carry

        a, b = max(first // 8, data_first), min(last // 8, low // 8)
        if make and a < b:
            lax.fori_loop(a, b, only_data, 0)
        x_loop(tx_ref, False, max(first // 8, low // 8), min(-(-last // 8), last_block), rows_in_keep, rows_out)

    spot0 = low + off + reach - data_base

    def data_of(t, x, group):
        return data_ref[t, pl.ds(x, group), spot0 : spot0 + rows, :].reshape(group * rows, LANES)

    correct(mid_ref, ty_ref, mats, plan["shifted"], 6, 2 * hx, rows, data_of, edge_ref)

    blocks = -(-(high - low) // 8)

    def back_in(t, j):
        here = pl.ds(pl.multiple_of(8 * j, 8), 8)
        there = pl.ds(pl.multiple_of(8 * j + low, 8), 8)
        v = [edge_ref[t, x, here, :] for x in range(hx)]
        v += [inner_ref[t, x, there, :] for x in range(cx - 2 * reach)]
        return [v + [edge_ref[t, x, here, :] for x in range(hx, 2 * hx)]]

    def back_out(t, j, n, values):
        here = pl.ds(pl.multiple_of(8 * j, 8), 8)
        for x, value in enumerate(values):
            mid_ref[t, x, here, :] = value

    x_loop(bx_ref, True, 0, rows // 8, back_in, back_out)
    base = low if prior_ref is not None else 0

    def finish(t, x, j, acc):
        at = 8 * j + low + 2 * reach
        scale = 8 * j + low + off
        old = est_ref[t, x, at : at + 8, :] * inv_ref[t, x, scale : scale + 8, :]
        if lane0:
            if t + 1 < tiles:
                more = est_ref[t + 1, x, at : at + 8, :] * inv_ref[t + 1, x, scale : scale + 8, :]
                lane = lax.broadcasted_iota(jnp.int32, (8, LANES), 1)
                old = jnp.where(lane >= lane0, old, more)
            old = pltpu.roll(old, LANES - lane0, 1)
        to = 8 * j + base
        out_ref[t, x, to : to + 8, :] = old * acc

    for t in range(outs):
        y_conv(mid_ref, by_ref, True, t, cx, blocks, finish)

    if prior_ref is not None:
        for t in range(outs):

            def copy(x, carry, t=t):
                out_ref[t, x, 0:low, :] = prior_ref[t, x, 0:low, :]
                return carry

            lax.fori_loop(0, cx, copy, 0)
    if pays:
        pack_both(out_ref, pays, odd, packed, hx, blocks, base // 8)


def body(observed, zone_of_slice, lateral_x, lateral_y, depth_psf, stitch_width):
    nz, cx, cy = observed.shape
    taps = lateral_x.shape[1]
    reach = (taps - 1) // 2
    zreach = (depth_psf.shape[0] - 1) // 2
    hz = 2 * zreach * ITERS
    hy = 2 * reach * ITERS
    hx = 2 * reach
    slabs = lax.axis_size("gz")
    tiles = ceil_to(nz + 2 * hz, LANES) // LANES
    f32 = jnp.float32

    zones = zone_of_slice.astype(f32)
    pad = tiles * LANES - nz - 2 * hz
    direct = slabs == 2 and nz % LANES == 0 and 4 * hz == LANES and cx % 2 == 0
    sx, sy = lax.axis_index("sx"), lax.axis_index("sy")
    place = jnp.stack([sx, sy]).astype(jnp.int32)

    def shape(*dims):
        return jax.ShapeDtypeStruct(dims, f32)

    def call(kernel, out_shape, args, scratch, limit, flops, scalars=0, unread=()):
        moved = sum(a.size * 4 for a in args) + sum(o.size * 4 for o in out_shape)
        spaces = [pltpu.SMEM] * scalars + [pltpu.VMEM] * (len(args) - scalars)
        spaces = [pl.ANY if n in unread else space for n, space in enumerate(spaces)]
        return pl.pallas_call(
            kernel,
            out_shape=out_shape,
            in_specs=[pl.BlockSpec(memory_space=space) for space in spaces],
            out_specs=[VMEM] * len(out_shape),
            scratch_shapes=[pltpu.VMEM(dims, f32) for dims in scratch],
            compiler_params=pltpu.CompilerParams(vmem_limit_bytes=limit << 20),
            cost_estimate=pl.CostEstimate(flops=flops, bytes_accessed=moved, transcendentals=0),
        )(*args)

    rounds_y = swaps(lax.axis_size("sy"))
    if direct:
        volume = observed.reshape(-1, LANES, cx, cy).transpose(0, 2, 3, 1)
        zone_rows = jnp.pad(zones.reshape(-1, LANES), ((0, 8 - nz // LANES), (0, 0)))
        edge, edge_z = shape(volume.shape[0], cx * hy, LANES), shape(cx * hy, LANES)
        first, second, first_z, second_z, borders = call(
            functools.partial(edges_kernel, hy, hz), [edge, edge, edge_z, edge_z, shape(cx // 2 * cy + 8, LANES)],
            (place, volume, zone_rows), [], 8, 1, scalars=1,
        )
        borders = lax.ppermute(borders, "gz", [(0, 1), (1, 0)])
        parts = [volume, lax.ppermute(first, "sy", both_ways(rounds_y[0])), lax.ppermute(second, "sy", both_ways(rounds_y[1]))]
        parts.append(borders)
        for value, pairs in ((first_z, rounds_y[0]), (second_z, rounds_y[1])):
            cross = [(2 * i + g, 2 * j + 1 - g) for i, j in pairs for g in range(2)]
            parts.append(lax.ppermute(value, ("sy", "gz"), both_ways(cross)))
        got_ids = borders[cx // 2 * cy :].reshape(-1)[:nz]
        ids_before, ids_after = got_ids[nz - hz :], got_ids[:hz]
    else:

        def with_zones(part, ids):
            flat = jnp.pad(ids, (0, cx * cy - ids.shape[0]))
            return jnp.concatenate([part, flat.reshape(1, cx, cy)], axis=0)

        ring = [(i, (i + 1) % slabs) for i in range(slabs)]
        first = lax.ppermute(with_zones(observed[nz - hz :], zones[nz - hz :]), "gz", ring)
        second = lax.ppermute(with_zones(observed[:hz], zones[:hz]), "gz", [(j, i) for i, j in ring])
        before, after = first[:hz], second[:hz]
        ids_before, ids_after = first[hz].reshape(-1)[:hz], second[hz].reshape(-1)[:hz]
        volume = jnp.concatenate([before, observed, after, jnp.zeros((pad, cx, cy), f32)], axis=0)
        volume = volume.reshape(tiles, LANES, cx, cy).transpose(0, 2, 3, 1)
        edge = shape(tiles, cx * hy, LANES)
        first, second = call(
            functools.partial(edges_kernel, hy, hz), [edge, edge], (place, volume), [], 8, 1, scalars=1
        )
        parts = [volume, lax.ppermute(first, "sy", both_ways(rounds_y[0])), lax.ppermute(second, "sy", both_ways(rounds_y[1]))]
    ids = jnp.concatenate([ids_before, zones, ids_after, jnp.full((pad,), -1.0, f32)])

    def lanes_of(kernels, names):
        match = (names[None, :] == jnp.arange(lateral_x.shape[0], dtype=f32)[:, None]).astype(f32)
        table = jnp.sum(match[:, None, :] * kernels[:, :, None], axis=0)
        table = table.reshape(taps, -1, 1, LANES).transpose(1, 0, 2, 3)
        return jnp.broadcast_to(table, (table.shape[0], taps, 8, LANES))

    tx, ty = lanes_of(lateral_x, ids), lanes_of(lateral_y, ids)
    own = ceil_to(nz, LANES) // LANES
    own_ids = jnp.concatenate([zones, jnp.full((own * LANES - nz,), -1.0, f32)])
    tx_own, ty_own = lanes_of(lateral_x, own_ids), lanes_of(lateral_y, own_ids)

    wide = cx + 2 * reach
    packed = nz + 2 * hz - (tiles - 1) * LANES <= LANES // 2
    planes = hx * (tiles - 1) + hx // 2 if packed else hx * tiles
    end0, end1, end2 = cy + 2 * hy, cy + 2 * hy - 4 * reach, cy
    mid1 = ceil_to(end1 // 2, 8) + 8
    mid2 = mid1 - ceil_to(4 * reach, 8)
    cut = ceil_to(mid1 + 4 * reach, 8)
    rounds_x = [both_ways(pairs) for pairs in swaps(lax.axis_size("sx"))]
    full = ceil_to(cy + 2 * hy + reach, 8)

    def pay_shapes(rows):
        return [shape(planes, ceil_to(rows, 8), LANES)] * 2

    def swap(pays):
        got = []
        for n in range(2):
            got.append(lax.ppermute(pays[n], "sx", rounds_x[n]))
        return got

    ext, *pays = call(
        functools.partial(assemble_kernel, packed, hx, cut, hz, len(parts)),
        [shape(tiles, cx, full, LANES)] + pay_shapes(cut) + pay_shapes(end0 - cut),
        (place, *parts), [], 8, 1, scalars=1,
    )
    halo_a = swap(pays[:2])
    halo_b = swap(pays[2:])

    wins = windows_of(tiles)
    size = wins[0][1] * LANES
    fh, fl, bh, bl, sh, sl = call(
        functools.partial(band_kernel, hz),
        [jax.ShapeDtypeStruct((len(wins), size, size), jnp.bfloat16)] * 4
        + [jax.ShapeDtypeStruct((len(wins), size, own * LANES), jnp.bfloat16)] * 2,
        (depth_psf, pays[-1]), [], 8, 1, scalars=1, unread=(1,),
    )
    stacks_x, stacks_y = stitch_width.shape[:2]
    weight, inv = call(
        functools.partial(norm_kernel, (cx, cy, hy, stacks_x, stacks_y)),
        [shape(wide, full, LANES), shape(tiles, cx, ceil_to(end1, 8), LANES)],
        (place, stitch_width.reshape(-1), pays[-1], tx, ty), [(tiles, cx, full, LANES)], 10, 1, scalars=2, unread=(2,),
    )
    shift = 2 * reach

    def inner(est, data_off, shifted, rows, need, back):
        plan = dict(data_off=data_off, shifted=shifted, need=need)
        args = (est, ext, weight, tx, ty, fh, fl) + back
        rows = ceil_to(rows, 8)
        return call(
            functools.partial(inner_kernel, plan),
            [shape(own if shifted else tiles, cx - shift, rows, LANES)], args,
            [(tiles, cx - shift, rows + 16, LANES)], 24, 1,
        )[0]

    def outer(est, halos, extra, inner_part, last, plan, outs):
        rows = ceil_to(plan["high"] - plan["low"] + 2 * reach, 8)
        back, lateral = ((sh, sl), (tx_own, ty_own)) if last else ((bh, bl), (tx, ty))
        args = (place, est) + tuple(h for _, pair in halos for h in pair) + extra
        args += (inner_part, inv, tx, ty) + lateral + (fh, fl) + back
        plan = dict(
            plan, hx=hx, packed=packed, halos=[rng for rng, _ in halos], make_data=not last, pay=not last,
            shifted=last, data_off=shift if last else 0, lane0=hz if last else 0,
        )
        scratch = [(tiles, cx, rows + 16, LANES), (own if last else tiles, 2 * hx, rows, LANES)]
        return call(functools.partial(outer_kernel, plan), outs, args, scratch, 16, 1, scalars=1)

    data_at = mid2 + 8
    spread1 = inner(ext, 0, False, end1 + shift, end0, (bh, bl))
    est_a, data_a, *pays = outer(
        ext, [((0, cut), halo_a)], (weight,), spread1, False,
        dict(low=0, high=mid1, data_base=0, prior=False),
        [shape(tiles, cx, mid1, LANES), shape(tiles, 2 * hx, cut, LANES)] + pay_shapes(mid1),
    )
    halo_c = swap(pays)
    est, data_b, *pays = outer(
        ext, [((0, cut), halo_a), ((cut, end0), halo_b)], (weight, est_a), spread1, False,
        dict(low=mid1, high=end1, data_base=data_at, prior=True),
        [shape(tiles, cx, ceil_to(end1, 8), LANES), shape(tiles, 2 * hx, full - data_at, LANES)] + pay_shapes(end1 - mid1),
    )
    halo_d = swap(pays)
    spread2 = inner(est, shift, True, end2 + shift, end1, (sh, sl))
    (out_a,) = outer(
        est, [((0, mid1), halo_c)], (data_a,), spread2, True,
        dict(low=0, high=mid2, data_base=0, prior=False), [shape(own, cx, mid2, LANES)],
    )
    (out_b,) = outer(
        est, [((0, mid1), halo_c), ((mid1, end1), halo_d)], (data_b,), spread2, True,
        dict(low=mid2, high=end2, data_base=data_at, prior=False), [shape(own, cx, end2 - mid2, LANES)],
    )
    estimate = jnp.concatenate([out_a, out_b], axis=2)
    return estimate.transpose(0, 3, 1, 2).reshape(own * LANES, cx, cy)[:nz]


def solution(mesh):
    in_specs = (P("gz", "sx", "sy"), P("gz"), P(), P(), P(), P())
    out_specs = P("gz", "sx", "sy")
    return jax.shard_map(body, mesh=mesh, in_specs=in_specs, out_specs=out_specs, check_vma=False)
```

```python
import functools

import jax
import jax.numpy as jnp
from jax import lax
from jax.experimental import pallas as pl
from jax.experimental.pallas import tpu as pltpu
from jax.sharding import PartitionSpec as P


ITERS = 2
LANES = 128
TINY = 1e-30
EDGE = 16
STEP = LANES - 2 * EDGE
VMEM = pl.BlockSpec(memory_space=pltpu.VMEM)


def ceil_to(value, unit):
    return -(-value // unit) * unit


def swaps(count):
    return [[(i, i + 1) for i in range(first, count - 1, 2)] for first in (0, 1)]


def both_ways(pairs):
    return pairs + [(j, i) for i, j in pairs]


def lane_is_low():
    return lax.broadcasted_iota(jnp.int32, (8, LANES), 1) < LANES // 2


def spin(value, shift):
    return pltpu.roll(value, shift % LANES, 1) if shift % LANES else value


def regroup(tiles, start):
    lane = lax.broadcasted_iota(jnp.int32, tiles[0].shape, 1)
    out = None
    for t, tile in enumerate(tiles):
        first = 0 if t == 0 else STEP * t + EDGE - start
        stop = LANES if t == len(tiles) - 1 else STEP * (t + 1) + EDGE - start
        if max(first, 0) < min(stop, LANES):
            value = spin(tile, STEP * t - start)
            out = value if out is None else jnp.where(lane >= first, value, out)
    return out


def window(roll_of, start, shape):
    first, off = divmod(start, LANES)
    if off == 0:
        return roll_of(first, 0)
    lane = lax.broadcasted_iota(jnp.int32, shape, 1)
    return jnp.where(lane < LANES - off, roll_of(first, LANES - off), roll_of(first + 1, LANES - off))


def halo_tiles(refs, odd, tiles, packed, hx, rows):
    planes, half = {}, hx // 2

    def plane(index):
        if index not in planes:
            planes[index] = by_side(odd, refs[0][index, rows, :], refs[1][index, rows, :])
        return planes[index]

    spans = contiguous(tiles)
    sides = []
    for side in range(2):
        out = [[] for _ in range(tiles)]
        for p in range(hx):

            def roll_of(k, shift, p=p):
                if packed and k == spans - 1:
                    return spin(plane(hx * k + p % half)[side], shift + (LANES // 2 if p >= half else 0))
                return spin(plane(hx * k + p)[side], shift)

            for t in range(tiles):
                out[t].append(window(roll_of, STEP * t, (8, LANES)))
        sides.append(out)
    return sides


def contiguous(tiles):
    return -(-(LANES + STEP * (tiles - 1)) // LANES)


def pack_both(src, pays, odd, packed, hx, blocks, src_block):
    high = src.shape[1] - hx
    pack_rows(src, pays[0], packed, hx, jnp.where(odd == 1, 0, high), blocks, src_block, 0)
    pack_rows(src, pays[1], packed, hx, jnp.where(odd == 1, high, 0), blocks, src_block, 0)


def by_side(odd, first, second):
    return jnp.where(odd == 1, first, second), jnp.where(odd == 1, second, first)


def pack_rows(src, pay, packed, hx, x0, blocks, src_block, pay_block):
    tiles = src.shape[0]
    spans = contiguous(tiles)
    half = hx // 2

    def step(j, carry):
        here = pl.ds(pl.multiple_of(8 * (j + src_block), 8), 8)
        there = pl.ds(pl.multiple_of(8 * (j + pay_block), 8), 8)
        rows = [[src[t, x0 + p, here, :] for t in range(tiles)] for p in range(hx)]
        for k in range(spans - 1 if packed else spans):
            for p in range(hx):
                pay[hx * k + p, there, :] = regroup(rows[p], LANES * k)
        if packed:
            last = LANES * (spans - 1)
            for p in range(half):
                other = spin(regroup(rows[p + half], last), LANES // 2)
                pay[hx * (spans - 1) + p, there, :] = jnp.where(lane_is_low(), regroup(rows[p], last), other)
        return carry

    lax.fori_loop(0, blocks, step, 0)


def conv_rows(k, v, width):
    out = []
    for x in range(width):
        acc = k[0] * v[x]
        for a in range(1, len(k)):
            acc = acc + k[a] * v[x + a]
        out.append(acc)
    return out


def y_conv(src, taps, reverse, t, width, blocks, emit):
    count = taps.shape[1]
    k = [taps[t, count - 1 - b if reverse else b] for b in range(count)]

    def step(x, carry):
        for j in range(blocks):
            acc = k[0] * src[t, x, 8 * j : 8 * j + 8, :]
            for b in range(1, count):
                acc = acc + k[b] * src[t, x, 8 * j + b : 8 * j + b + 8, :]
            emit(t, x, j, acc)
        return carry

    lax.fori_loop(0, width, step, 0)


def depth_rows(parts, both_ref):
    rows = parts[0].shape[0]
    whole = jnp.concatenate(parts, axis=0)
    hi = whole.astype(jnp.bfloat16)
    lo = (whole - hi.astype(jnp.float32)).astype(jnp.bfloat16)
    res = jnp.dot(jnp.concatenate([hi, lo], axis=1), both_ref[...], preferred_element_type=jnp.float32)
    res = res[:, :LANES] + res[:, LANES:]
    return [res[rows * t : rows * (t + 1)] for t in range(len(parts))]


def x_loop(taps, reverse, first, last, rows_in, rows_out):
    tiles, count = taps.shape[:2]

    def step(j, carry):
        rows = rows_in(j)
        for t in range(tiles):
            k = [taps[t, count - 1 - a if reverse else a] for a in range(count)]
            for n, v in enumerate(rows[t]):
                rows_out(t, j, n, conv_rows(k, v, len(v) - count + 1))
        return carry

    if first < last:
        lax.fori_loop(first, last, step, 0)


def y_group(mid_ref, taps, t, first, group, blocks):
    count = taps.shape[1]
    k = [taps[t, b] for b in range(count)]
    out = []
    for x in [first + n for n in range(group)]:
        for j in range(blocks):
            acc = k[0] * mid_ref[t, x, 8 * j : 8 * j + 8, :]
            for b in range(1, count):
                acc = acc + k[b] * mid_ref[t, x, 8 * j + b : 8 * j + b + 8, :]
            out.append(acc)
    return jnp.concatenate(out, axis=0)


def correct(mid_ref, ty_ref, mats, starts, group, count, rows, data_of, spread_ref):
    forward_ref, back_ref = mats
    tiles = mid_ref.shape[0]
    group = next(n for n in range(group, 0, -1) if count % n == 0 and n * rows % 16 == 0)

    def depth(i, carry):
        first = group * i
        blurred = [y_group(mid_ref, ty_ref, t, first, group, rows // 8) for t in range(tiles)]
        blurred = depth_rows(blurred, forward_ref)
        ratio = [data_of(t, first, group) / jnp.maximum(blurred[t], TINY) for t in range(tiles)]
        spread = depth_rows(ratio, back_ref)
        for t, start in enumerate(starts):
            spread_ref[t, pl.ds(first, group), 0:rows, :] = regroup(spread, start).reshape(group, rows, LANES)
        return carry

    lax.fori_loop(0, count // group, depth, 0)


def inner_kernel(plan, est_ref, obs_ref, w_ref, tx_ref, ty_ref, forward_ref, back_ref, spread_ref, mid_ref):
    tiles, cx = est_ref.shape[:2]
    reach = (tx_ref.shape[1] - 1) // 2
    rows = spread_ref.shape[2]
    first = plan["data_off"] + reach
    count = cx - 2 * reach

    def rows_in(j):
        here = pl.ds(pl.multiple_of(8 * j, 8), 8)
        return [[[est_ref[t, x, here, :] for x in range(cx)]] for t in range(tiles)]

    def rows_out(t, j, n, values):
        here = pl.ds(pl.multiple_of(8 * j, 8), 8)
        for x, value in enumerate(values):
            mid_ref[t, x, here, :] = value

    x_loop(tx_ref, False, 0, -(-plan["need"] // 8), rows_in, rows_out)

    def data_of(t, x, group):
        seen = obs_ref[t, pl.ds(x + reach, group), first : first + rows, :]
        return (seen * w_ref[pl.ds(x + 2 * reach, group), first : first + rows, :]).reshape(group * rows, LANES)

    correct(mid_ref, ty_ref, (forward_ref, back_ref), plan["starts"], 2, count, rows, data_of, spread_ref)


def norm_kernel(plan, place_ref, bands_ref, _, tx_ref, ty_ref, w_ref, out_ref, mid_ref):
    cx, cy, hy, stacks_x, stacks_y = plan
    tiles, count = tx_ref.shape[:2]
    reach = (count - 1) // 2
    width = out_ref.shape[1]
    full = w_ref.shape[1]
    sx, sy = place_ref[0], place_ref[1]
    row = lax.broadcasted_iota(jnp.int32, (full, LANES), 0)
    for x in range(cx + 2 * reach):
        a = (x - reach) // cx
        px = (x - reach) % cx
        gx = sx + a
        value = jnp.zeros((full, LANES), jnp.float32)
        for b, first in ((-1, 0), (0, hy), (1, hy + cy)):
            gy = sy + b
            inside = (gx >= 0) & (gx < stacks_x) & (gy >= 0) & (gy < stacks_y)
            spot = 2 * (jnp.clip(gx, 0, stacks_x - 1) * stacks_y + jnp.clip(gy, 0, stacks_y - 1))
            along = jnp.where(inside, jnp.where(px < bands_ref[spot], 0.5, 1.0), 0.0)
            across = jnp.where(row - hy - b * cy < bands_ref[spot + 1], 0.5, 1.0)
            value = jnp.where(row >= first, across * along, value)
        w_ref[x] = value

    def rows_in(j):
        rows = pl.ds(pl.multiple_of(8 * j, 8), 8)
        return [[[w_ref[x, rows, :] for x in range(width + count - 1)]]] * tiles

    def rows_out(t, j, n, values):
        rows = pl.ds(pl.multiple_of(8 * j, 8), 8)
        for x, value in enumerate(values):
            mid_ref[t, x, rows, :] = value

    x_loop(tx_ref, True, 0, full // 8, rows_in, rows_out)
    for t in range(tiles):
        ky = [ty_ref[t, count - 1 - b] for b in range(count)]

        def ystep(x, carry, ky=ky, t=t):
            for j in range(out_ref.shape[2] // 8):
                at = 8 * j + reach
                acc = ky[0] * mid_ref[t, x, at : at + 8, :]
                for b in range(1, count):
                    acc = acc + ky[b] * mid_ref[t, x, at + b : at + b + 8, :]
                out_ref[t, x, 8 * j : 8 * j + 8, :] = 1.0 / jnp.maximum(acc, TINY)
            return carry

        lax.fori_loop(0, width, ystep, 0)


def band_kernel(psf_ref, _, forward_ref, back_ref):
    taps = psf_ref.shape[0]
    total = psf_ref[0]
    for j in range(1, taps):
        total = total + psf_ref[j]
    shape = (LANES, LANES)
    off = lax.broadcasted_iota(jnp.int32, shape, 1) - lax.broadcasted_iota(jnp.int32, shape, 0) + (taps - 1) // 2
    band, flip = jnp.zeros(shape, jnp.float32), jnp.zeros(shape, jnp.float32)
    for j in range(taps):
        band = jnp.where(off == j, psf_ref[j], band)
        flip = jnp.where(off == taps - 1 - j, psf_ref[j], flip)
    for matrix, ref in ((band, forward_ref), (flip, back_ref)):
        matrix = matrix / jnp.full(shape, total, jnp.float32)
        hi = matrix.astype(jnp.bfloat16)
        ref[:LANES, :LANES] = hi
        ref[LANES:, :LANES] = hi
        ref[:LANES, LANES:] = (matrix - hi.astype(jnp.float32)).astype(jnp.bfloat16)
        ref[LANES:, LANES:] = jnp.zeros(shape, jnp.bfloat16)


def overlapping(tiles, shift, main, halo):
    series = main if halo is None else [halo, *main, halo]
    start = 0 if halo is None else LANES - shift
    return [window(lambda k, turn: spin(series[k], turn), start + STEP * t, main[0].shape) for t in range(tiles)]


def edges_kernel(hy, shift, place_ref, vol_ref, *refs):
    tiles, cx, cy = vol_ref.shape[:3]
    odd = place_ref[1] % 2
    direct = len(refs) > 2
    if direct:
        zones_ref, first_ref, second_ref, first_z, second_z, depth_ref = refs
        lane = lax.broadcasted_iota(jnp.int32, (cy, LANES), 1)
        half = cx // 2

        def outmost(x):
            return pltpu.roll(jnp.where(lane < LANES // 2, vol_ref[0, x], vol_ref[tiles - 1, x]), shift, 1)

        for x in range(half):
            other = pltpu.roll(outmost(x + half), LANES // 2, 1)
            depth_ref[cy * x : cy * x + cy, :] = jnp.where(lane < LANES // 2, outmost(x), other)
        depth_ref[cy * half :, :] = zones_ref[...]
    else:
        first_ref, second_ref = refs
    lane = lax.broadcasted_iota(jnp.int32, (hy, LANES), 1)
    for x in range(cx):
        to = slice(hy * x, hy * x + hy)
        both = []
        for t in range(tiles):
            low, high = vol_ref[t, x, 0:hy, :], vol_ref[t, x, cy - hy : cy, :]
            both.append((jnp.where(odd == 1, low, high), jnp.where(odd == 1, high, low)))
            first_ref[t, to, :], second_ref[t, to, :] = both[-1]
        if direct:
            for n, ref in enumerate((first_z, second_z)):
                ref[to, :] = jnp.where(lane < LANES // 2, both[0][n], both[-1][n])


def assemble_kernel(packed, hx, cut, shift, refs_in, place_ref, *refs):
    vol_ref, first_ref, second_ref = refs[:3]
    depth_ref, first_z, second_z = refs[3:6] if refs_in == 6 else (None,) * 3
    ext_ref, *pays = refs[refs_in:]
    main, cx, cy = vol_ref.shape[:3]
    hy = first_ref.shape[1] // cx
    end = cy + 2 * hy
    odd = place_ref[1] % 2
    half = cx // 2

    for x in range(cx):
        edge = slice(hy * x, hy * x + hy)
        low, high = zip(*[by_side(odd, first_ref[t, edge, :], second_ref[t, edge, :]) for t in range(main)])
        low_z = high_z = halo = None
        if depth_ref is not None:
            low_z, high_z = by_side(odd, first_z[edge, :], second_z[edge, :])
            halo = depth_ref[cy * (x % half) : cy * (x % half) + cy, :]
            halo = spin(halo, (LANES // 2 if x >= half else 0) - shift)
        tiles = ext_ref.shape[0]
        low = overlapping(tiles, shift, list(low), low_z)
        mids = overlapping(tiles, shift, [vol_ref[t, x] for t in range(main)], halo)
        high = overlapping(tiles, shift, list(high), high_z)
        for t in range(ext_ref.shape[0]):
            ext_ref[t, x, 0:hy, :] = low[t]
            ext_ref[t, x, hy : hy + cy, :] = mids[t]
            ext_ref[t, x, hy + cy : end, :] = high[t]
            ext_ref[t, x, end:, :] = jnp.zeros((ext_ref.shape[2] - end, LANES), jnp.float32)
    odd_x = place_ref[0] % 2
    for n in range(2):
        start, stop = (0, cut) if n == 0 else (cut, end)
        pack_both(ext_ref, pays[2 * n : 2 * n + 2], odd_x, packed, hx, -(-(stop - start) // 8), start // 8)


def outer_kernel(plan, place_ref, *refs):
    refs = list(refs)
    odd = place_ref[0] % 2
    take = refs.pop
    est_ref = take(0)
    halos = [(take(0), take(0), first, last) for first, last in plan["halos"]]
    make = plan["make_data"]
    w_ref = take(0) if make else None
    data_in = None if make else take(0)
    prior_ref = take(0) if plan["prior"] else None
    inner_ref, inv_ref, tx_ref, ty_ref, bx_ref, by_ref = [take(0) for _ in range(6)]
    mats = [take(0) for _ in range(2)]
    out_ref = take(0)
    data_ref = take(0) if make else data_in
    pays = [take(0), take(0)] if plan["pay"] else None
    mid_ref, edge_ref = refs
    packed, hx, low, high = plan["packed"], plan["hx"], plan["low"], plan["high"]
    data_base, off, starts = plan["data_base"], plan["data_off"], plan["starts"]
    tiles, cx = est_ref.shape[:2]
    outs = out_ref.shape[0]
    count = tx_ref.shape[1]
    reach = (count - 1) // 2
    rows = edge_ref.shape[2]
    last_block = -(-(high + 4 * reach) // 8)
    data_first = data_base // 8 if make else low // 8

    for lo_ref, hi_ref, first, last in halos:

        def rows_in(j, lo_ref=lo_ref, hi_ref=hi_ref, first=first):
            here = pl.ds(pl.multiple_of(8 * j, 8), 8)
            there = pl.ds(pl.multiple_of(8 * j - first, 8), 8)
            lows, highs = halo_tiles((lo_ref, hi_ref), odd, tiles, packed, hx, there)
            return [
                [
                    lows[t] + [est_ref[t, x, here, :] for x in range(hx)],
                    [est_ref[t, x, here, :] for x in range(cx - hx, cx)] + highs[t],
                ]
                for t in range(tiles)
            ]

        def keep(t, j, pair):
            here = pl.ds(pl.multiple_of(8 * j, 8), 8)
            there = pl.ds(pl.multiple_of(8 * j - data_base, 8), 8)
            for n, v in enumerate(pair):
                for x in range(hx):
                    data_ref[t, hx * n + x, there, :] = w_ref[x + cx * n, here, :] * v[x + reach]

        def rows_in_keep(j, rows_in=rows_in, keep=keep):
            rows = rows_in(j)
            if make:
                for t in range(tiles):
                    keep(t, j, rows[t])
            return rows

        def rows_out(t, j, n, values):
            mid = pl.ds(pl.multiple_of(8 * j - low, 8), 8)
            for x, value in enumerate(values):
                mid_ref[t, hx * n + x, mid, :] = value

        def only_data(j, carry, rows_in=rows_in, keep=keep):
            for t, pair in enumerate(rows_in(j)):
                keep(t, j, pair)
            return carry

        a, b = max(first // 8, data_first), min(last // 8, low // 8)
        if make and a < b:
            lax.fori_loop(a, b, only_data, 0)
        x_loop(tx_ref, False, max(first // 8, low // 8), min(-(-last // 8), last_block), rows_in_keep, rows_out)

    spot0 = low + off + reach - data_base

    def data_of(t, x, group):
        return data_ref[t, pl.ds(x, group), spot0 : spot0 + rows, :].reshape(group * rows, LANES)

    correct(mid_ref, ty_ref, mats, starts, 6, 2 * hx, rows, data_of, edge_ref)

    blocks = -(-(high - low) // 8)

    def back_in(j):
        here = pl.ds(pl.multiple_of(8 * j, 8), 8)
        there = pl.ds(pl.multiple_of(8 * j + low, 8), 8)
        rows = []
        for t in range(outs):
            v = [edge_ref[t, x, here, :] for x in range(hx)]
            v += [inner_ref[t, x, there, :] for x in range(cx - 2 * reach)]
            rows.append([v + [edge_ref[t, x, here, :] for x in range(hx, 2 * hx)]])
        return rows

    def back_out(t, j, n, values):
        here = pl.ds(pl.multiple_of(8 * j, 8), 8)
        for x, value in enumerate(values):
            mid_ref[t, x, here, :] = value

    x_loop(bx_ref, True, 0, rows // 8, back_in, back_out)
    base = low if prior_ref is not None else 0

    def finish(t, x, j, acc):
        at = 8 * j + low + 2 * reach
        scale = 8 * j + low + off
        if starts[t] == STEP * t:
            old = est_ref[t, x, at : at + 8, :] * inv_ref[t, x, scale : scale + 8, :]
        else:
            old = [est_ref[n, x, at : at + 8, :] * inv_ref[n, x, scale : scale + 8, :] for n in range(tiles)]
            old = regroup(old, starts[t])
        to = 8 * j + base
        out_ref[t, x, to : to + 8, :] = old * acc

    for t in range(outs):
        y_conv(mid_ref, by_ref, True, t, cx, blocks, finish)

    if prior_ref is not None:
        for t in range(outs):

            def copy(x, carry, t=t):
                out_ref[t, x, 0:low, :] = prior_ref[t, x, 0:low, :]
                return carry

            lax.fori_loop(0, cx, copy, 0)
    if pays:
        pack_both(out_ref, pays, odd, packed, hx, blocks, base // 8)


def body(observed, zone_of_slice, lateral_x, lateral_y, depth_psf, stitch_width):
    nz, cx, cy = observed.shape
    taps = lateral_x.shape[1]
    reach = (taps - 1) // 2
    zreach = (depth_psf.shape[0] - 1) // 2
    hz = 2 * zreach * ITERS
    hy = 2 * reach * ITERS
    hx = 2 * reach
    slabs = lax.axis_size("gz")
    tiles = 1 + max(0, -(-(nz + 2 * hz - LANES) // STEP))
    spans = contiguous(tiles)
    f32 = jnp.float32

    zones = zone_of_slice.astype(f32)
    pad = spans * LANES - nz - 2 * hz
    direct = slabs == 2 and nz % LANES == 0 and 4 * hz == LANES and cx % 2 == 0
    sx, sy = lax.axis_index("sx"), lax.axis_index("sy")
    place = jnp.stack([sx, sy]).astype(jnp.int32)

    def shape(*dims):
        return jax.ShapeDtypeStruct(dims, f32)

    def call(kernel, out_shape, args, scratch, limit, flops, scalars=0, unread=()):
        moved = sum(a.size * 4 for a in args) + sum(o.size * 4 for o in out_shape)
        spaces = [pltpu.SMEM] * scalars + [pltpu.VMEM] * (len(args) - scalars)
        spaces = [pl.ANY if n in unread else space for n, space in enumerate(spaces)]
        return pl.pallas_call(
            kernel,
            out_shape=out_shape,
            in_specs=[pl.BlockSpec(memory_space=space) for space in spaces],
            out_specs=[VMEM] * len(out_shape),
            scratch_shapes=[pltpu.VMEM(dims, f32) for dims in scratch],
            compiler_params=pltpu.CompilerParams(vmem_limit_bytes=limit << 20),
            cost_estimate=pl.CostEstimate(flops=flops, bytes_accessed=moved, transcendentals=0),
        )(*args)

    rounds_y = swaps(lax.axis_size("sy"))
    if direct:
        volume = observed.reshape(-1, LANES, cx, cy).transpose(0, 2, 3, 1)
        zone_rows = jnp.pad(zones.reshape(-1, LANES), ((0, 8 - nz // LANES), (0, 0)))
        edge, edge_z = shape(volume.shape[0], cx * hy, LANES), shape(cx * hy, LANES)
        first, second, first_z, second_z, borders = call(
            functools.partial(edges_kernel, hy, hz), [edge, edge, edge_z, edge_z, shape(cx // 2 * cy + 8, LANES)],
            (place, volume, zone_rows), [], 8, 1, scalars=1,
        )
        borders = lax.ppermute(borders, "gz", [(0, 1), (1, 0)])
        parts = [volume, lax.ppermute(first, "sy", both_ways(rounds_y[0])), lax.ppermute(second, "sy", both_ways(rounds_y[1]))]
        parts.append(borders)
        for value, pairs in ((first_z, rounds_y[0]), (second_z, rounds_y[1])):
            cross = [(2 * i + g, 2 * j + 1 - g) for i, j in pairs for g in range(2)]
            parts.append(lax.ppermute(value, ("sy", "gz"), both_ways(cross)))
        got_ids = borders[cx // 2 * cy :].reshape(-1)[:nz]
        ids_before, ids_after = got_ids[nz - hz :], got_ids[:hz]
    else:

        def with_zones(part, ids):
            flat = jnp.pad(ids, (0, cx * cy - ids.shape[0]))
            return jnp.concatenate([part, flat.reshape(1, cx, cy)], axis=0)

        ring = [(i, (i + 1) % slabs) for i in range(slabs)]
        first = lax.ppermute(with_zones(observed[nz - hz :], zones[nz - hz :]), "gz", ring)
        second = lax.ppermute(with_zones(observed[:hz], zones[:hz]), "gz", [(j, i) for i, j in ring])
        before, after = first[:hz], second[:hz]
        ids_before, ids_after = first[hz].reshape(-1)[:hz], second[hz].reshape(-1)[:hz]
        volume = jnp.concatenate([before, observed, after, jnp.zeros((pad, cx, cy), f32)], axis=0)
        volume = volume.reshape(spans, LANES, cx, cy).transpose(0, 2, 3, 1)
        edge = shape(spans, cx * hy, LANES)
        first, second = call(
            functools.partial(edges_kernel, hy, hz), [edge, edge], (place, volume), [], 8, 1, scalars=1
        )
        parts = [volume, lax.ppermute(first, "sy", both_ways(rounds_y[0])), lax.ppermute(second, "sy", both_ways(rounds_y[1]))]
    ids = jnp.concatenate([ids_before, zones, ids_after, jnp.full((pad,), -1.0, f32)])
    ids = jnp.concatenate([ids[STEP * t : STEP * t + LANES] for t in range(tiles)])

    def lanes_of(kernels, names):
        match = (names[None, :] == jnp.arange(lateral_x.shape[0], dtype=f32)[:, None]).astype(f32)
        table = jnp.sum(match[:, None, :] * kernels[:, :, None], axis=0)
        table = table.reshape(taps, -1, 1, LANES).transpose(1, 0, 2, 3)
        return jnp.broadcast_to(table, (table.shape[0], taps, 8, LANES))

    tx, ty = lanes_of(lateral_x, ids), lanes_of(lateral_y, ids)
    own = ceil_to(nz, LANES) // LANES
    own_ids = jnp.concatenate([zones, jnp.full((own * LANES - nz,), -1.0, f32)])
    tx_own, ty_own = lanes_of(lateral_x, own_ids), lanes_of(lateral_y, own_ids)

    wide = cx + 2 * reach
    packed = LANES + STEP * (tiles - 1) - (spans - 1) * LANES <= LANES // 2
    planes = hx * (spans - 1) + hx // 2 if packed else hx * spans
    end0, end1, end2 = cy + 2 * hy, cy + 2 * hy - 4 * reach, cy
    mid1 = ceil_to(end1 // 2, 8) + 8
    mid2 = mid1 - ceil_to(4 * reach, 8)
    cut = ceil_to(mid1 + 4 * reach, 8)
    rounds_x = [both_ways(pairs) for pairs in swaps(lax.axis_size("sx"))]
    full = ceil_to(cy + 2 * hy + reach, 8)

    def pay_shapes(rows):
        return [shape(planes, ceil_to(rows, 8), LANES)] * 2

    def swap(pays):
        got = []
        for n in range(2):
            got.append(lax.ppermute(pays[n], "sx", rounds_x[n]))
        return got

    ext, *pays = call(
        functools.partial(assemble_kernel, packed, hx, cut, hz, len(parts)),
        [shape(tiles, cx, full, LANES)] + pay_shapes(cut) + pay_shapes(end0 - cut),
        (place, *parts), [], 8, 1, scalars=1,
    )
    halo_a = swap(pays[:2])
    halo_b = swap(pays[2:])

    forward, back = call(
        band_kernel, [jax.ShapeDtypeStruct((2 * LANES, 2 * LANES), jnp.bfloat16)] * 2,
        (depth_psf, pays[-1]), [], 8, 1, scalars=1, unread=(1,),
    )
    stacks_x, stacks_y = stitch_width.shape[:2]
    weight, inv = call(
        functools.partial(norm_kernel, (cx, cy, hy, stacks_x, stacks_y)),
        [shape(wide, full, LANES), shape(tiles, cx, ceil_to(end1, 8), LANES)],
        (place, stitch_width.reshape(-1), pays[-1], tx, ty), [(tiles, cx, full, LANES)], 10, 1, scalars=2, unread=(2,),
    )
    shift = 2 * reach

    overlap = tuple(STEP * t for t in range(tiles))
    alone = tuple(hz + LANES * t for t in range(own))

    def inner(est, data_off, starts, rows, need):
        plan = dict(data_off=data_off, starts=starts, need=need)
        rows = ceil_to(rows, 8)
        return call(
            functools.partial(inner_kernel, plan), [shape(len(starts), cx - shift, rows, LANES)],
            (est, ext, weight, tx, ty, forward, back), [(tiles, cx - shift, rows + 16, LANES)], 24, 1,
        )[0]

    def outer(est, halos, extra, inner_part, last, plan, outs):
        rows = ceil_to(plan["high"] - plan["low"] + 2 * reach, 8)
        lateral = (tx_own, ty_own) if last else (tx, ty)
        starts = alone if last else overlap
        args = (place, est) + tuple(h for _, pair in halos for h in pair) + extra
        args += (inner_part, inv, tx, ty) + lateral + (forward, back)
        plan = dict(
            plan, hx=hx, packed=packed, halos=[rng for rng, _ in halos], make_data=not last, pay=not last,
            starts=starts, data_off=shift if last else 0,
        )
        scratch = [(tiles, cx, rows + 16, LANES), (len(starts), 2 * hx, rows, LANES)]
        return call(functools.partial(outer_kernel, plan), outs, args, scratch, 16, 1, scalars=1)

    data_at = mid2 + 8
    spread1 = inner(ext, 0, overlap, end1 + shift, end0)
    est_a, data_a, *pays = outer(
        ext, [((0, cut), halo_a)], (weight,), spread1, False,
        dict(low=0, high=mid1, data_base=0, prior=False),
        [shape(tiles, cx, mid1, LANES), shape(tiles, 2 * hx, cut, LANES)] + pay_shapes(mid1),
    )
    halo_c = swap(pays)
    est, data_b, *pays = outer(
        ext, [((0, cut), halo_a), ((cut, end0), halo_b)], (weight, est_a), spread1, False,
        dict(low=mid1, high=end1, data_base=data_at, prior=True),
        [shape(tiles, cx, ceil_to(end1, 8), LANES), shape(tiles, 2 * hx, full - data_at, LANES)] + pay_shapes(end1 - mid1),
    )
    halo_d = swap(pays)
    spread2 = inner(est, shift, alone, end2 + shift, end1)
    (out_a,) = outer(
        est, [((0, mid1), halo_c)], (data_a,), spread2, True,
        dict(low=0, high=mid2, data_base=0, prior=False), [shape(own, cx, mid2, LANES)],
    )
    (out_b,) = outer(
        est, [((0, mid1), halo_c), ((mid1, end1), halo_d)], (data_b,), spread2, True,
        dict(low=mid2, high=end2, data_base=data_at, prior=False), [shape(own, cx, end2 - mid2, LANES)],
    )
    estimate = jnp.concatenate([out_a, out_b], axis=2)
    return estimate.transpose(0, 3, 1, 2).reshape(own * LANES, cx, cy)[:nz]


def solution(mesh):
    in_specs = (P("gz", "sx", "sy"), P("gz"), P(), P(), P(), P())
    out_specs = P("gz", "sx", "sy")
    return jax.shard_map(body, mesh=mesh, in_specs=in_specs, out_specs=out_specs, check_vma=False)
```

```python
import functools

import jax
import jax.numpy as jnp
from jax import lax
from jax.experimental import pallas as pl
from jax.experimental.pallas import tpu as pltpu
from jax.sharding import PartitionSpec as P


ITERS = 2
LANES = 128
TINY = 1e-30
EDGE = 16
STEP = LANES - 2 * EDGE
LAP = LANES - STEP
VMEM = pl.BlockSpec(memory_space=pltpu.VMEM)


def ceil_to(value, unit):
    return -(-value // unit) * unit


def swaps(count):
    return [[(i, i + 1) for i in range(first, count - 1, 2)] for first in (0, 1)]


def both_ways(pairs):
    return pairs + [(j, i) for i, j in pairs]


def spin(value, shift):
    return pltpu.roll(value, shift % LANES, 1) if shift % LANES else value


def regroup(tiles, start):
    lane = lax.broadcasted_iota(jnp.int32, tiles[0].shape, 1)
    out = None
    for t, tile in enumerate(tiles):
        first = 0 if t == 0 else STEP * t + EDGE - start
        stop = LANES if t == len(tiles) - 1 else STEP * (t + 1) + EDGE - start
        if max(first, 0) < min(stop, LANES):
            value = spin(tile, STEP * t - start)
            out = value if out is None else jnp.where(lane >= first, value, out)
    return out


def halo_tiles(refs, odd, tiles, packed, hx, rows):
    planes, half = {}, hx // 2

    def plane(index, side):
        if index not in planes:
            planes[index] = by_side(odd, refs[0][index, rows, :], refs[1][index, rows, :])
        return planes[index][side]

    sides = []
    lane = lax.broadcasted_iota(jnp.int32, (8, LANES), 1)
    for side in range(2):
        out = [[] for _ in range(tiles)]
        for p in range(hx):
            if not packed:
                for t in range(tiles):
                    out[t].append(plane(hx * t + p, side))
                continue
            one, two, end = plane(p, side), plane(hx + p, side), plane(2 * hx + p % half, side)
            out[0].append(one)
            out[1].append(jnp.where(lane < LAP, spin(one, LAP), two))
            out[2].append(jnp.where(lane < 2 * LAP, spin(two, LAP), spin(end, LANES // 2 if p >= half else 0)))
        sides.append(out)
    return sides


def pack_both(src, pays, odd, packed, hx, blocks, src_block):
    high = src.shape[1] - hx
    pack_rows(src, pays[0], packed, hx, jnp.where(odd == 1, 0, high), blocks, src_block, 0)
    pack_rows(src, pays[1], packed, hx, jnp.where(odd == 1, high, 0), blocks, src_block, 0)


def by_side(odd, first, second):
    return jnp.where(odd == 1, first, second), jnp.where(odd == 1, second, first)


def pack_rows(src, pay, packed, hx, x0, blocks, src_block, pay_block):
    tiles = src.shape[0]
    half = hx // 2

    def step(j, carry):
        here = pl.ds(pl.multiple_of(8 * (j + src_block), 8), 8)
        there = pl.ds(pl.multiple_of(8 * (j + pay_block), 8), 8)
        lane = lax.broadcasted_iota(jnp.int32, (8, LANES), 1)
        for p in range(hx):
            for t in range(1 if packed else tiles):
                pay[hx * t + p, there, :] = src[t, x0 + p, here, :]
            if packed:
                last = src[2, x0 + p, here, :]
                pay[hx + p, there, :] = jnp.where(lane < LAP, spin(last, -LAP), src[1, x0 + p, here, :])
                if p < half:
                    other = spin(src[2, x0 + p + half, here, :], LANES // 2)
                    pay[2 * hx + p, there, :] = jnp.where(lane < LANES // 2, other, last)
        return carry

    lax.fori_loop(0, blocks, step, 0)


def conv_rows(k, v, width):
    out = []
    for x in range(width):
        acc = k[0] * v[x]
        for a in range(1, len(k)):
            acc = acc + k[a] * v[x + a]
        out.append(acc)
    return out


def y_conv(src, taps, reverse, t, width, blocks, emit):
    count = taps.shape[1]
    k = [taps[t, count - 1 - b if reverse else b] for b in range(count)]

    def step(x, carry):
        for j in range(blocks):
            acc = k[0] * src[t, x, 8 * j : 8 * j + 8, :]
            for b in range(1, count):
                acc = acc + k[b] * src[t, x, 8 * j + b : 8 * j + b + 8, :]
            emit(t, x, j, acc)
        return carry

    lax.fori_loop(0, width, step, 0)


def halves(parts):
    whole = jnp.concatenate(parts, axis=0)
    hi = whole.astype(jnp.bfloat16)
    return jnp.concatenate([hi, (whole - hi.astype(jnp.float32)).astype(jnp.bfloat16)], axis=1)


def depth_sums(pair, matrix):
    res = jnp.dot(pair, matrix, preferred_element_type=jnp.float32)
    return res[:, :LANES] + res[:, LANES:]


def own_pairs(tiles, starts):
    pairs = []
    for k, start in enumerate(starts):
        for t in range(tiles):
            first = max(0 if t == 0 else STEP * t + EDGE - start, 0)
            stop = min(LANES if t == tiles - 1 else STEP * (t + 1) + EDGE - start, LANES)
            if first < stop:
                pairs.append((k, t, first, stop))
    return pairs


def x_loop(taps, reverse, first, last, rows_in, rows_out):
    tiles, count = taps.shape[:2]

    def step(j, carry):
        rows = rows_in(j)
        for t in range(tiles):
            k = [taps[t, count - 1 - a if reverse else a] for a in range(count)]
            for n, v in enumerate(rows[t]):
                rows_out(t, j, n, conv_rows(k, v, len(v) - count + 1))
        return carry

    if first < last:
        lax.fori_loop(first, last, step, 0)


def y_group(mid_ref, taps, t, first, group, blocks):
    count = taps.shape[1]
    k = [taps[t, b] for b in range(count)]
    out = []
    for x in [first + n for n in range(group)]:
        for j in range(blocks):
            acc = k[0] * mid_ref[t, x, 8 * j : 8 * j + 8, :]
            for b in range(1, count):
                acc = acc + k[b] * mid_ref[t, x, 8 * j + b : 8 * j + b + 8, :]
            out.append(acc)
    return jnp.concatenate(out, axis=0)


def correct(mid_ref, ty_ref, mats, starts, group, count, rows, data_of, spread_ref):
    forward_ref, back_ref, *more = mats
    tiles = mid_ref.shape[0]
    group = next(n for n in range(group, 0, -1) if count % n == 0 and n * rows % 16 == 0)

    def depth(i, carry):
        first = group * i
        blurred = [y_group(mid_ref, ty_ref, t, first, group, rows // 8) for t in range(tiles)]
        size = group * rows
        blurred = depth_sums(halves(blurred), forward_ref[...])
        ratio = []
        for t in range(tiles):
            ratio.append(data_of(t, first, group) / jnp.maximum(blurred[size * t : size * (t + 1)], TINY))
        ratio = halves(ratio)
        if starts[0] == 0:
            spread = depth_sums(ratio, back_ref[...])
            spread = [spread[size * t : size * (t + 1)] for t in range(tiles)]
            if tiles > 1:
                ends = depth_sums(ratio, more[0][...])
                ends = [ends[size * t : size * (t + 1)] for t in range(tiles)]
                lane = lax.broadcasted_iota(jnp.int32, (size, LANES), 1)
                for t in range(tiles):
                    if t > 0:
                        spread[t] = jnp.where(lane < EDGE, ends[t - 1], spread[t])
                    if t < tiles - 1:
                        spread[t] = jnp.where(lane >= LANES - EDGE, ends[t + 1], spread[t])
        else:
            spread = [None] * len(starts)
            for n, (k, t, _, _) in enumerate(own_pairs(tiles, starts)):
                part = depth_sums(ratio[size * t : size * (t + 1)], back_ref[n])
                spread[k] = part if spread[k] is None else spread[k] + part
        for t, value in enumerate(spread):
            spread_ref[t, pl.ds(first, group), 0:rows, :] = value.reshape(group, rows, LANES)
        return carry

    lax.fori_loop(0, count // group, depth, 0)


def inner_kernel(plan, est_ref, obs_ref, w_ref, tx_ref, ty_ref, *refs):
    *mats, spread_ref, mid_ref = refs
    tiles, cx = est_ref.shape[:2]
    reach = (tx_ref.shape[1] - 1) // 2
    rows = spread_ref.shape[2]
    first = plan["data_off"] + reach
    count = cx - 2 * reach

    def rows_in(j):
        here = pl.ds(pl.multiple_of(8 * j, 8), 8)
        return [[[est_ref[t, x, here, :] for x in range(cx)]] for t in range(tiles)]

    def rows_out(t, j, n, values):
        here = pl.ds(pl.multiple_of(8 * j, 8), 8)
        for x, value in enumerate(values):
            mid_ref[t, x, here, :] = value

    x_loop(tx_ref, False, 0, -(-plan["need"] // 8), rows_in, rows_out)

    def data_of(t, x, group):
        seen = obs_ref[t, pl.ds(x + reach, group), first : first + rows, :]
        return (seen * w_ref[pl.ds(x + 2 * reach, group), first : first + rows, :]).reshape(group * rows, LANES)

    correct(mid_ref, ty_ref, mats, plan["starts"], 2, count, rows, data_of, spread_ref)


def norm_kernel(plan, place_ref, bands_ref, _, tx_ref, ty_ref, w_ref, out_ref, mid_ref):
    cx, cy, hy, stacks_x, stacks_y = plan
    tiles, count = tx_ref.shape[:2]
    reach = (count - 1) // 2
    width = out_ref.shape[1]
    full = w_ref.shape[1]
    sx, sy = place_ref[0], place_ref[1]
    row = lax.broadcasted_iota(jnp.int32, (full, LANES), 0)
    for x in range(cx + 2 * reach):
        a = (x - reach) // cx
        px = (x - reach) % cx
        gx = sx + a
        value = jnp.zeros((full, LANES), jnp.float32)
        for b, first in ((-1, 0), (0, hy), (1, hy + cy)):
            gy = sy + b
            inside = (gx >= 0) & (gx < stacks_x) & (gy >= 0) & (gy < stacks_y)
            spot = 2 * (jnp.clip(gx, 0, stacks_x - 1) * stacks_y + jnp.clip(gy, 0, stacks_y - 1))
            along = jnp.where(inside, jnp.where(px < bands_ref[spot], 0.5, 1.0), 0.0)
            across = jnp.where(row - hy - b * cy < bands_ref[spot + 1], 0.5, 1.0)
            value = jnp.where(row >= first, across * along, value)
        w_ref[x] = value

    def rows_in(j):
        rows = pl.ds(pl.multiple_of(8 * j, 8), 8)
        return [[[w_ref[x, rows, :] for x in range(width + count - 1)]]] * tiles

    def rows_out(t, j, n, values):
        rows = pl.ds(pl.multiple_of(8 * j, 8), 8)
        for x, value in enumerate(values):
            mid_ref[t, x, rows, :] = value

    x_loop(tx_ref, True, 0, full // 8, rows_in, rows_out)
    for t in range(tiles):
        ky = [ty_ref[t, count - 1 - b] for b in range(count)]

        def ystep(x, carry, ky=ky, t=t):
            for j in range(out_ref.shape[2] // 8):
                at = 8 * j + reach
                acc = ky[0] * mid_ref[t, x, at : at + 8, :]
                for b in range(1, count):
                    acc = acc + ky[b] * mid_ref[t, x, at + b : at + b + 8, :]
                out_ref[t, x, 8 * j : 8 * j + 8, :] = 1.0 / jnp.maximum(acc, TINY)
            return carry

        lax.fori_loop(0, width, ystep, 0)


def band_kernel(pairs, starts, psf_ref, _, forward_ref, back_ref, ends_ref, own_ref):
    taps = psf_ref.shape[0]
    total = psf_ref[0]
    for j in range(1, taps):
        total = total + psf_ref[j]
    shape = (LANES, LANES)
    row = lax.broadcasted_iota(jnp.int32, shape, 0)
    lane = lax.broadcasted_iota(jnp.int32, shape, 1)

    def fill(ref, target, sign, keep):
        off = sign * (target - row) + (taps - 1) // 2
        matrix = jnp.zeros(shape, jnp.float32)
        for j in range(taps):
            matrix = jnp.where(off == j, psf_ref[j], matrix)
        matrix = matrix / jnp.full(shape, total, jnp.float32)
        if keep is not None:
            matrix = jnp.where(keep, matrix, 0.0)
        hi = matrix.astype(jnp.bfloat16)
        ref[:LANES, :LANES] = hi
        ref[LANES:, :LANES] = hi
        ref[:LANES, LANES:] = (matrix - hi.astype(jnp.float32)).astype(jnp.bfloat16)
        ref[LANES:, LANES:] = jnp.zeros(shape, jnp.bfloat16)

    fill(forward_ref, lane, 1, None)
    fill(back_ref, lane, -1, None)
    side = (lane < EDGE) | (lane >= LANES - EDGE)
    fill(ends_ref, jnp.where(lane < EDGE, lane + STEP, lane - STEP), -1, side)
    for n, (k, t, first, stop) in enumerate(pairs):
        fill(own_ref.at[n], lane + starts[k] - STEP * t, -1, (lane >= first) & (lane < stop))


def with_halo(parts, halo, turned, width):
    if halo is None:
        return parts
    lane = lax.broadcasted_iota(jnp.int32, halo.shape, 1)
    first = jnp.where(lane < width, halo, parts[0])
    last = jnp.where(lane >= LANES - width, turned, parts[-1])
    return [first, *parts[1:-1], last]


def edges_kernel(hy, width, turn, place_ref, vol_ref, *refs):
    tiles, cx, cy = vol_ref.shape[:3]
    odd = place_ref[1] % 2
    direct = len(refs) > 2
    if direct:
        zones_ref, first_ref, second_ref, first_z, second_z, depth_ref = refs
        lane = lax.broadcasted_iota(jnp.int32, (cy, LANES), 1)
        half = cx // 2

        def outmost(low, high, at):
            return jnp.where(at < width, spin(high, -turn), low)

        for x in range(half):
            one, two = [outmost(vol_ref[0, n], vol_ref[tiles - 1, n], lane) for n in (x, x + half)]
            depth_ref[cy * x : cy * x + cy, :] = jnp.where(lane < LANES // 2, one, spin(two, LANES // 2))
        depth_ref[cy * half :, :] = zones_ref[...]
    else:
        first_ref, second_ref = refs
    lane = lax.broadcasted_iota(jnp.int32, (hy, LANES), 1)
    for x in range(cx):
        to = slice(hy * x, hy * x + hy)
        both = []
        for t in range(tiles):
            low, high = vol_ref[t, x, 0:hy, :], vol_ref[t, x, cy - hy : cy, :]
            both.append((jnp.where(odd == 1, low, high), jnp.where(odd == 1, high, low)))
            first_ref[t, to, :], second_ref[t, to, :] = both[-1]
        if direct:
            for n, ref in enumerate((first_z, second_z)):
                ref[to, :] = outmost(both[0][n], both[-1][n], lane)


def assemble_kernel(packed, hx, cut, shift, refs_in, place_ref, *refs):
    vol_ref, first_ref, second_ref = refs[:3]
    depth_ref, first_z, second_z = refs[3:6] if refs_in == 6 else (None,) * 3
    ext_ref, *pays = refs[refs_in:]
    main, cx, cy = vol_ref.shape[:3]
    hy = first_ref.shape[1] // cx
    end = cy + 2 * hy
    odd = place_ref[1] % 2
    half = cx // 2

    tiles = ext_ref.shape[0]
    for x in range(cx):
        edge = slice(hy * x, hy * x + hy)
        low, high = zip(*[by_side(odd, first_ref[t, edge, :], second_ref[t, edge, :]) for t in range(main)])
        mids = [vol_ref[t, x] for t in range(main)]
        if depth_ref is not None:
            low_z, high_z = by_side(odd, first_z[edge, :], second_z[edge, :])
            low = with_halo(low, low_z, spin(low_z, LANES // 2), shift)
            high = with_halo(high, high_z, spin(high_z, LANES // 2), shift)
            halo = depth_ref[cy * (x % half) : cy * (x % half) + cy, :]
            pair = (halo, spin(halo, LANES // 2))
            mids = with_halo(mids, *(pair if x < half else pair[::-1]), shift)
        for t in range(tiles):
            ext_ref[t, x, 0:hy, :] = low[t]
            ext_ref[t, x, hy : hy + cy, :] = mids[t]
            ext_ref[t, x, hy + cy : end, :] = high[t]
            ext_ref[t, x, end:, :] = jnp.zeros((ext_ref.shape[2] - end, LANES), jnp.float32)
    odd_x = place_ref[0] % 2
    for n in range(2):
        start, stop = (0, cut) if n == 0 else (cut, end)
        pack_both(ext_ref, pays[2 * n : 2 * n + 2], odd_x, packed, hx, -(-(stop - start) // 8), start // 8)


def outer_kernel(plan, place_ref, *refs):
    refs = list(refs)
    odd = place_ref[0] % 2
    take = refs.pop
    est_ref = take(0)
    halos = [(take(0), take(0), first, last) for first, last in plan["halos"]]
    make = plan["make_data"]
    w_ref = take(0) if make else None
    data_in = None if make else take(0)
    prior_ref = take(0) if plan["prior"] else None
    inner_ref, inv_ref, tx_ref, ty_ref, bx_ref, by_ref = [take(0) for _ in range(6)]
    mats = [take(0) for _ in range(plan["mats"])]
    out_ref = take(0)
    data_ref = take(0) if make else data_in
    pays = [take(0), take(0)] if plan["pay"] else None
    mid_ref, edge_ref = refs
    packed, hx, low, high = plan["packed"], plan["hx"], plan["low"], plan["high"]
    data_base, off, starts = plan["data_base"], plan["data_off"], plan["starts"]
    tiles, cx = est_ref.shape[:2]
    outs = out_ref.shape[0]
    count = tx_ref.shape[1]
    reach = (count - 1) // 2
    rows = edge_ref.shape[2]
    last_block = -(-(high + 4 * reach) // 8)
    data_first = data_base // 8 if make else low // 8

    for lo_ref, hi_ref, first, last in halos:

        def rows_in(j, lo_ref=lo_ref, hi_ref=hi_ref, first=first):
            here = pl.ds(pl.multiple_of(8 * j, 8), 8)
            there = pl.ds(pl.multiple_of(8 * j - first, 8), 8)
            lows, highs = halo_tiles((lo_ref, hi_ref), odd, tiles, packed, hx, there)
            return [
                [
                    lows[t] + [est_ref[t, x, here, :] for x in range(hx)],
                    [est_ref[t, x, here, :] for x in range(cx - hx, cx)] + highs[t],
                ]
                for t in range(tiles)
            ]

        def keep(t, j, pair):
            here = pl.ds(pl.multiple_of(8 * j, 8), 8)
            there = pl.ds(pl.multiple_of(8 * j - data_base, 8), 8)
            for n, v in enumerate(pair):
                for x in range(hx):
                    data_ref[t, hx * n + x, there, :] = w_ref[x + cx * n, here, :] * v[x + reach]

        def rows_in_keep(j, rows_in=rows_in, keep=keep):
            rows = rows_in(j)
            if make:
                for t in range(tiles):
                    keep(t, j, rows[t])
            return rows

        def rows_out(t, j, n, values):
            mid = pl.ds(pl.multiple_of(8 * j - low, 8), 8)
            for x, value in enumerate(values):
                mid_ref[t, hx * n + x, mid, :] = value

        def only_data(j, carry, rows_in=rows_in, keep=keep):
            for t, pair in enumerate(rows_in(j)):
                keep(t, j, pair)
            return carry

        a, b = max(first // 8, data_first), min(last // 8, low // 8)
        if make and a < b:
            lax.fori_loop(a, b, only_data, 0)
        x_loop(tx_ref, False, max(first // 8, low // 8), min(-(-last // 8), last_block), rows_in_keep, rows_out)

    spot0 = low + off + reach - data_base

    def data_of(t, x, group):
        return data_ref[t, pl.ds(x, group), spot0 : spot0 + rows, :].reshape(group * rows, LANES)

    correct(mid_ref, ty_ref, mats, starts, 6, 2 * hx, rows, data_of, edge_ref)

    blocks = -(-(high - low) // 8)

    def back_in(j):
        here = pl.ds(pl.multiple_of(8 * j, 8), 8)
        there = pl.ds(pl.multiple_of(8 * j + low, 8), 8)
        rows = []
        for t in range(outs):
            v = [edge_ref[t, x, here, :] for x in range(hx)]
            v += [inner_ref[t, x, there, :] for x in range(cx - 2 * reach)]
            rows.append([v + [edge_ref[t, x, here, :] for x in range(hx, 2 * hx)]])
        return rows

    def back_out(t, j, n, values):
        here = pl.ds(pl.multiple_of(8 * j, 8), 8)
        for x, value in enumerate(values):
            mid_ref[t, x, here, :] = value

    x_loop(bx_ref, True, 0, rows // 8, back_in, back_out)
    base = low if prior_ref is not None else 0

    def finish(t, x, j, acc):
        at = 8 * j + low + 2 * reach
        scale = 8 * j + low + off
        if starts[t] == STEP * t:
            old = est_ref[t, x, at : at + 8, :] * inv_ref[t, x, scale : scale + 8, :]
        else:
            old = [est_ref[n, x, at : at + 8, :] * inv_ref[n, x, scale : scale + 8, :] for n in range(tiles)]
            old = regroup(old, starts[t])
        to = 8 * j + base
        out_ref[t, x, to : to + 8, :] = old * acc

    for t in range(outs):
        y_conv(mid_ref, by_ref, True, t, cx, blocks, finish)

    if prior_ref is not None:
        for t in range(outs):

            def copy(x, carry, t=t):
                out_ref[t, x, 0:low, :] = prior_ref[t, x, 0:low, :]
                return carry

            lax.fori_loop(0, cx, copy, 0)
    if pays:
        pack_both(out_ref, pays, odd, packed, hx, blocks, base // 8)


def body(observed, zone_of_slice, lateral_x, lateral_y, depth_psf, stitch_width):
    nz, cx, cy = observed.shape
    taps = lateral_x.shape[1]
    reach = (taps - 1) // 2
    zreach = (depth_psf.shape[0] - 1) // 2
    hz = 2 * zreach * ITERS
    hy = 2 * reach * ITERS
    hx = 2 * reach
    slabs = lax.axis_size("gz")
    tiles = 1 + max(0, -(-(nz + 2 * hz - LANES) // STEP))
    f32 = jnp.float32

    zones = zone_of_slice.astype(f32)
    pad = LANES + STEP * (tiles - 1) - nz - 2 * hz
    direct = slabs == 2 and tiles > 1 and pad == 0 and nz % LANES == 0 and hz == LAP and cx % 2 == 0
    sx, sy = lax.axis_index("sx"), lax.axis_index("sy")
    place = jnp.stack([sx, sy]).astype(jnp.int32)

    def shape(*dims):
        return jax.ShapeDtypeStruct(dims, f32)

    def call(kernel, out_shape, args, scratch, limit, flops, scalars=0, unread=()):
        moved = sum(a.size * 4 for a in args) + sum(o.size * 4 for o in out_shape)
        spaces = [pltpu.SMEM] * scalars + [pltpu.VMEM] * (len(args) - scalars)
        spaces = [pl.ANY if n in unread else space for n, space in enumerate(spaces)]
        return pl.pallas_call(
            kernel,
            out_shape=out_shape,
            in_specs=[pl.BlockSpec(memory_space=space) for space in spaces],
            out_specs=[VMEM] * len(out_shape),
            scratch_shapes=[pltpu.VMEM(dims, f32) for dims in scratch],
            compiler_params=pltpu.CompilerParams(vmem_limit_bytes=limit << 20),
            cost_estimate=pl.CostEstimate(flops=flops, bytes_accessed=moved, transcendentals=0),
        )(*args)

    def lanes_first(value):
        parts = jnp.stack([value[STEP * t : STEP * t + LANES] for t in range(tiles)])
        return parts.transpose(0, 2, 3, 1)

    rounds_y = swaps(lax.axis_size("sy"))
    if direct:
        volume = lanes_first(jnp.pad(observed, ((hz, hz), (0, 0), (0, 0))))
        zone_rows = jnp.pad(zones.reshape(-1, LANES), ((0, 8 - nz // LANES), (0, 0)))
        edge, edge_z = shape(volume.shape[0], cx * hy, LANES), shape(cx * hy, LANES)
        first, second, first_z, second_z, borders = call(
            functools.partial(edges_kernel, hy, hz, nz - STEP * (tiles - 1)), [edge, edge, edge_z, edge_z, shape(cx // 2 * cy + 8, LANES)],
            (place, volume, zone_rows), [], 8, 1, scalars=1,
        )
        borders = lax.ppermute(borders, "gz", [(0, 1), (1, 0)])
        parts = [volume, lax.ppermute(first, "sy", both_ways(rounds_y[0])), lax.ppermute(second, "sy", both_ways(rounds_y[1]))]
        parts.append(borders)
        for value, pairs in ((first_z, rounds_y[0]), (second_z, rounds_y[1])):
            cross = [(2 * i + g, 2 * j + 1 - g) for i, j in pairs for g in range(2)]
            parts.append(lax.ppermute(value, ("sy", "gz"), both_ways(cross)))
        got_ids = borders[cx // 2 * cy :].reshape(-1)[:nz]
        ids_before, ids_after = got_ids[nz - hz :], got_ids[:hz]
    else:

        def with_zones(part, ids):
            flat = jnp.pad(ids, (0, cx * cy - ids.shape[0]))
            return jnp.concatenate([part, flat.reshape(1, cx, cy)], axis=0)

        ring = [(i, (i + 1) % slabs) for i in range(slabs)]
        first = lax.ppermute(with_zones(observed[nz - hz :], zones[nz - hz :]), "gz", ring)
        second = lax.ppermute(with_zones(observed[:hz], zones[:hz]), "gz", [(j, i) for i, j in ring])
        before, after = first[:hz], second[:hz]
        ids_before, ids_after = first[hz].reshape(-1)[:hz], second[hz].reshape(-1)[:hz]
        volume = lanes_first(jnp.concatenate([before, observed, after, jnp.zeros((pad, cx, cy), f32)], axis=0))
        edge = shape(tiles, cx * hy, LANES)
        first, second = call(
            functools.partial(edges_kernel, hy, hz, nz - STEP * (tiles - 1)), [edge, edge], (place, volume), [], 8, 1, scalars=1
        )
        parts = [volume, lax.ppermute(first, "sy", both_ways(rounds_y[0])), lax.ppermute(second, "sy", both_ways(rounds_y[1]))]
    ids = jnp.concatenate([ids_before, zones, ids_after, jnp.full((pad,), -1.0, f32)])
    ids = jnp.concatenate([ids[STEP * t : STEP * t + LANES] for t in range(tiles)])

    def lanes_of(kernels, names):
        match = (names[None, :] == jnp.arange(lateral_x.shape[0], dtype=f32)[:, None]).astype(f32)
        table = jnp.sum(match[:, None, :] * kernels[:, :, None], axis=0)
        table = table.reshape(taps, -1, 1, LANES).transpose(1, 0, 2, 3)
        return jnp.broadcast_to(table, (table.shape[0], taps, 8, LANES))

    tx, ty = lanes_of(lateral_x, ids), lanes_of(lateral_y, ids)
    own = ceil_to(nz, LANES) // LANES
    own_ids = jnp.concatenate([zones, jnp.full((own * LANES - nz,), -1.0, f32)])
    tx_own, ty_own = lanes_of(lateral_x, own_ids), lanes_of(lateral_y, own_ids)

    wide = cx + 2 * reach
    packed = tiles == 3
    planes = 2 * hx + hx // 2 if packed else hx * tiles
    end0, end1, end2 = cy + 2 * hy, cy + 2 * hy - 4 * reach, cy
    mid1 = ceil_to(end1 // 2, 8) + 8
    mid2 = mid1 - ceil_to(4 * reach, 8)
    cut = ceil_to(mid1 + 4 * reach, 8)
    rounds_x = [both_ways(pairs) for pairs in swaps(lax.axis_size("sx"))]
    full = ceil_to(cy + 2 * hy + reach, 8)

    def pay_shapes(rows):
        return [shape(planes, ceil_to(rows, 8), LANES)] * 2

    def swap(pays):
        got = []
        for n in range(2):
            got.append(lax.ppermute(pays[n], "sx", rounds_x[n]))
        return got

    ext, *pays = call(
        functools.partial(assemble_kernel, packed, hx, cut, hz, len(parts)),
        [shape(tiles, cx, full, LANES)] + pay_shapes(cut) + pay_shapes(end0 - cut),
        (place, *parts), [], 8, 1, scalars=1,
    )
    halo_a = swap(pays[:2])
    halo_b = swap(pays[2:])

    overlap = tuple(STEP * t for t in range(tiles))
    alone = tuple(hz + LANES * t for t in range(own))
    pairs = own_pairs(tiles, alone)
    forward, back, ends, back_own = call(
        functools.partial(band_kernel, pairs, alone),
        [jax.ShapeDtypeStruct((2 * LANES, 2 * LANES), jnp.bfloat16)] * 3
        + [jax.ShapeDtypeStruct((len(pairs), 2 * LANES, 2 * LANES), jnp.bfloat16)],
        (depth_psf, pays[-1]), [], 8, 1, scalars=1, unread=(1,),
    )
    stacks_x, stacks_y = stitch_width.shape[:2]
    weight, inv = call(
        functools.partial(norm_kernel, (cx, cy, hy, stacks_x, stacks_y)),
        [shape(wide, full, LANES), shape(tiles, cx, ceil_to(end1, 8), LANES)],
        (place, stitch_width.reshape(-1), pays[-1], tx, ty), [(tiles, cx, full, LANES)], 10, 1, scalars=2, unread=(2,),
    )
    shift = 2 * reach

    mats = {overlap: (forward, back, ends), alone: (forward, back_own)}

    def inner(est, data_off, starts, rows, need):
        plan = dict(data_off=data_off, starts=starts, need=need)
        rows = ceil_to(rows, 8)
        return call(
            functools.partial(inner_kernel, plan), [shape(len(starts), cx - shift, rows, LANES)],
            (est, ext, weight, tx, ty, *mats[starts]), [(tiles, cx - shift, rows + 16, LANES)], 24, 1,
        )[0]

    def outer(est, halos, extra, inner_part, last, plan, outs):
        rows = ceil_to(plan["high"] - plan["low"] + 2 * reach, 8)
        lateral = (tx_own, ty_own) if last else (tx, ty)
        starts = alone if last else overlap
        args = (place, est) + tuple(h for _, pair in halos for h in pair) + extra
        args += (inner_part, inv, tx, ty) + lateral + mats[starts]
        plan = dict(
            plan, hx=hx, packed=packed, halos=[rng for rng, _ in halos], make_data=not last, pay=not last,
            starts=starts, mats=len(mats[starts]), data_off=shift if last else 0,
        )
        scratch = [(tiles, cx, rows + 16, LANES), (len(starts), 2 * hx, rows, LANES)]
        return call(functools.partial(outer_kernel, plan), outs, args, scratch, 16, 1, scalars=1)

    data_at = mid2 + 8
    spread1 = inner(ext, 0, overlap, end1 + shift, end0)
    est_a, data_a, *pays = outer(
        ext, [((0, cut), halo_a)], (weight,), spread1, False,
        dict(low=0, high=mid1, data_base=0, prior=False),
        [shape(tiles, cx, mid1, LANES), shape(tiles, 2 * hx, cut, LANES)] + pay_shapes(mid1),
    )
    halo_c = swap(pays)
    est, data_b, *pays = outer(
        ext, [((0, cut), halo_a), ((cut, end0), halo_b)], (weight, est_a), spread1, False,
        dict(low=mid1, high=end1, data_base=data_at, prior=True),
        [shape(tiles, cx, ceil_to(end1, 8), LANES), shape(tiles, 2 * hx, full - data_at, LANES)] + pay_shapes(end1 - mid1),
    )
    halo_d = swap(pays)
    spread2 = inner(est, shift, alone, end2 + shift, end1)
    (out_a,) = outer(
        est, [((0, mid1), halo_c)], (data_a,), spread2, True,
        dict(low=0, high=mid2, data_base=0, prior=False), [shape(own, cx, mid2, LANES)],
    )
    (out_b,) = outer(
        est, [((0, mid1), halo_c), ((mid1, end1), halo_d)], (data_b,), spread2, True,
        dict(low=mid2, high=end2, data_base=data_at, prior=False), [shape(own, cx, end2 - mid2, LANES)],
    )
    estimate = jnp.concatenate([out_a, out_b], axis=2)
    return estimate.transpose(0, 3, 1, 2).reshape(own * LANES, cx, cy)[:nz]


def solution(mesh):
    in_specs = (P("gz", "sx", "sy"), P("gz"), P(), P(), P(), P())
    out_specs = P("gz", "sx", "sy")
    return jax.shard_map(body, mesh=mesh, in_specs=in_specs, out_specs=out_specs, check_vma=False)
```

```python
import functools

import jax
import jax.numpy as jnp
from jax import lax
from jax.experimental import pallas as pl
from jax.experimental.pallas import tpu as pltpu
from jax.sharding import PartitionSpec as P


ITERS = 2
LANES = 128
TINY = 1e-30
EDGE = 16
STEP = LANES - 2 * EDGE
LAP = LANES - STEP
VMEM = pl.BlockSpec(memory_space=pltpu.VMEM)


def ceil_to(value, unit):
    return -(-value // unit) * unit


def swaps(count):
    return [[(i, i + 1) for i in range(first, count - 1, 2)] for first in (0, 1)]


def both_ways(pairs):
    return pairs + [(j, i) for i, j in pairs]


def spin(value, shift):
    return pltpu.roll(value, shift % LANES, 1) if shift % LANES else value


def regroup(tiles, start):
    lane = lax.broadcasted_iota(jnp.int32, tiles[0].shape, 1)
    out = None
    for t, tile in enumerate(tiles):
        first = 0 if t == 0 else STEP * t + EDGE - start
        stop = LANES if t == len(tiles) - 1 else STEP * (t + 1) + EDGE - start
        if max(first, 0) < min(stop, LANES):
            value = spin(tile, STEP * t - start)
            out = value if out is None else jnp.where(lane >= first, value, out)
    return out


def halo_tiles(refs, odd, tiles, packed, hx, rows):
    planes, half = {}, hx // 2

    def plane(index, side):
        if index not in planes:
            planes[index] = by_side(odd, refs[0][index, rows, :], refs[1][index, rows, :])
        return planes[index][side]

    sides = []
    lane = lax.broadcasted_iota(jnp.int32, (8, LANES), 1)
    for side in range(2):
        out = [[] for _ in range(tiles)]
        for p in range(hx):
            if not packed:
                for t in range(tiles):
                    out[t].append(plane(hx * t + p, side))
                continue
            one, two, end = plane(p, side), plane(hx + p, side), plane(2 * hx + p % half, side)
            out[0].append(one)
            out[1].append(jnp.where(lane < LAP, spin(one, LAP), two))
            out[2].append(jnp.where(lane < 2 * LAP, spin(two, LAP), spin(end, LANES // 2 if p >= half else 0)))
        sides.append(out)
    return sides


def pack_both(src, pays, odd, packed, hx, blocks, src_block):
    high = src.shape[1] - hx
    pack_rows(src, pays[0], packed, hx, jnp.where(odd == 1, 0, high), blocks, src_block, 0)
    pack_rows(src, pays[1], packed, hx, jnp.where(odd == 1, high, 0), blocks, src_block, 0)


def by_side(odd, first, second):
    return jnp.where(odd == 1, first, second), jnp.where(odd == 1, second, first)


def pack_rows(src, pay, packed, hx, x0, blocks, src_block, pay_block):
    tiles = src.shape[0]
    half = hx // 2

    def step(j, carry):
        here = pl.ds(pl.multiple_of(8 * (j + src_block), 8), 8)
        there = pl.ds(pl.multiple_of(8 * (j + pay_block), 8), 8)
        lane = lax.broadcasted_iota(jnp.int32, (8, LANES), 1)
        for p in range(hx):
            for t in range(1 if packed else tiles):
                pay[hx * t + p, there, :] = src[t, x0 + p, here, :]
            if packed:
                last = src[2, x0 + p, here, :]
                pay[hx + p, there, :] = jnp.where(lane < LAP, spin(last, -LAP), src[1, x0 + p, here, :])
                if p < half:
                    other = spin(src[2, x0 + p + half, here, :], LANES // 2)
                    pay[2 * hx + p, there, :] = jnp.where(lane < LANES // 2, other, last)
        return carry

    lax.fori_loop(0, blocks, step, 0)


def conv_rows(k, v, width):
    out = []
    for x in range(width):
        acc = k[0] * v[x]
        for a in range(1, len(k)):
            acc = acc + k[a] * v[x + a]
        out.append(acc)
    return out


def y_conv(src, taps, reverse, t, width, blocks, emit):
    count = taps.shape[1]
    k = [taps[t, count - 1 - b if reverse else b] for b in range(count)]

    def step(x, carry):
        for j in range(blocks):
            acc = k[0] * src[t, x, 8 * j : 8 * j + 8, :]
            for b in range(1, count):
                acc = acc + k[b] * src[t, x, 8 * j + b : 8 * j + b + 8, :]
            emit(t, x, j, acc)
        return carry

    lax.fori_loop(0, width, step, 0)


def halves(parts):
    whole = jnp.concatenate(parts, axis=0)
    hi = whole.astype(jnp.bfloat16)
    return jnp.concatenate([hi, (whole - hi.astype(jnp.float32)).astype(jnp.bfloat16)], axis=1)


def depth_sums(pair, matrix):
    res = jnp.dot(pair, matrix, preferred_element_type=jnp.float32)
    return res[:, :LANES] + res[:, LANES:]


def own_pairs(tiles, starts):
    pairs = []
    for k, start in enumerate(starts):
        for t in range(tiles):
            first = max(0 if t == 0 else STEP * t + EDGE - start, 0)
            stop = min(LANES if t == tiles - 1 else STEP * (t + 1) + EDGE - start, LANES)
            if first < stop:
                pairs.append((k, t, first, stop))
    return pairs


def x_loop(taps, reverse, first, last, rows_in, rows_out):
    tiles, count = taps.shape[:2]

    def step(j, carry):
        rows = rows_in(j)
        for t in range(tiles):
            k = [taps[t, count - 1 - a if reverse else a] for a in range(count)]
            for n, v in enumerate(rows[t]):
                rows_out(t, j, n, conv_rows(k, v, len(v) - count + 1))
        return carry

    if first < last:
        lax.fori_loop(first, last, step, 0)


def y_group(mid_ref, taps, t, first, group, blocks):
    count = taps.shape[1]
    k = [taps[t, b] for b in range(count)]
    out = []
    for x in [first + n for n in range(group)]:
        for j in range(blocks):
            acc = k[0] * mid_ref[t, x, 8 * j : 8 * j + 8, :]
            for b in range(1, count):
                acc = acc + k[b] * mid_ref[t, x, 8 * j + b : 8 * j + b + 8, :]
            out.append(acc)
    return jnp.concatenate(out, axis=0)


def correct(mid_ref, ty_ref, mats, starts, group, count, rows, data_of, spread_ref):
    forward_ref, back_ref, *more = mats
    tiles = mid_ref.shape[0]
    group = next(n for n in range(group, 0, -1) if count % n == 0 and n * rows % 16 == 0)

    def depth(i, carry):
        first = group * i
        blurred = [y_group(mid_ref, ty_ref, t, first, group, rows // 8) for t in range(tiles)]
        size = group * rows
        blurred = depth_sums(halves(blurred), forward_ref[...])
        ratio = []
        for t in range(tiles):
            ratio.append(data_of(t, first, group) / jnp.maximum(blurred[size * t : size * (t + 1)], TINY))
        ratio = halves(ratio)
        if starts[0] == 0:
            spread = depth_sums(ratio, back_ref[...])
            spread = [spread[size * t : size * (t + 1)] for t in range(tiles)]
            if tiles > 1:
                ends = depth_sums(ratio, more[0][...])
                ends = [ends[size * t : size * (t + 1)] for t in range(tiles)]
                lane = lax.broadcasted_iota(jnp.int32, (size, LANES), 1)
                for t in range(tiles):
                    if t > 0:
                        spread[t] = jnp.where(lane < EDGE, ends[t - 1], spread[t])
                    if t < tiles - 1:
                        spread[t] = jnp.where(lane >= LANES - EDGE, ends[t + 1], spread[t])
        else:
            spread = [None] * len(starts)
            for n, (k, t, _, _) in enumerate(own_pairs(tiles, starts)):
                part = depth_sums(ratio[size * t : size * (t + 1)], back_ref[n])
                spread[k] = part if spread[k] is None else spread[k] + part
        for t, value in enumerate(spread):
            spread_ref[t, pl.ds(first, group), 0:rows, :] = value.reshape(group, rows, LANES)
        return carry

    lax.fori_loop(0, count // group, depth, 0)


def inner_kernel(plan, est_ref, obs_ref, w_ref, tx_ref, ty_ref, *refs):
    *mats, spread_ref, mid_ref = refs
    tiles, cx = est_ref.shape[:2]
    reach = (tx_ref.shape[1] - 1) // 2
    rows = spread_ref.shape[2]
    first = plan["data_off"] + reach
    count = cx - 2 * reach

    def rows_in(j):
        here = pl.ds(pl.multiple_of(8 * j, 8), 8)
        return [[[est_ref[t, x, here, :] for x in range(cx)]] for t in range(tiles)]

    def rows_out(t, j, n, values):
        here = pl.ds(pl.multiple_of(8 * j, 8), 8)
        for x, value in enumerate(values):
            mid_ref[t, x, here, :] = value

    x_loop(tx_ref, False, 0, -(-plan["need"] // 8), rows_in, rows_out)

    def data_of(t, x, group):
        seen = obs_ref[t, pl.ds(x + reach, group), first : first + rows, :]
        return (seen * w_ref[pl.ds(x + 2 * reach, group), first : first + rows, :]).reshape(group * rows, LANES)

    correct(mid_ref, ty_ref, mats, plan["starts"], 10, count, rows, data_of, spread_ref)


def norm_kernel(plan, place_ref, bands_ref, _, tx_ref, ty_ref, w_ref, out_ref, mid_ref):
    cx, cy, hy, stacks_x, stacks_y = plan
    tiles, count = tx_ref.shape[:2]
    reach = (count - 1) // 2
    width = out_ref.shape[1]
    full = w_ref.shape[1]
    sx, sy = place_ref[0], place_ref[1]
    row = lax.broadcasted_iota(jnp.int32, (full, LANES), 0)
    for x in range(cx + 2 * reach):
        a = (x - reach) // cx
        px = (x - reach) % cx
        gx = sx + a
        value = jnp.zeros((full, LANES), jnp.float32)
        for b, first in ((-1, 0), (0, hy), (1, hy + cy)):
            gy = sy + b
            inside = (gx >= 0) & (gx < stacks_x) & (gy >= 0) & (gy < stacks_y)
            spot = 2 * (jnp.clip(gx, 0, stacks_x - 1) * stacks_y + jnp.clip(gy, 0, stacks_y - 1))
            along = jnp.where(inside, jnp.where(px < bands_ref[spot], 0.5, 1.0), 0.0)
            across = jnp.where(row - hy - b * cy < bands_ref[spot + 1], 0.5, 1.0)
            value = jnp.where(row >= first, across * along, value)
        w_ref[x] = value

    def rows_in(j):
        rows = pl.ds(pl.multiple_of(8 * j, 8), 8)
        return [[[w_ref[x, rows, :] for x in range(width + count - 1)]]] * tiles

    def rows_out(t, j, n, values):
        rows = pl.ds(pl.multiple_of(8 * j, 8), 8)
        for x, value in enumerate(values):
            mid_ref[t, x, rows, :] = value

    x_loop(tx_ref, True, 0, full // 8, rows_in, rows_out)
    for t in range(tiles):
        ky = [ty_ref[t, count - 1 - b] for b in range(count)]

        def ystep(x, carry, ky=ky, t=t):
            for j in range(out_ref.shape[2] // 8):
                at = 8 * j + reach
                acc = ky[0] * mid_ref[t, x, at : at + 8, :]
                for b in range(1, count):
                    acc = acc + ky[b] * mid_ref[t, x, at + b : at + b + 8, :]
                out_ref[t, x, 8 * j : 8 * j + 8, :] = 1.0 / jnp.maximum(acc, TINY)
            return carry

        lax.fori_loop(0, width, ystep, 0)


def band_kernel(pairs, starts, psf_ref, _, forward_ref, back_ref, ends_ref, own_ref):
    taps = psf_ref.shape[0]
    total = psf_ref[0]
    for j in range(1, taps):
        total = total + psf_ref[j]
    shape = (LANES, LANES)
    row = lax.broadcasted_iota(jnp.int32, shape, 0)
    lane = lax.broadcasted_iota(jnp.int32, shape, 1)

    def fill(ref, target, sign, keep):
        off = sign * (target - row) + (taps - 1) // 2
        matrix = jnp.zeros(shape, jnp.float32)
        for j in range(taps):
            matrix = jnp.where(off == j, psf_ref[j], matrix)
        matrix = matrix / jnp.full(shape, total, jnp.float32)
        if keep is not None:
            matrix = jnp.where(keep, matrix, 0.0)
        hi = matrix.astype(jnp.bfloat16)
        ref[:LANES, :LANES] = hi
        ref[LANES:, :LANES] = hi
        ref[:LANES, LANES:] = (matrix - hi.astype(jnp.float32)).astype(jnp.bfloat16)
        ref[LANES:, LANES:] = jnp.zeros(shape, jnp.bfloat16)

    fill(forward_ref, lane, 1, None)
    fill(back_ref, lane, -1, None)
    side = (lane < EDGE) | (lane >= LANES - EDGE)
    fill(ends_ref, jnp.where(lane < EDGE, lane + STEP, lane - STEP), -1, side)
    for n, (k, t, first, stop) in enumerate(pairs):
        fill(own_ref.at[n], lane + starts[k] - STEP * t, -1, (lane >= first) & (lane < stop))


def with_halo(parts, halo, turned, width):
    if halo is None:
        return parts
    lane = lax.broadcasted_iota(jnp.int32, halo.shape, 1)
    first = jnp.where(lane < width, halo, parts[0])
    last = jnp.where(lane >= LANES - width, turned, parts[-1])
    return [first, *parts[1:-1], last]


def edges_kernel(hy, width, turn, place_ref, vol_ref, *refs):
    tiles, cx, cy = vol_ref.shape[:3]
    odd = place_ref[1] % 2
    direct = len(refs) > 2
    if direct:
        zones_ref, first_ref, second_ref, first_z, second_z, depth_ref = refs
        lane = lax.broadcasted_iota(jnp.int32, (cy, LANES), 1)
        half = cx // 2

        def outmost(low, high, at):
            return jnp.where(at < width, spin(high, -turn), low)

        for x in range(half):
            one, two = [outmost(vol_ref[0, n], vol_ref[tiles - 1, n], lane) for n in (x, x + half)]
            depth_ref[cy * x : cy * x + cy, :] = jnp.where(lane < LANES // 2, one, spin(two, LANES // 2))
        depth_ref[cy * half :, :] = zones_ref[...]
    else:
        first_ref, second_ref = refs
    lane = lax.broadcasted_iota(jnp.int32, (hy, LANES), 1)
    kept = []
    for x in range(cx):
        to = slice(hy * x, hy * x + hy)
        both = []
        for t in range(tiles):
            low, high = vol_ref[t, x, 0:hy, :], vol_ref[t, x, cy - hy : cy, :]
            both.append((jnp.where(odd == 1, low, high), jnp.where(odd == 1, high, low)))
            first_ref[t, to, :], second_ref[t, to, :] = both[-1]
        if direct:
            kept.append([outmost(both[0][n], both[-1][n], lane) for n in range(2)])
            if x >= half:
                to = slice(hy * (x - half), hy * (x - half) + hy)
                for n, ref in enumerate((first_z, second_z)):
                    ref[to, :] = jnp.where(lane < LANES // 2, kept[x - half][n], spin(kept[x][n], LANES // 2))


def assemble_kernel(packed, hx, cut, shift, refs_in, place_ref, *refs):
    vol_ref, first_ref, second_ref = refs[:3]
    depth_ref, first_z, second_z = refs[3:6] if refs_in == 6 else (None,) * 3
    ext_ref, *pays = refs[refs_in:]
    main, cx, cy = vol_ref.shape[:3]
    hy = first_ref.shape[1] // cx
    end = cy + 2 * hy
    odd = place_ref[1] % 2
    half = cx // 2

    tiles = ext_ref.shape[0]
    for x in range(cx):
        edge = slice(hy * x, hy * x + hy)
        low, high = zip(*[by_side(odd, first_ref[t, edge, :], second_ref[t, edge, :]) for t in range(main)])
        mids = [vol_ref[t, x] for t in range(main)]
        if depth_ref is not None:
            edge_z = slice(hy * (x % half), hy * (x % half) + hy)
            low_z, high_z = [(z, spin(z, LANES // 2)) for z in by_side(odd, first_z[edge_z, :], second_z[edge_z, :])]
            low = with_halo(low, *(low_z if x < half else low_z[::-1]), shift)
            high = with_halo(high, *(high_z if x < half else high_z[::-1]), shift)
            halo = depth_ref[cy * (x % half) : cy * (x % half) + cy, :]
            pair = (halo, spin(halo, LANES // 2))
            mids = with_halo(mids, *(pair if x < half else pair[::-1]), shift)
        for t in range(tiles):
            ext_ref[t, x, 0:hy, :] = low[t]
            ext_ref[t, x, hy : hy + cy, :] = mids[t]
            ext_ref[t, x, hy + cy : end, :] = high[t]
            ext_ref[t, x, end:, :] = jnp.zeros((ext_ref.shape[2] - end, LANES), jnp.float32)
    pack_both(ext_ref, pays, place_ref[0] % 2, packed, hx, -(-cut // 8), 0)


def pack_kernel(packed, hx, first, stop, place_ref, ext_ref, *pays):
    pack_both(ext_ref, pays, place_ref[0] % 2, packed, hx, -(-(stop - first) // 8), first // 8)


def outer_kernel(plan, place_ref, *refs):
    refs = list(refs)
    odd = place_ref[0] % 2
    take = refs.pop
    est_ref = take(0)
    halos = [(take(0), take(0), first, last) for first, last in plan["halos"]]
    make = plan["make_data"]
    w_ref = take(0) if make else None
    data_in = None if make else take(0)
    prior_ref = take(0) if plan["prior"] else None
    inner_ref, inv_ref, tx_ref, ty_ref, bx_ref, by_ref = [take(0) for _ in range(6)]
    mats = [take(0) for _ in range(plan["mats"])]
    out_ref = take(0)
    data_ref = take(0) if make else data_in
    pays = [take(0), take(0)] if plan["pay"] else None
    mid_ref, edge_ref = refs
    packed, hx, low, high = plan["packed"], plan["hx"], plan["low"], plan["high"]
    data_base, off, starts = plan["data_base"], plan["data_off"], plan["starts"]
    tiles, cx = est_ref.shape[:2]
    outs = out_ref.shape[0]
    count = tx_ref.shape[1]
    reach = (count - 1) // 2
    rows = edge_ref.shape[2]
    last_block = -(-(high + 4 * reach) // 8)
    data_first = data_base // 8 if make else low // 8

    for lo_ref, hi_ref, first, last in halos:

        def rows_in(j, lo_ref=lo_ref, hi_ref=hi_ref, first=first):
            here = pl.ds(pl.multiple_of(8 * j, 8), 8)
            there = pl.ds(pl.multiple_of(8 * j - first, 8), 8)
            lows, highs = halo_tiles((lo_ref, hi_ref), odd, tiles, packed, hx, there)
            return [
                [
                    lows[t] + [est_ref[t, x, here, :] for x in range(hx)],
                    [est_ref[t, x, here, :] for x in range(cx - hx, cx)] + highs[t],
                ]
                for t in range(tiles)
            ]

        def keep(t, j, pair):
            here = pl.ds(pl.multiple_of(8 * j, 8), 8)
            there = pl.ds(pl.multiple_of(8 * j - data_base, 8), 8)
            for n, v in enumerate(pair):
                for x in range(hx):
                    data_ref[t, hx * n + x, there, :] = w_ref[x + cx * n, here, :] * v[x + reach]

        def rows_in_keep(j, rows_in=rows_in, keep=keep):
            rows = rows_in(j)
            if make:
                for t in range(tiles):
                    keep(t, j, rows[t])
            return rows

        def rows_out(t, j, n, values):
            mid = pl.ds(pl.multiple_of(8 * j - low, 8), 8)
            for x, value in enumerate(values):
                mid_ref[t, hx * n + x, mid, :] = value

        def only_data(j, carry, rows_in=rows_in, keep=keep):
            for t, pair in enumerate(rows_in(j)):
                keep(t, j, pair)
            return carry

        a, b = max(first // 8, data_first), min(last // 8, low // 8)
        if make and a < b:
            lax.fori_loop(a, b, only_data, 0)
        x_loop(tx_ref, False, max(first // 8, low // 8), min(-(-last // 8), last_block), rows_in_keep, rows_out)

    spot0 = low + off + reach - data_base

    def data_of(t, x, group):
        return data_ref[t, pl.ds(x, group), spot0 : spot0 + rows, :].reshape(group * rows, LANES)

    correct(mid_ref, ty_ref, mats, starts, 12, 2 * hx, rows, data_of, edge_ref)

    blocks = -(-(high - low) // 8)

    def back_in(j):
        here = pl.ds(pl.multiple_of(8 * j, 8), 8)
        there = pl.ds(pl.multiple_of(8 * j + low, 8), 8)
        rows = []
        for t in range(outs):
            v = [edge_ref[t, x, here, :] for x in range(hx)]
            v += [inner_ref[t, x, there, :] for x in range(cx - 2 * reach)]
            rows.append([v + [edge_ref[t, x, here, :] for x in range(hx, 2 * hx)]])
        return rows

    def back_out(t, j, n, values):
        here = pl.ds(pl.multiple_of(8 * j, 8), 8)
        for x, value in enumerate(values):
            mid_ref[t, x, here, :] = value

    x_loop(bx_ref, True, 0, rows // 8, back_in, back_out)
    base = low if prior_ref is not None else 0

    def finish(t, x, j, acc):
        at = 8 * j + low + 2 * reach
        scale = 8 * j + low + off
        if starts[t] == STEP * t:
            old = est_ref[t, x, at : at + 8, :] * inv_ref[t, x, scale : scale + 8, :]
        else:
            old = [est_ref[n, x, at : at + 8, :] * inv_ref[n, x, scale : scale + 8, :] for n in range(tiles)]
            old = regroup(old, starts[t])
        to = 8 * j + base
        out_ref[t, x, to : to + 8, :] = old * acc

    for t in range(outs):
        y_conv(mid_ref, by_ref, True, t, cx, blocks, finish)

    if prior_ref is not None:
        for t in range(outs):

            def copy(x, carry, t=t):
                out_ref[t, x, 0:low, :] = prior_ref[t, x, 0:low, :]
                return carry

            lax.fori_loop(0, cx, copy, 0)
    if pays:
        pack_both(out_ref, pays, odd, packed, hx, blocks, base // 8)


def body(observed, zone_of_slice, lateral_x, lateral_y, depth_psf, stitch_width):
    nz, cx, cy = observed.shape
    taps = lateral_x.shape[1]
    reach = (taps - 1) // 2
    zreach = (depth_psf.shape[0] - 1) // 2
    hz = 2 * zreach * ITERS
    hy = 2 * reach * ITERS
    hx = 2 * reach
    slabs = lax.axis_size("gz")
    tiles = 1 + max(0, -(-(nz + 2 * hz - LANES) // STEP))
    f32 = jnp.float32

    zones = zone_of_slice.astype(f32)
    pad = LANES + STEP * (tiles - 1) - nz - 2 * hz
    direct = slabs == 2 and tiles > 1 and pad == 0 and nz % LANES == 0 and hz == LAP and cx % 2 == 0
    sx, sy = lax.axis_index("sx"), lax.axis_index("sy")
    place = jnp.stack([sx, sy]).astype(jnp.int32)

    def shape(*dims):
        return jax.ShapeDtypeStruct(dims, f32)

    def call(kernel, out_shape, args, scratch, limit, flops, scalars=0, unread=()):
        moved = sum(a.size * 4 for a in args) + sum(o.size * 4 for o in out_shape)
        spaces = [pltpu.SMEM] * scalars + [pltpu.VMEM] * (len(args) - scalars)
        spaces = [pl.ANY if n in unread else space for n, space in enumerate(spaces)]
        return pl.pallas_call(
            kernel,
            out_shape=out_shape,
            in_specs=[pl.BlockSpec(memory_space=space) for space in spaces],
            out_specs=[VMEM] * len(out_shape),
            scratch_shapes=[pltpu.VMEM(dims, f32) for dims in scratch],
            compiler_params=pltpu.CompilerParams(vmem_limit_bytes=limit << 20),
            cost_estimate=pl.CostEstimate(flops=flops, bytes_accessed=moved, transcendentals=0),
        )(*args)

    def lanes_first(value):
        parts = jnp.stack([value[STEP * t : STEP * t + LANES] for t in range(tiles)])
        return parts.transpose(0, 2, 3, 1)

    rounds_y = swaps(lax.axis_size("sy"))
    if direct:
        volume = lanes_first(jnp.pad(observed, ((hz, hz), (0, 0), (0, 0))))
        zone_rows = jnp.pad(zones.reshape(-1, LANES), ((0, 8 - nz // LANES), (0, 0)))
        edge, edge_z = shape(volume.shape[0], cx * hy, LANES), shape(cx // 2 * hy, LANES)
        first, second, first_z, second_z, borders = call(
            functools.partial(edges_kernel, hy, hz, nz - STEP * (tiles - 1)), [edge, edge, edge_z, edge_z, shape(cx // 2 * cy + 8, LANES)],
            (place, volume, zone_rows), [], 8, 1, scalars=1,
        )
        borders = lax.ppermute(borders, "gz", [(0, 1), (1, 0)])
        parts = [volume, lax.ppermute(first, "sy", both_ways(rounds_y[0])), lax.ppermute(second, "sy", both_ways(rounds_y[1]))]
        parts.append(borders)
        for value, pairs in ((first_z, rounds_y[0]), (second_z, rounds_y[1])):
            cross = [(2 * i + g, 2 * j + 1 - g) for i, j in pairs for g in range(2)]
            parts.append(lax.ppermute(value, ("sy", "gz"), both_ways(cross)))
        got_ids = borders[cx // 2 * cy :].reshape(-1)[:nz]
        ids_before, ids_after = got_ids[nz - hz :], got_ids[:hz]
    else:

        def with_zones(part, ids):
            flat = jnp.pad(ids, (0, cx * cy - ids.shape[0]))
            return jnp.concatenate([part, flat.reshape(1, cx, cy)], axis=0)

        ring = [(i, (i + 1) % slabs) for i in range(slabs)]
        first = lax.ppermute(with_zones(observed[nz - hz :], zones[nz - hz :]), "gz", ring)
        second = lax.ppermute(with_zones(observed[:hz], zones[:hz]), "gz", [(j, i) for i, j in ring])
        before, after = first[:hz], second[:hz]
        ids_before, ids_after = first[hz].reshape(-1)[:hz], second[hz].reshape(-1)[:hz]
        volume = lanes_first(jnp.concatenate([before, observed, after, jnp.zeros((pad, cx, cy), f32)], axis=0))
        edge = shape(tiles, cx * hy, LANES)
        first, second = call(
            functools.partial(edges_kernel, hy, hz, nz - STEP * (tiles - 1)), [edge, edge], (place, volume), [], 8, 1, scalars=1
        )
        parts = [volume, lax.ppermute(first, "sy", both_ways(rounds_y[0])), lax.ppermute(second, "sy", both_ways(rounds_y[1]))]
    ids = jnp.concatenate([ids_before, zones, ids_after, jnp.full((pad,), -1.0, f32)])
    ids = jnp.concatenate([ids[STEP * t : STEP * t + LANES] for t in range(tiles)])

    def lanes_of(kernels, names):
        match = (names[None, :] == jnp.arange(lateral_x.shape[0], dtype=f32)[:, None]).astype(f32)
        table = jnp.sum(match[:, None, :] * kernels[:, :, None], axis=0)
        table = table.reshape(taps, -1, 1, LANES).transpose(1, 0, 2, 3)
        return jnp.broadcast_to(table, (table.shape[0], taps, 8, LANES))

    tx, ty = lanes_of(lateral_x, ids), lanes_of(lateral_y, ids)
    own = ceil_to(nz, LANES) // LANES
    own_ids = jnp.concatenate([zones, jnp.full((own * LANES - nz,), -1.0, f32)])
    tx_own, ty_own = lanes_of(lateral_x, own_ids), lanes_of(lateral_y, own_ids)

    wide = cx + 2 * reach
    packed = tiles == 3
    planes = 2 * hx + hx // 2 if packed else hx * tiles
    end0, end1, end2 = cy + 2 * hy, cy + 2 * hy - 4 * reach, cy
    mid1 = ceil_to(end1 // 2, 8) + 8
    mid2 = mid1 - ceil_to(4 * reach, 8)
    cut = ceil_to(mid1 + 4 * reach, 8)
    rounds_x = [both_ways(pairs) for pairs in swaps(lax.axis_size("sx"))]
    full = ceil_to(cy + 2 * hy + reach, 8)

    def pay_shapes(rows):
        return [shape(planes, ceil_to(rows, 8), LANES)] * 2

    def swap(pays):
        got = []
        for n in range(2):
            got.append(lax.ppermute(pays[n], "sx", rounds_x[n]))
        return got

    ext, *pays = call(
        functools.partial(assemble_kernel, packed, hx, cut, hz, len(parts)),
        [shape(tiles, cx, full, LANES)] + pay_shapes(cut),
        (place, *parts), [], 8, 1, scalars=1,
    )
    halo_a = swap(pays)
    pack = functools.partial(pack_kernel, packed, hx, cut, end0)
    rest = call(pack, pay_shapes(end0 - cut), (place, ext), [], 8, 1, scalars=1)
    halo_b = swap(rest)

    overlap = tuple(STEP * t for t in range(tiles))
    alone = tuple(hz + LANES * t for t in range(own))
    pairs = own_pairs(tiles, alone)
    forward, back, ends, back_own = call(
        functools.partial(band_kernel, pairs, alone),
        [jax.ShapeDtypeStruct((2 * LANES, 2 * LANES), jnp.bfloat16)] * 3
        + [jax.ShapeDtypeStruct((len(pairs), 2 * LANES, 2 * LANES), jnp.bfloat16)],
        (depth_psf, rest[-1]), [], 8, 1, scalars=1, unread=(1,),
    )
    stacks_x, stacks_y = stitch_width.shape[:2]
    weight, inv = call(
        functools.partial(norm_kernel, (cx, cy, hy, stacks_x, stacks_y)),
        [shape(wide, full, LANES), shape(tiles, cx, ceil_to(end1, 8), LANES)],
        (place, stitch_width.reshape(-1), rest[-1], tx, ty), [(tiles, cx, full, LANES)], 10, 1, scalars=2, unread=(2,),
    )
    shift = 2 * reach

    mats = {overlap: (forward, back, ends), alone: (forward, back_own)}

    def inner(est, data_off, starts, rows, need):
        plan = dict(data_off=data_off, starts=starts, need=need)
        rows = ceil_to(rows, 8)
        return call(
            functools.partial(inner_kernel, plan), [shape(len(starts), cx - shift, rows, LANES)],
            (est, ext, weight, tx, ty, *mats[starts]), [(tiles, cx - shift, rows + 16, LANES)], 24, 1,
        )[0]

    def outer(est, halos, extra, inner_part, last, plan, outs):
        rows = ceil_to(plan["high"] - plan["low"] + 2 * reach, 8)
        lateral = (tx_own, ty_own) if last else (tx, ty)
        starts = alone if last else overlap
        args = (place, est) + tuple(h for _, pair in halos for h in pair) + extra
        args += (inner_part, inv, tx, ty) + lateral + mats[starts]
        plan = dict(
            plan, hx=hx, packed=packed, halos=[rng for rng, _ in halos], make_data=not last, pay=not last,
            starts=starts, mats=len(mats[starts]), data_off=shift if last else 0,
        )
        scratch = [(tiles, cx, rows + 16, LANES), (len(starts), 2 * hx, rows, LANES)]
        return call(functools.partial(outer_kernel, plan), outs, args, scratch, 16, 1, scalars=1)

    data_at = mid2 + 8
    spread1 = inner(ext, 0, overlap, end1 + shift, end0)
    est_a, data_a, *pays = outer(
        ext, [((0, cut), halo_a)], (weight,), spread1, False,
        dict(low=0, high=mid1, data_base=0, prior=False),
        [shape(tiles, cx, mid1, LANES), shape(tiles, 2 * hx, cut, LANES)] + pay_shapes(mid1),
    )
    halo_c = swap(pays)
    est, data_b, *pays = outer(
        ext, [((0, cut), halo_a), ((cut, end0), halo_b)], (weight, est_a), spread1, False,
        dict(low=mid1, high=end1, data_base=data_at, prior=True),
        [shape(tiles, cx, ceil_to(end1, 8), LANES), shape(tiles, 2 * hx, full - data_at, LANES)] + pay_shapes(end1 - mid1),
    )
    halo_d = swap(pays)
    spread2 = inner(est, shift, alone, end2 + shift, end1)
    (out_a,) = outer(
        est, [((0, mid1), halo_c)], (data_a,), spread2, True,
        dict(low=0, high=mid2, data_base=0, prior=False), [shape(own, cx, mid2, LANES)],
    )
    (out_b,) = outer(
        est, [((0, mid1), halo_c), ((mid1, end1), halo_d)], (data_b,), spread2, True,
        dict(low=mid2, high=end2, data_base=data_at, prior=False), [shape(own, cx, end2 - mid2, LANES)],
    )
    estimate = jnp.concatenate([out_a, out_b], axis=2)
    return estimate.transpose(0, 3, 1, 2).reshape(own * LANES, cx, cy)[:nz]


def solution(mesh):
    in_specs = (P("gz", "sx", "sy"), P("gz"), P(), P(), P(), P())
    out_specs = P("gz", "sx", "sy")
    return jax.shard_map(body, mesh=mesh, in_specs=in_specs, out_specs=out_specs, check_vma=False)
```
